512 devices in a mesh: gx: 8 (over z_lo), gy: 8 (over y, core), gz: 8 (over x, z_hi).
Axes of the slice: x: 4, y: 4, z: 16 (z_hi: 2, z_lo: 8; z = z_hi * 8 + z_lo), core: 2. Of those that a mesh axis runs over, the one named last changes fastest.
Arguments:
- positions_now: float32 [64, 32, 8, 4, 128], P('gx', 'gy', 'gz'), may hold values from 0 to 1
- velocities: float32 [64, 32, 8, 3, 128], P('gx', 'gy', 'gz'), may hold values from -6 to 6
- positions_next: float32 [64, 32, 8, 3, 128], P('gx', 'gy', 'gz'), may hold values from 0 to 1
- halo_counts: int32 [64, 32, 8], P('gx', 'gy', 'gz'), may hold values from 1 to 128, as said below
- neighbour_lists: int32 [64, 32, 8, 14], P('gx', 'gy', 'gz'), may hold values from 0 to 26, as said below
- descendants: int32 [64, 32, 8, 2, 128], P('gx', 'gy', 'gz'), may hold values from 0 to 127, as said below
Outputs:
- drift: float32 [64, 32, 8, 3, 128], P('gx', 'gy', 'gz')
- tension: float32 [64, 32, 8, 128], P('gx', 'gy', 'gz')
The draws below stay inside these ranges and needn't reach their ends.
Inputs may be any that keep to these rules, and one draw needn't show every extreme that they name: `halo_counts`: every cell holds 1 to 128 live halos; some cell holds exactly 128. `neighbour_lists`: each cell's list begins with code 13 (the cell itself) and holds distinct codes. `descendants`: row 0 is a code 0 to 26; row 1 is a live slot of the descendant's cell.
All inputs are finite; a program needn't handle non-finite values.
Results may differ from the reference program's by a relative error of at most 0.0003.
Values sent between devices are 32-bit elements; how exact they have to be, the bound alone decides.
No kernel may reach another device: no remote copies, remote signals or barrier semaphores. Data moves between devices by JAX's collectives and lax.ppermute only.
A program may use at most 64 MiB of HBM per device.

```python
import jax
import jax.numpy as jnp
from jax import lax

SLOTS = 128
NBR = 14
NX = 64
NY = 32
NZ = 8


def make_counts(key):
    shape = (NX, NY, NZ)
    xpos = jnp.arange(NX, dtype=jnp.int32)[:, None, None]
    upper = 32 + 96 * (xpos + 1) // NX
    raw = jax.random.randint(key, shape, 0, 1 << 20, dtype=jnp.int32)
    counts = 1 + raw % upper
    return counts.at[NX - 1, 0, 0].set(SLOTS)


def draw_halo_counts(key, part):
    return make_counts(jax.random.fold_in(key, 11))


def draw_neighbour_lists(key, part):
    sub = jax.random.fold_in(key, 23)
    scores = jax.random.randint(sub, (NX, NY, NZ, 26), 0, 1 << 20, dtype=jnp.int32) * 32 + jnp.arange(26, dtype=jnp.int32)
    order = jnp.argsort(scores, axis=-1, stable=True)[..., :NBR - 1].astype(jnp.int32)
    codes = jnp.where(order < 13, order, order + 1)
    selfcode = jnp.full((NX, NY, NZ, 1), 13, jnp.int32)
    return jnp.concatenate([selfcode, codes], axis=-1)


def draw_descendants(key, part):
    counts = make_counts(jax.random.fold_in(key, 11))
    sub = jax.random.fold_in(key, 37)
    first, second = jax.random.split(sub)
    codes = jax.random.randint(first, (NX, NY, NZ, SLOTS), 0, 27, dtype=jnp.int32)
    rolled = []
    for code in range(27):
        dx, dy, dz = (code // 9 - 1, code // 3 % 3 - 1, code % 3 - 1)
        rolled.append(jnp.roll(counts, (-dx, -dy, -dz), axis=(0, 1, 2)))
    table = jnp.stack(rolled, axis=-1)
    hits = (codes[..., None] == jnp.arange(27, dtype=jnp.int32)).astype(jnp.int32)
    target_count = jnp.sum(hits * table[:, :, :, None, :], axis=-1)
    raw = jax.random.randint(second, (NX, NY, NZ, SLOTS), 0, 1 << 20, dtype=jnp.int32)
    slotid = raw % target_count
    return jnp.stack([codes, slotid], axis=3)


def shard_levels(rng, extent, pieces, low, largest):
    loudness = 1.0
    for position, parts in pieces:
        heights = jax.random.uniform(jax.random.fold_in(jax.random.fold_in(rng, 6), position), (parts,), jnp.float32, low / len(pieces), largest / len(pieces))
        loudness = loudness * jnp.repeat(jnp.exp(heights), extent[position] // parts).reshape((-1,) + (1,) * (len(extent) - 1 - position))
    return loudness


def noise(own_key, shape, scale, limit, cuts=(), kind=jnp.bfloat16):
    result = scale * jax.random.normal(own_key, shape, jnp.float32)
    if cuts:
        result = result * shard_levels(own_key, shape, cuts, -0.22, 0.18)
    return jnp.clip(result, -limit, limit).astype(kind)


def setup_inputs(seed: int = 0) -> dict:
    splits = jax.random.split(jax.random.key(seed), 7)
    positions_now = jnp.clip(1.0 * jax.random.uniform(splits[0], (NX, NY, NZ, 4, SLOTS), jnp.float32) ** shard_levels(splits[0], (NX, NY, NZ, 4, SLOTS), ((0, 8), (1, 8), (2, 8)), -0.2, 0.2), 0.0, 1.0)
    velocities = noise(splits[1], (NX, NY, NZ, 3, SLOTS), 1.0, 6.0, ((0, 8), (1, 8), (2, 8)), jnp.float32)
    positions_next = jnp.clip(1.0 * jax.random.uniform(splits[2], (NX, NY, NZ, 3, SLOTS), jnp.float32) ** shard_levels(splits[2], (NX, NY, NZ, 3, SLOTS), ((0, 8), (1, 8), (2, 8)), -0.2, 0.2), 0.0, 1.0)
    halo_counts = draw_halo_counts(jax.random.fold_in(splits[6], 71), 0)
    neighbour_lists = draw_neighbour_lists(jax.random.fold_in(splits[6], 71), 0)
    descendants = draw_descendants(jax.random.fold_in(splits[6], 71), 0)
    return {"positions_now": positions_now, "velocities": velocities, "positions_next": positions_next, "halo_counts": halo_counts, "neighbour_lists": neighbour_lists, "descendants": descendants}


EPS_SQ = 0.01
STEP_DT = 0.3
HALF_KICK = 0.045

def offsets_of(code):
    return (code // 9 - 1, code // 3 % 3 - 1, code % 3 - 1)

def stack_state(positions_now, positions_next, halo_counts):
    slots = positions_now.shape[-1]
    live = (jnp.arange(slots, dtype=jnp.int32)[None, None, None, :] < halo_counts[..., None]).astype(jnp.float32)
    masses = positions_now[:, :, :, 3:4, :] * live[:, :, :, None, :]
    return (jnp.concatenate([positions_now[:, :, :, :3, :], masses, positions_next], axis=3), live)

def predict(padded, neighbour_lists, velocities, descendants, halo_counts):
    cx, cy, cz = neighbour_lists.shape[:3]
    width = neighbour_lists.shape[3]
    px, py, pz = (cx + 2, cy + 2, cz + 2)
    slots = padded.shape[-1]
    cells = cx * cy * cz
    flat = padded.reshape(px * py * pz, 7, slots)
    next_rows = jnp.transpose(flat[:, 4:7, :], (0, 2, 1)).reshape(px * py * pz * slots, 3)
    grid = jnp.indices((cx, cy, cz), dtype=jnp.int32).reshape(3, cells)
    base = ((grid[0] + 1) * py + grid[1] + 1) * pz + grid[2] + 1
    group = 32 if cells % 32 == 0 else cells
    blocks = cells // group
    lists = neighbour_lists.reshape(blocks, group, width)
    vel = velocities.reshape(blocks, group, 3, slots)
    desc = descendants.reshape(blocks, group, 2, slots)
    counts = halo_counts.reshape(blocks, group)
    bases = base.reshape(blocks, group)

    def one_group(items):
        base_g, list_g, vel_g, desc_g, count_g = items
        own = flat[base_g]
        pos = own[:, :3, :]

        def step(accel, code):
            dx, dy, dz = offsets_of(code)
            source = flat[base_g + dx * py * pz + dy * pz + dz]
            offset = jnp.stack([dx, dy, dz], 1).astype(jnp.float32)
            spot = offset[:, :, None] + source[:, :3, :]
            diff = spot[:, :, None, :] - pos[:, :, :, None]
            dist_sq = lax.optimization_barrier(jnp.sum(diff * diff, axis=1)) + EPS_SQ
            weight = source[:, 3, None, :] / (dist_sq * jnp.sqrt(dist_sq))
            return (accel + lax.optimization_barrier(jnp.sum(diff * weight[:, None, :, :], axis=3)), None)
        accel, _ = lax.scan(step, jnp.zeros(pos.shape, jnp.float32), jnp.transpose(list_g))
        predicted = pos + STEP_DT * vel_g + HALF_KICK * accel
        dcode = desc_g[:, 0, :]
        dslot = desc_g[:, 1, :]
        ddx, ddy, ddz = offsets_of(dcode)
        target = base_g[:, None] + ddx * py * pz + ddy * pz + ddz
        found = jnp.transpose(next_rows[target * slots + dslot], (0, 2, 1))
        offset = jnp.stack([ddx, ddy, ddz], 1).astype(jnp.float32)
        error = offset + found - predicted
        live = (jnp.arange(slots, dtype=jnp.int32)[None, :] < count_g[:, None]).astype(jnp.float32)
        drift = error * live[:, None, :]
        squared = lax.optimization_barrier(jnp.sum(error * error, axis=1)) * live
        return (drift, squared)
    drift, squared = lax.map(one_group, (bases, lists, vel, desc, counts))
    return (drift.reshape(cx, cy, cz, 3, slots), squared.reshape(cx, cy, cz, slots))

def reference(positions_now, velocities, positions_next, halo_counts, neighbour_lists, descendants):
    state, live = stack_state(positions_now, positions_next, halo_counts)
    padded = jnp.pad(state, ((1, 1), (1, 1), (1, 1), (0, 0), (0, 0)), mode='wrap')
    drift, squared = predict(padded, neighbour_lists, velocities, descendants, halo_counts)
    mean_sq = jnp.sum(squared) / jnp.sum(live)
    return (drift, squared / (mean_sq + 1e-06))
```

```python
import functools

import jax
import jax.numpy as jnp
from jax import lax
from jax.experimental import pallas as pl
from jax.experimental.pallas import tpu as pltpu
from jax.sharding import Mesh
from jax.sharding import PartitionSpec as P

AXES = ("gx", "gy_0", "gy_1", "gz_0", "gz_1")
GY = ("gy_0", "gy_1")
GZ = ("gz_0", "gz_1")
ZRING = ("gx", "gz_1")
XYC = ("gz_0", "gy_0", "gy_1")

EPS_SQ = 0.01
STEP_DT = 0.3
HALF_KICK = 0.045


def ring(count, step):
    return [(i, (i + step) % count) for i in range(count)]


def xhop_pairs(count):
    pairs = []
    for x in range(count):
        pairs.append((2 * x, 2 * ((x + 1) % count)))
        pairs.append((2 * x + 1, 2 * ((x - 1) % count) + 1))
    return pairs


def zring_pairs(low, step):
    total = 2 * low

    def flat(z):
        return (z % low) * 2 + z // low

    return [(flat(z), flat((z + step) % total)) for z in range(total)]


def split3(v):
    high = v.astype(jnp.bfloat16).astype(jnp.float32)
    rest = v - high
    mid = rest.astype(jnp.bfloat16).astype(jnp.float32)
    return high, mid, rest - mid


def kernel(half_ref, nbr_ref, cnt_ref, off_ref, st_ref, vel_ref, desc_ref, drift_ref, sq_ref, part_ref):
    cx, cy = vel_ref.shape[0], vel_ref.shape[1]
    width = nbr_ref.shape[3]
    half = half_ref[0]
    sub = lax.broadcasted_iota(jnp.int32, (8, 128), 0)
    lane = lax.broadcasted_iota(jnp.int32, (1, 128), 1)
    zero8 = jnp.zeros((8, 128), jnp.float32)

    def plane_of(dz):
        z = half + dz - 1
        return jnp.where(z < 0, 2, z)

    def one_cell(c, carry):
        total, count = carry
        x = c // cy
        y = c % cy
        own = st_ref[half, x + 1, y + 1]
        centred = jnp.where(sub < 3, own - 0.5, 0.0)
        norm = jnp.sum(centred * centred, axis=0, keepdims=True) + EPS_SQ
        p8 = jnp.where(sub < 3, -2.0 * centred, jnp.where(sub == 3, 1.0, jnp.where(sub == 4, norm, 0.0)))
        ph, pm, pll = split3(p8)
        pcat = jnp.concatenate([ph, ph, ph, pm, pm, pll] + [zero8] * 10, axis=0)
        pt = jnp.transpose(pcat).astype(jnp.bfloat16)
        acc = zero8
        for k in range(width):
            code = nbr_ref[x, y, 0, k]
            dx = code // 9
            dy = (code // 3) % 3
            dz = code % 3
            src = st_ref[plane_of(dz), x + dx, y + dy]
            spot = src + off_ref[code]
            inner = jnp.where(sub < 3, spot, 0.0)
            far = jnp.sum(inner * inner, axis=0, keepdims=True)
            s8 = jnp.where(sub < 3, spot, jnp.where(sub == 3, far, jnp.where(sub == 4, 1.0, 0.0)))
            m8 = jnp.where(sub < 3, spot, jnp.where(sub == 3, 1.0, 0.0)) * src[3:4]
            sh, sm, sl = split3(s8)
            scat = jnp.concatenate([sh, sm, sl, sh, sm, sh] + [zero8] * 10, axis=0).astype(jnp.bfloat16)
            dist = lax.dot_general(pt, scat, (((1,), (0,)), ((), ())), preferred_element_type=jnp.float32)
            inv = lax.rsqrt(dist)
            weight = inv * inv * inv
            wh = weight.astype(jnp.bfloat16)
            wl = (weight - wh.astype(jnp.float32)).astype(jnp.bfloat16)
            mh, mm, ml = split3(m8)
            mcat = jnp.concatenate([mh, mm, ml, zero8], axis=0).astype(jnp.bfloat16)
            nt = (((1,), (1,)), ((), ()))
            a1 = lax.dot_general(mcat, wh, nt, preferred_element_type=jnp.float32)
            a2 = lax.dot_general(mcat[:16], wl, nt, preferred_element_type=jnp.float32)
            acc = acc + ((a1[16:24] + a2[8:16]) + (a1[8:16] + a2[:8])) + a1[:8]
        accel = acc - centred * acc[3:4]
        dcode = desc_ref[x, y, 0, 0:1, :]
        dslot = jnp.broadcast_to(desc_ref[x, y, 0, 1:2, :], (8, 128))
        found = zero8
        for code in range(27):
            dx, dy, dz = code // 9, code // 3 % 3, code % 3
            src = st_ref[plane_of(dz), x + dx, y + dy]
            got = jnp.take_along_axis(src, dslot, axis=1)
            found = jnp.where(dcode == code, got, found)
        ox = (dcode >= 9).astype(jnp.int32) + (dcode >= 18).astype(jnp.int32)
        rest = dcode - 9 * ox
        oy = (rest >= 3).astype(jnp.int32) + (rest >= 6).astype(jnp.int32)
        oz = rest - 3 * oy
        offset = jnp.concatenate([ox, oy, oz], axis=0).astype(jnp.float32) - 1.0
        predicted = own[:3] + STEP_DT * vel_ref[x, y, 0] + HALF_KICK * accel[:3]
        error = offset + found[4:7] - predicted
        alive = lane < cnt_ref[x, y, 0]
        drift_ref[x, y, 0] = jnp.where(alive, error, 0.0)
        squared = jnp.where(alive, jnp.sum(error * error, axis=0, keepdims=True), 0.0)
        sq_ref[x, y] = squared
        return total + squared, count + cnt_ref[x, y, 0]

    total, count = lax.fori_loop(0, cx * cy, one_cell, (jnp.zeros((1, 128), jnp.float32), jnp.int32(0)))
    folded = total + pltpu.roll(jnp.broadcast_to(total, (8, 128)), 64, 1)[:1]
    live = jnp.where(lane == 64, count.astype(jnp.float32), 0.0)
    part_ref[...] = jnp.where(lane < 64, folded, live)


def shards(positions_now, velocities, positions_next, halo_counts, neighbour_lists, descendants):
    cx, cy, cz, _, slots = positions_now.shape
    half = lax.axis_index("gz_1")
    xs = lax.axis_size("gz_0")
    low = lax.axis_size("gx")
    live = (jnp.arange(slots, dtype=jnp.int32) < halo_counts[..., None]).astype(jnp.float32)
    mass = positions_now[..., 3:4, :] * live[..., None, :]
    own = jnp.concatenate(
        [positions_now[..., :3, :], mass, positions_next, jnp.zeros_like(mass)], axis=3
    )[:, :, 0]
    other = lax.ppermute(own, "gz_1", [(0, 1), (1, 0)])
    pair = jnp.where(half == 0, jnp.stack([own, other]), jnp.stack([other, own]))
    below = lax.ppermute(pair[:, cx - 1 :], ZRING, zring_pairs(low, 1))
    above = lax.ppermute(pair[:, :1], ZRING, zring_pairs(low, -1))
    pair = jnp.concatenate([below, pair, above], axis=1)
    sent = jnp.where(half == 0, pair[1], pair[0])
    far = lax.ppermute(sent, GZ, xhop_pairs(xs))
    cube = jnp.concatenate([pair, far[None]], axis=0)
    ny = lax.axis_size(GY)
    below = lax.ppermute(cube[:, :, cy - 1 :], GY, ring(ny, 1))
    above = lax.ppermute(cube[:, :, :1], GY, ring(ny, -1))
    cube = jnp.concatenate([below, cube, above], axis=2)
    codes = jnp.arange(27, dtype=jnp.int32)
    table = jnp.stack([codes // 9, codes // 3 % 3, codes % 3], 1).astype(jnp.float32) - 1.5
    table = jnp.broadcast_to(jnp.pad(table, ((0, 0), (0, 5)))[:, :, None], (27, 8, 128))
    smem = pl.BlockSpec(memory_space=pltpu.SMEM)
    vmem = pl.BlockSpec(memory_space=pltpu.VMEM)
    drift, squared, part = pl.pallas_call(
        kernel,
        in_specs=[smem, smem, smem, vmem, vmem, vmem, vmem],
        out_specs=[vmem, vmem, vmem],
        out_shape=[
            jax.ShapeDtypeStruct((cx, cy, cz, 3, slots), jnp.float32),
            jax.ShapeDtypeStruct((cx, cy, cz, slots), jnp.float32),
            jax.ShapeDtypeStruct((1, slots), jnp.float32),
        ],
        compiler_params=pltpu.CompilerParams(vmem_limit_bytes=32 << 20),
    )(half[None], neighbour_lists, halo_counts, table, cube, velocities, descendants)

    def gathered(row, axes):
        count = lax.axis_size(axes)
        rows = jnp.broadcast_to(row, (count, slots))
        return jnp.sum(lax.all_to_all(rows, axes, 0, 0, tiled=True), axis=0, keepdims=True)

    sums = gathered(gathered(part, XYC), ZRING)
    mean_sq = jnp.sum(sums[:, :64]) / jnp.sum(sums[:, 64:])
    return drift, squared / (mean_sq + 1e-06)


def solution(mesh):
    finer = Mesh(mesh.devices.reshape(mesh.shape["gx"], 4, 2, 4, 2), AXES)
    return jax.shard_map(
        shards,
        mesh=finer,
        in_specs=(
            P("gx", GY, GZ, None, None),
            P("gx", GY, GZ, None, None),
            P("gx", GY, GZ, None, None),
            P("gx", GY, GZ),
            P("gx", GY, GZ, None),
            P("gx", GY, GZ, None, None),
        ),
        out_specs=(P("gx", GY, GZ, None, None), P("gx", GY, GZ, None)),
        check_vma=False,
    )
```

```python
import functools

import jax
import jax.numpy as jnp
from jax import lax
from jax.experimental import pallas as pl
from jax.experimental.pallas import tpu as pltpu
from jax.sharding import Mesh
from jax.sharding import PartitionSpec as P

AXES = ("gx", "gy_0", "gy_1", "gz_0", "gz_1")
GY = ("gy_0", "gy_1")
GZ = ("gz_0", "gz_1")
ZRING = ("gx", "gz_1")
XYC = ("gz_0", "gy_0", "gy_1")

EPS_SQ = 0.01
STEP_DT = 0.3
HALF_KICK = 0.045


def ring(count, step):
    return [(i, (i + step) % count) for i in range(count)]


def xhop_pairs(count):
    pairs = []
    for x in range(count):
        pairs.append((2 * x, 2 * ((x + 1) % count)))
        pairs.append((2 * x + 1, 2 * ((x - 1) % count) + 1))
    return pairs


def zring_pairs(low, step):
    total = 2 * low

    def flat(z):
        return (z % low) * 2 + z // low

    return [(flat(z), flat((z + step) % total)) for z in range(total)]


def split3(v):
    high = v.astype(jnp.bfloat16).astype(jnp.float32)
    rest = v - high
    mid = rest.astype(jnp.bfloat16).astype(jnp.float32)
    return high, mid, rest - mid


def assemble(cnt_ref, now_ref, next_ref, own_ref):
    lane = lax.broadcasted_iota(jnp.int32, (1, 128), 1)
    for x in range(now_ref.shape[0]):
        for y in range(now_ref.shape[1]):
            own_ref[x, y, :3] = now_ref[x, y, 0, :3]
            own_ref[x, y, 3:4] = jnp.where(lane < cnt_ref[y, 0, x], now_ref[x, y, 0, 3:4], 0.0)
            own_ref[x, y, 4:7] = next_ref[x, y, :, 0]
            own_ref[x, y, 7:] = jnp.zeros((1, 128), jnp.float32)


def kernel(
    half_ref, nbr_ref, cnt_ref, off_ref, st_ref, vel_ref, desc_ref, drift_ref, sq_ref, part_ref, out_ref, sems
):
    cx, cy = vel_ref.shape[0], vel_ref.shape[1]
    width = nbr_ref.shape[3]
    half = half_ref[0]
    sub = lax.broadcasted_iota(jnp.int32, (8, 128), 0)
    wide = lax.broadcasted_iota(jnp.int32, (8, width * 128), 0)
    lane = lax.broadcasted_iota(jnp.int32, (1, 128), 1)
    f32, bf16 = jnp.float32, jnp.bfloat16

    def plane_of(dz):
        z = half + dz - 1
        return jnp.where(z < 0, 2, z)

    def acceleration(x, y, own):
        centred = jnp.where(sub < 3, own - 0.5, 0.0)
        norm = jnp.sum(centred * centred, axis=0, keepdims=True) + EPS_SQ
        p8 = jnp.where(sub < 3, -2.0 * centred, jnp.where(sub == 3, 1.0, jnp.where(sub == 4, norm, 0.0)))
        ph, pm, pl3 = split3(p8)
        pcat = jnp.concatenate([ph, ph, ph, pm, pm, pl3], axis=0).astype(bf16)
        spots, masses = [], []
        for k in range(width):
            code = nbr_ref[x, y, 0, k]
            dx = code // 9
            dy = (code // 3) % 3
            dz = code % 3
            src = st_ref[plane_of(dz), x + dx, y + dy]
            spots.append(src + off_ref[code])
            masses.append(src[3:4])
        spot = jnp.concatenate(spots, axis=1)
        mass = jnp.concatenate(masses, axis=1)
        inner = jnp.where(wide < 3, spot, 0.0)
        far = jnp.sum(inner * inner, axis=0, keepdims=True)
        s8 = jnp.where(wide < 3, spot, jnp.where(wide == 3, far, jnp.where(wide == 4, 1.0, 0.0)))
        m8 = jnp.where(wide < 3, spot, jnp.where(wide == 3, 1.0, 0.0)) * mass
        sh, sm, sl = split3(s8)
        mh, mm, ml = split3(m8)
        scat = jnp.transpose(jnp.concatenate([sh, sm, sl, sh, sm, sh], axis=0)).astype(bf16)
        mcat = jnp.concatenate([mh, mm, ml, jnp.zeros_like(ml)], axis=0).astype(bf16)
        dist = jnp.dot(scat, pcat, preferred_element_type=f32)
        inv = lax.rsqrt(dist)
        weight = inv * inv * inv
        wh = weight.astype(bf16)
        wl = (weight - wh.astype(f32)).astype(bf16)
        a1 = jnp.dot(mcat, wh, preferred_element_type=f32)
        a2 = jnp.dot(mcat[:16], wl, preferred_element_type=f32)
        acc = ((a1[16:24] + a2[8:16]) + (a1[8:16] + a2[:8])) + a1[:8]
        return acc - centred * acc[3:4]

    def one_cell(x, y):
        own = st_ref[half, x + 1, y + 1]
        accel = acceleration(x, y, own)
        dcode = desc_ref[x, y, 0, 0:1, :]
        dslot = jnp.broadcast_to(desc_ref[x, y, 0, 1:2, :], (8, 128))
        found = jnp.zeros((8, 128), f32)
        for code in range(27):
            dx, dy, dz = code // 9, code // 3 % 3, code % 3
            src = st_ref[plane_of(dz), x + dx, y + dy]
            got = jnp.take_along_axis(src, dslot, axis=1)
            found = jnp.where(dcode == code, got, found)
        ox = (dcode >= 9).astype(jnp.int32) + (dcode >= 18).astype(jnp.int32)
        rest = dcode - 9 * ox
        oy = (rest >= 3).astype(jnp.int32) + (rest >= 6).astype(jnp.int32)
        oz = rest - 3 * oy
        offset = jnp.concatenate([ox, oy, oz], axis=0).astype(f32) - 1.0
        predicted = own[:3] + STEP_DT * vel_ref[x, y, :, 0] + HALF_KICK * accel[:3]
        error = offset + found[4:7] - predicted
        alive = lane < cnt_ref[y, 0, x]
        out_ref[x, y, :, 0] = jnp.where(alive, error, 0.0)
        squared = jnp.where(alive, jnp.sum(error * error, axis=0, keepdims=True), 0.0)
        sq_ref[x, y] = squared
        return squared

    def one_row(x, carry):
        total, count = carry
        for y in range(cy):
            total = total + one_cell(x, y)
            count = count + cnt_ref[y, 0, x]
        pltpu.make_async_copy(out_ref.at[x], drift_ref.at[x], sems.at[x]).start()
        return total, count

    total, count = lax.fori_loop(0, cx, one_row, (jnp.zeros((1, 128), f32), jnp.int32(0)))
    folded = total + pltpu.roll(jnp.broadcast_to(total, (8, 128)), 64, 1)[:1]
    live = jnp.where(lane == 64, count.astype(f32), 0.0)
    part_ref[...] = jnp.where(lane < 64, folded, live)
    for x in range(cx):
        pltpu.make_async_copy(out_ref.at[x], drift_ref.at[x], sems.at[x]).wait()


def shards(positions_now, velocities, positions_next, halo_counts, neighbour_lists, descendants):
    cx, cy, cz, _, slots = positions_now.shape
    half = lax.axis_index("gz_1")
    xs = lax.axis_size("gz_0")
    low = lax.axis_size("gx")
    smem = pl.BlockSpec(memory_space=pltpu.SMEM)
    vmem = pl.BlockSpec(memory_space=pltpu.VMEM)
    nxt = jnp.transpose(positions_next, (0, 1, 3, 2, 4))
    vel = jnp.transpose(velocities, (0, 1, 3, 2, 4))
    counts = jnp.transpose(halo_counts, (1, 2, 0))
    own = pl.pallas_call(
        assemble,
        in_specs=[smem, vmem, vmem],
        out_specs=vmem,
        out_shape=jax.ShapeDtypeStruct((cx, cy, 8, slots), jnp.float32),
    )(counts, positions_now, nxt)
    other = lax.ppermute(own, "gz_1", [(0, 1), (1, 0)])
    pair = jnp.where(half == 0, jnp.stack([own, other]), jnp.stack([other, own]))
    below = lax.ppermute(pair[:, cx - 1 :], ZRING, zring_pairs(low, 1))
    above = lax.ppermute(pair[:, :1], ZRING, zring_pairs(low, -1))
    pair = jnp.concatenate([below, pair, above], axis=1)
    sent = jnp.where(half == 0, pair[1], pair[0])
    far = lax.ppermute(sent, GZ, xhop_pairs(xs))
    cube = jnp.concatenate([pair, far[None]], axis=0)
    ny = lax.axis_size(GY)
    below = lax.ppermute(cube[:, :, cy - 1 :], GY, ring(ny, 1))
    above = lax.ppermute(cube[:, :, :1], GY, ring(ny, -1))
    cube = jnp.concatenate([below, cube, above], axis=2)
    codes = jnp.arange(27, dtype=jnp.int32)
    table = jnp.stack([codes // 9, codes // 3 % 3, codes % 3], 1).astype(jnp.float32) - 1.5
    table = jnp.broadcast_to(jnp.pad(table, ((0, 0), (0, 5)))[:, :, None], (27, 8, 128))
    drift, squared, part = pl.pallas_call(
        kernel,
        in_specs=[smem, smem, smem, vmem, vmem, vmem, vmem],
        out_specs=[pl.BlockSpec(memory_space=pl.ANY), vmem, vmem],
        out_shape=[
            jax.ShapeDtypeStruct((cx, cy, 3, cz, slots), jnp.float32),
            jax.ShapeDtypeStruct((cx, cy, cz, slots), jnp.float32),
            jax.ShapeDtypeStruct((1, slots), jnp.float32),
        ],
        scratch_shapes=[
            pltpu.VMEM((cx, cy, 3, cz, slots), jnp.float32),
            pltpu.SemaphoreType.DMA((cx,)),
        ],
        compiler_params=pltpu.CompilerParams(vmem_limit_bytes=48 << 20),
    )(half[None], neighbour_lists, counts, table, cube, vel, descendants)

    def gathered(row, axes):
        count = lax.axis_size(axes)
        rows = jnp.broadcast_to(row, (count, slots))
        return jnp.sum(lax.all_to_all(rows, axes, 0, 0, tiled=True), axis=0, keepdims=True)

    sums = gathered(gathered(part, XYC), ZRING)
    mean_sq = jnp.sum(sums[:, :64]) / jnp.sum(sums[:, 64:])
    return jnp.transpose(drift, (0, 1, 3, 2, 4)), squared / (mean_sq + 1e-06)


def solution(mesh):
    finer = Mesh(mesh.devices.reshape(mesh.shape["gx"], 4, 2, 4, 2), AXES)
    return jax.shard_map(
        shards,
        mesh=finer,
        in_specs=(
            P("gx", GY, GZ, None, None),
            P("gx", GY, GZ, None, None),
            P("gx", GY, GZ, None, None),
            P("gx", GY, GZ),
            P("gx", GY, GZ, None),
            P("gx", GY, GZ, None, None),
        ),
        out_specs=(P("gx", GY, GZ, None, None), P("gx", GY, GZ, None)),
        check_vma=False,
    )
```

```python
import functools

import jax
import jax.numpy as jnp
import numpy as np
from jax import lax
from jax.experimental import pallas as pl
from jax.experimental.pallas import tpu as pltpu
from jax.sharding import Mesh
from jax.sharding import PartitionSpec as P

AXES = ("gx", "gy_0", "gy_1", "gz_0", "gz_1")
GY = ("gy_0", "gy_1")
GZ = ("gz_0", "gz_1")
ZRING = ("gx", "gz_1")
XYC = ("gz_0", "gy_0", "gy_1")

EPS_SQ = 0.01
STEP_DT = 0.3
HALF_KICK = 0.045


def ring(count, step):
    return [(i, (i + step) % count) for i in range(count)]


def xhop_pairs(count):
    pairs = []
    for x in range(count):
        pairs.append((2 * x, 2 * ((x + 1) % count)))
        pairs.append((2 * x + 1, 2 * ((x - 1) % count) + 1))
    return pairs


def zring_pairs(low, step):
    total = 2 * low

    def flat(z):
        return (z % low) * 2 + z // low

    return [(flat(z), flat((z + step) % total)) for z in range(total)]


def split3(v):
    high = v.astype(jnp.bfloat16).astype(jnp.float32)
    rest = v - high
    mid = rest.astype(jnp.bfloat16).astype(jnp.float32)
    return high, mid, rest - mid


def assemble(cnt_ref, now_ref, next_ref, own_ref):
    lane = lax.broadcasted_iota(jnp.int32, (1, 128), 1)
    for x in range(now_ref.shape[0]):
        for y in range(now_ref.shape[1]):
            own_ref[x, y, :3] = now_ref[x, y, 0, :3]
            own_ref[x, y, 3:4] = jnp.where(lane < cnt_ref[y, 0, x], now_ref[x, y, 0, 3:4], 0.0)
            own_ref[x, y, 4:7] = next_ref[x, y, :, 0]
            own_ref[x, y, 7:] = jnp.zeros((1, 128), jnp.float32)


CLASSES = 4
BATCH = 36
F32, BF16, I32 = jnp.float32, jnp.bfloat16, jnp.int32


def item_table(cx, cy):
    px = cx + 2
    table = np.zeros((2, 3, 3, 27), np.int32)
    for half in range(2):
        for xe in range(3):
            for ye in range(3):
                for code in range(27):
                    dx, dy, dz = code // 9, code // 3 % 3, code % 3
                    plane = 0 if dz == 1 else (1 if (dz == 2) == (half == 0) else 2)
                    x_in = not (xe == 0 and dx == 0 or xe == 2 and dx == 2)
                    if ye == 0 and dy == 0 or ye == 2 and dy == 2:
                        kind, step = 3, (3 * px if dy == 2 else 0) + plane * px + dx
                    elif plane == 2:
                        kind, step = 2, dx * cy + dy - 1
                    elif plane == 1:
                        kind, step = 1, dx * cy + dy - 1
                    elif x_in:
                        kind, step = 0, (dx - 1) * cy + dy - 1
                    else:
                        kind = 1
                        step = px * cy + dy - 1 if dx == 0 else (px + 1 - (cx - 1)) * cy + dy - 1
                    table[half, xe, ye, code] = 4 * (1024 * step + 32 * code) + kind
    return table.reshape(-1)


def offset_table():
    codes = np.arange(27)
    rows = np.stack([codes // 9, codes // 3 % 3, codes % 3], 1).astype(np.float32) - 0.5
    return np.broadcast_to(np.pad(rows, ((0, 0), (0, 5)))[:, :, None], (27, 8, 128)).copy()


def sublanes():
    return lax.broadcasted_iota(I32, (8, 128), 0)


def source_features(src, index, st_ref, mc_ref):
    sub = sublanes()
    q = jnp.where(sub < 3, src - 0.5, 0.0)
    norm = jnp.sum(q * q, axis=0, keepdims=True)
    s8 = jnp.where(sub < 3, -2.0 * q, jnp.where(sub == 3, norm, jnp.where(sub == 4, 1.0, 0.0)))
    m8 = jnp.where(sub == 3, 1.0, q) * src[3:4]
    sh, sm, sl = split3(s8)
    mh, mm, ml = split3(m8)
    st_ref[index] = jnp.transpose(jnp.concatenate([sh, sm, sl, sh, sm, sh], axis=0)).astype(BF16)
    mc_ref[index] = jnp.concatenate([mh, mm, ml, jnp.zeros_like(ml)], axis=0).astype(BF16)


def run_items(kind, cap, list_ref, count_ref, st_ref, mc_ref, own_of, off_ref, acc_ref):
    sub = sublanes()
    count = count_ref[kind]

    def batch(b, carry):
        sums = []
        for t in range(BATCH):
            place = b * BATCH + t
            valid = place < count
            item = jnp.where(valid, list_ref[kind * cap + place], 0)
            src, code, cell = item >> 10, (item >> 5) & 31, item & 31
            p = jnp.where(sub < 3, own_of(cell) - off_ref[code], 0.0)
            norm = jnp.sum(p * p, axis=0, keepdims=True) + EPS_SQ
            p8 = jnp.where(sub == 3, 1.0, jnp.where(sub == 4, norm, p))
            ph, pm, pr = split3(p8)
            pcat = jnp.concatenate([ph, ph, ph, pm, pm, pr], axis=0).astype(BF16)
            dist = jnp.dot(st_ref[src], pcat, preferred_element_type=F32)
            inv = lax.rsqrt(dist)
            weight = inv * inv * inv
            wh = weight.astype(BF16)
            wl = (weight - wh.astype(F32)).astype(BF16)
            mc = mc_ref[src]
            a = jnp.dot(
                jnp.concatenate([mc, mc], axis=1), jnp.concatenate([wh, wl], axis=0), preferred_element_type=F32
            )
            a8 = (a[16:24] + a[8:16]) + a[:8]
            sums.append((cell, (a8 - p * a8[3:4]) * valid.astype(F32)))
        for cell, add in sums:
            acc_ref[cell] = acc_ref[cell] + add
        return carry

    lax.fori_loop(0, (count + BATCH - 1) // BATCH, batch, 0)


def own_pass(half_ref, table_ref, nbr_ref, off_ref, own_ref, list_ref, count_ref, acc_ref, st_ref, mc_ref, *, cap):
    cx, cy = own_ref.shape[0], own_ref.shape[1]
    width = nbr_ref.shape[3]
    half = half_ref[0]
    for kind in range(CLASSES):
        count_ref[kind] = 0
    acc_ref[...] = jnp.zeros(acc_ref.shape, F32)

    def one_row(x, carry):
        xe = jnp.where(x == 0, 0, jnp.where(x == cx - 1, 2, 1))
        for y in range(cy):
            cell = x * cy + y
            ye = (0 if y == 0 else 1) if y < cy - 1 else 2
            row = ((half * 3 + xe) * 3 + ye) * 27
            for k in range(width):
                entry = table_ref[row + nbr_ref[x, y, 0, k]]
                kind = entry & 3
                item = (entry >> 2) + jnp.where(kind == 3, cell + 1024 * x, 1025 * cell)
                place = count_ref[kind]
                list_ref[kind * cap + place] = item
                count_ref[kind] = place + 1
            source_features(own_ref[x, y], cell, st_ref, mc_ref)
        return carry

    lax.fori_loop(0, cx, one_row, 0)
    run_items(0, cap, list_ref, count_ref, st_ref, mc_ref, lambda c: own_ref[c // cy, c % cy], off_ref, acc_ref)


def other_pass(list_ref, count_ref, off_ref, own_ref, other_ref, acc_ref, st_ref, mc_ref, *, cap):
    px, cy = own_ref.shape[0], own_ref.shape[1]
    acc_ref[...] = jnp.zeros(acc_ref.shape, F32)

    rows = px // 2

    def some_rows(part, carry):
        for step in range(rows):
            x = part * rows + step
            for y in range(cy):
                source_features(other_ref[x, y], x * cy + y, st_ref, mc_ref)
        return carry

    lax.fori_loop(0, 2, some_rows, 0)
    for y in range(cy):
        source_features(own_ref[0, y], px * cy + y, st_ref, mc_ref)
        source_features(own_ref[px - 1, y], (px + 1) * cy + y, st_ref, mc_ref)
    run_items(1, cap, list_ref, count_ref, st_ref, mc_ref, lambda c: own_ref[c // cy + 1, c % cy], off_ref, acc_ref)


def far_pass(list_ref, count_ref, off_ref, own_ref, far_ref, acc_ref, st_ref, mc_ref, *, cap):
    px, cy = own_ref.shape[0], own_ref.shape[1]
    acc_ref[...] = jnp.zeros(acc_ref.shape, F32)

    rows = px // 2

    def some_rows(part, carry):
        for step in range(rows):
            x = part * rows + step
            for y in range(cy):
                source_features(far_ref[x, y], x * cy + y, st_ref, mc_ref)
        return carry

    lax.fori_loop(0, 2, some_rows, 0)
    run_items(2, cap, list_ref, count_ref, st_ref, mc_ref, lambda c: own_ref[c // cy + 1, c % cy], off_ref, acc_ref)


def last_pass(
    half_ref, list_ref, count_ref, cnt_ref, off_ref, own_ref, other_ref, far_ref, low_ref, high_ref,
    acc0_ref, acc1_ref, acc2_ref, vel_ref, desc_ref,
    drift_ref, sq_ref, part_ref,
    acc_ref, st_ref, mc_ref, cube_ref, out_ref, sems, *, cap
):
    px, cy = own_ref.shape[0], own_ref.shape[1]
    cx = px - 2
    half = half_ref[0]
    lane = lax.broadcasted_iota(I32, (1, 128), 1)
    acc_ref[...] = acc0_ref[...] + acc1_ref[...] + acc2_ref[...]

    rows = px // 2

    def strips(part, carry):
        for step in range(rows):
            x = part * rows + step
            for plane in range(3):
                source_features(low_ref[plane, x], plane * px + x, st_ref, mc_ref)
                source_features(high_ref[plane, x], (3 + plane) * px + x, st_ref, mc_ref)
        return carry

    lax.fori_loop(0, 2, strips, 0)
    run_items(3, cap, list_ref, count_ref, st_ref, mc_ref, lambda c: own_ref[c // cy + 1, c % cy], off_ref, acc_ref)

    def fill(z, ref, plane):
        cube_ref[z, :, 0] = low_ref[plane]
        cube_ref[z, :, 1 : cy + 1] = ref[...]
        cube_ref[z, :, cy + 1] = high_ref[plane]

    fill(1, own_ref, 0)

    @pl.when(half == 0)
    def _():
        fill(0, far_ref, 2)
        fill(2, other_ref, 1)

    @pl.when(half != 0)
    def _():
        fill(0, other_ref, 1)
        fill(2, far_ref, 2)

    def one_cell(x, y):
        own = own_ref[x + 1, y]
        accel = acc_ref[x * cy + y]
        dcode = desc_ref[x, y, 0, 0:1, :]
        dslot = jnp.broadcast_to(desc_ref[x, y, 0, 1:2, :], (8, 128))
        found = jnp.zeros((8, 128), F32)
        for code in range(27):
            dx, dy, dz = code // 9, code // 3 % 3, code % 3
            got = jnp.take_along_axis(cube_ref[dz, x + dx, y + dy], dslot, axis=1)
            found = jnp.where(dcode == code, got, found)
        ox = (dcode >= 9).astype(I32) + (dcode >= 18).astype(I32)
        rest = dcode - 9 * ox
        oy = (rest >= 3).astype(I32) + (rest >= 6).astype(I32)
        oz = rest - 3 * oy
        offset = jnp.concatenate([ox, oy, oz], axis=0).astype(F32) - 1.0
        predicted = own[:3] + STEP_DT * vel_ref[x, y, :, 0] + HALF_KICK * accel[:3]
        error = offset + found[4:7] - predicted
        alive = lane < cnt_ref[y, 0, x]
        out_ref[x, y, :, 0] = jnp.where(alive, error, 0.0)
        squared = jnp.where(alive, jnp.sum(error * error, axis=0, keepdims=True), 0.0)
        sq_ref[x, y] = squared
        return squared

    def one_row(x, carry):
        total, count = carry
        for y in range(cy):
            total = total + one_cell(x, y)
            count = count + cnt_ref[y, 0, x]
        pltpu.make_async_copy(out_ref.at[x], drift_ref.at[x], sems.at[x]).start()
        return total, count

    total, count = lax.fori_loop(0, cx, one_row, (jnp.zeros((1, 128), F32), jnp.int32(0)))
    folded = total + pltpu.roll(jnp.broadcast_to(total, (8, 128)), 64, 1)[:1]
    live = jnp.where(lane == 64, count.astype(F32), 0.0)
    part_ref[...] = jnp.where(lane < 64, folded, live)
    for x in range(cx):
        pltpu.make_async_copy(out_ref.at[x], drift_ref.at[x], sems.at[x]).wait()


SMEM = pl.BlockSpec(memory_space=pltpu.SMEM)
VMEM = pl.BlockSpec(memory_space=pltpu.VMEM)


def cost(items):
    pairs = items * 128 * 128
    return pl.CostEstimate(flops=400 * pairs, transcendentals=pairs, bytes_accessed=1 << 20)


def params():
    return pltpu.CompilerParams(vmem_limit_bytes=40 << 20)


def features_of(sources):
    return [pltpu.VMEM((sources, 128, 48), BF16), pltpu.VMEM((sources, 32, 128), BF16)]


def first_forces(half, neighbour_lists, own):
    cx, cy = own.shape[:2]
    items = cx * cy * neighbour_lists.shape[3]
    cap = items + 2 * BATCH
    return pl.pallas_call(
        functools.partial(own_pass, cap=cap),
        in_specs=[SMEM, SMEM, SMEM, VMEM, VMEM],
        out_specs=[SMEM, SMEM, VMEM],
        out_shape=[
            jax.ShapeDtypeStruct((CLASSES * cap,), I32),
            jax.ShapeDtypeStruct((CLASSES,), I32),
            jax.ShapeDtypeStruct((cx * cy, 8, 128), F32),
        ],
        scratch_shapes=features_of(cx * cy),
        cost_estimate=cost(items // 4),
        compiler_params=params(),
    )(half, item_table(cx, cy), neighbour_lists, offset_table(), own)


def more_forces(body, lists, counts, own, planes):
    px, cy = own.shape[:2]
    cells = (px - 2) * cy
    cap = lists.shape[0] // CLASSES
    return pl.pallas_call(
        functools.partial(body, cap=cap),
        in_specs=[SMEM, SMEM, VMEM, VMEM, VMEM],
        out_specs=VMEM,
        out_shape=jax.ShapeDtypeStruct((cells, 8, 128), F32),
        scratch_shapes=features_of((px + 2) * cy),
        cost_estimate=cost(cap // 4),
        compiler_params=params(),
    )(lists, counts, offset_table(), own, planes)


def finish(half, lists, counts, cnt, own, other, far, low, high, sums, vel, descendants):
    px, cy = own.shape[:2]
    cx = px - 2
    cap = lists.shape[0] // CLASSES
    return pl.pallas_call(
        functools.partial(last_pass, cap=cap),
        in_specs=[SMEM] * 4 + [VMEM] * 11,
        out_specs=[pl.BlockSpec(memory_space=pl.ANY), VMEM, VMEM],
        out_shape=[
            jax.ShapeDtypeStruct((cx, cy, 3, 1, 128), F32),
            jax.ShapeDtypeStruct((cx, cy, 1, 128), F32),
            jax.ShapeDtypeStruct((1, 128), F32),
        ],
        scratch_shapes=[pltpu.VMEM((cx * cy, 8, 128), F32)]
        + features_of(6 * px)
        + [
            pltpu.VMEM((3, px, cy + 2, 8, 128), F32),
            pltpu.VMEM((cx, cy, 3, 1, 128), F32),
            pltpu.SemaphoreType.DMA((cx,)),
        ],
        cost_estimate=cost(cap // 4),
        compiler_params=params(),
    )(half, lists, counts, cnt, offset_table(), own, other, far, low, high, *sums, vel, descendants)


def shards(positions_now, velocities, positions_next, halo_counts, neighbour_lists, descendants):
    cx, cy, cz, _, slots = positions_now.shape
    half = lax.axis_index("gz_1")
    xs = lax.axis_size("gz_0")
    zs = lax.axis_size("gx")
    ny = lax.axis_size(GY)
    nxt = jnp.transpose(positions_next, (0, 1, 3, 2, 4))
    vel = jnp.transpose(velocities, (0, 1, 3, 2, 4))
    cnt = jnp.transpose(halo_counts, (1, 2, 0))
    own = pl.pallas_call(
        assemble,
        in_specs=[SMEM, VMEM, VMEM],
        out_specs=VMEM,
        out_shape=jax.ShapeDtypeStruct((cx, cy, 8, slots), F32),
    )(cnt, positions_now, nxt)
    other = lax.ppermute(own, "gz_1", [(0, 1), (1, 0)])
    lists, counts, acc0 = first_forces(half[None], neighbour_lists, own)

    def both(x):
        ends = own[x], other[x]
        return jnp.where(half == 0, jnp.stack(ends), jnp.stack(ends[::-1]))

    below = lax.ppermute(both(cx - 1), ZRING, zring_pairs(zs, 1))
    above = lax.ppermute(both(0), ZRING, zring_pairs(zs, -1))

    def widened(block, plane):
        ends = [jnp.where(plane == 0, v[0], v[1])[None] for v in (below, above)]
        return jnp.concatenate([ends[0], block, ends[1]], axis=0)

    own = widened(own, half)
    other = widened(other, 1 - half)
    far = lax.ppermute(other, GZ, xhop_pairs(xs))
    acc1 = more_forces(other_pass, lists, counts, own, other)
    planes = (own, other, far)
    low = lax.ppermute(jnp.stack([v[:, cy - 1] for v in planes]), GY, ring(ny, 1))
    high = lax.ppermute(jnp.stack([v[:, 0] for v in planes]), GY, ring(ny, -1))
    acc2 = more_forces(far_pass, lists, counts, own, far)
    drift, squared, part = finish(
        half[None], lists, counts, cnt, *planes, low, high, (acc0, acc1, acc2), vel, descendants
    )

    def gathered(row, axes):
        count = lax.axis_size(axes)
        rows = jnp.broadcast_to(row, (count, slots))
        return jnp.sum(lax.all_to_all(rows, axes, 0, 0, tiled=True), axis=0, keepdims=True)

    sums = gathered(gathered(part, XYC), ZRING)
    mean_sq = jnp.sum(sums[:, :64]) / jnp.sum(sums[:, 64:])
    return jnp.transpose(drift, (0, 1, 3, 2, 4)), squared / (mean_sq + 1e-06)


def solution(mesh):
    finer = Mesh(mesh.devices.reshape(mesh.shape["gx"], 4, 2, 4, 2), AXES)
    return jax.shard_map(
        shards,
        mesh=finer,
        in_specs=(
            P("gx", GY, GZ, None, None),
            P("gx", GY, GZ, None, None),
            P("gx", GY, GZ, None, None),
            P("gx", GY, GZ),
            P("gx", GY, GZ, None),
            P("gx", GY, GZ, None, None),
        ),
        out_specs=(P("gx", GY, GZ, None, None), P("gx", GY, GZ, None)),
        check_vma=False,
    )
```

```python
import functools

import jax
import jax.numpy as jnp
import numpy as np
from jax import lax
from jax.experimental import pallas as pl
from jax.experimental.pallas import tpu as pltpu
from jax.sharding import Mesh
from jax.sharding import PartitionSpec as P

AXES = ("gx", "gy_0", "gy_1", "gz_0", "gz_1")
GY = ("gy_0", "gy_1")
GZ = ("gz_0", "gz_1")
ZRING = ("gx", "gz_1")
XYC = ("gz_0", "gy_0", "gy_1")

EPS_SQ = 0.01
STEP_DT = 0.3
HALF_KICK = 0.045


def ring(count, step):
    return [(i, (i + step) % count) for i in range(count)]


def xhop_pairs(count):
    pairs = []
    for x in range(count):
        pairs.append((2 * x, 2 * ((x + 1) % count)))
        pairs.append((2 * x + 1, 2 * ((x - 1) % count) + 1))
    return pairs


def zring_pairs(low, step):
    total = 2 * low

    def flat(z):
        return (z % low) * 2 + z // low

    return [(flat(z), flat((z + step) % total)) for z in range(total)]


def split3(v):
    high = v.astype(jnp.bfloat16).astype(jnp.float32)
    rest = v - high
    mid = rest.astype(jnp.bfloat16).astype(jnp.float32)
    return high, mid, rest - mid


def assemble(cnt_ref, now_ref, next_ref, own_ref):
    lane = lax.broadcasted_iota(jnp.int32, (1, 128), 1)
    cx, cy = now_ref.shape[:2]
    for x in range(cx):
        for y in range(cy):
            cell = x * cy + y
            own_ref[cell, :3] = now_ref[x, y, 0, :3]
            own_ref[cell, 3:4] = jnp.where(lane < cnt_ref[y, 0, x], now_ref[x, y, 0, 3:4], 0.0)
            own_ref[cell, 4:7] = next_ref[x, y, :, 0]
            own_ref[cell, 7:] = jnp.zeros((1, 128), jnp.float32)


CLASSES = 4
BATCH = 36
F32, BF16, I32 = jnp.float32, jnp.bfloat16, jnp.int32


def item_table(cx, cy):
    px = cx + 2
    table = np.zeros((2, 3, 3, 27), np.int32)
    for half in range(2):
        for xe in range(3):
            for ye in range(3):
                for code in range(27):
                    dx, dy, dz = code // 9, code // 3 % 3, code % 3
                    plane = 0 if dz == 1 else (1 if (dz == 2) == (half == 0) else 2)
                    x_in = not (xe == 0 and dx == 0 or xe == 2 and dx == 2)
                    if ye == 0 and dy == 0 or ye == 2 and dy == 2:
                        kind, step = 3, (3 * px if dy == 2 else 0) + plane * px + dx
                    elif plane == 2:
                        kind, step = 2, dx * cy + dy - 1
                    elif plane == 1:
                        kind, step = 1, dx * cy + dy - 1
                    elif x_in:
                        kind, step = 0, (dx - 1) * cy + dy - 1
                    else:
                        kind = 1
                        step = px * cy + dy - 1 if dx == 0 else (px + 1 - (cx - 1)) * cy + dy - 1
                    table[half, xe, ye, code] = 4 * (1024 * step + 32 * code) + kind
    return table.reshape(-1)


def offset_table():
    codes = np.arange(27)
    rows = np.stack([codes // 9, codes // 3 % 3, codes % 3], 1).astype(np.float32) - 0.5
    return np.broadcast_to(np.pad(rows, ((0, 0), (0, 5)))[:, :, None], (27, 8, 128)).copy()


def sublanes():
    return lax.broadcasted_iota(I32, (8, 128), 0)


def source_features(src, index, st_ref, mc_ref):
    sub = sublanes()
    q = jnp.where(sub < 3, src - 0.5, 0.0)
    norm = jnp.sum(q * q, axis=0, keepdims=True)
    s8 = jnp.where(sub < 3, -2.0 * q, jnp.where(sub == 3, norm, jnp.where(sub == 4, 1.0, 0.0)))
    m8 = jnp.where(sub == 3, 1.0, q) * src[3:4]
    sh, sm, sl = split3(s8)
    mh, mm, ml = split3(m8)
    st_ref[index] = jnp.transpose(jnp.concatenate([sh, sm, sl, sh, sm, sh], axis=0)).astype(BF16)
    mc_ref[index] = jnp.concatenate([mh, mm, ml, jnp.zeros_like(ml)], axis=0).astype(BF16)


def run_items(kind, cap, list_ref, count_ref, st_ref, mc_ref, own_of, off_ref, acc_ref):
    sub = sublanes()
    count = count_ref[kind]

    def batch(b, carry):
        sums = []
        for t in range(BATCH):
            place = b * BATCH + t
            valid = place < count
            item = jnp.where(valid, list_ref[kind * cap + place], 0)
            src, code, cell = item >> 10, (item >> 5) & 31, item & 31
            p = jnp.where(sub < 3, own_of(cell) - off_ref[code], 0.0)
            norm = jnp.sum(p * p, axis=0, keepdims=True) + EPS_SQ
            p8 = jnp.where(sub == 3, 1.0, jnp.where(sub == 4, norm, p))
            ph, pm, pr = split3(p8)
            pcat = jnp.concatenate([ph, ph, ph, pm, pm, pr], axis=0).astype(BF16)
            dist = jnp.dot(st_ref[src], pcat, preferred_element_type=F32)
            inv = lax.rsqrt(dist)
            weight = inv * inv * inv
            wh = weight.astype(BF16)
            wl = (weight - wh.astype(F32)).astype(BF16)
            mc = mc_ref[src]
            a = jnp.dot(
                jnp.concatenate([mc, mc], axis=1), jnp.concatenate([wh, wl], axis=0), preferred_element_type=F32
            )
            a8 = (a[16:24] + a[8:16]) + a[:8]
            sums.append((cell, (a8 - p * a8[3:4]) * valid.astype(F32)))
        for cell, add in sums:
            acc_ref[cell] = acc_ref[cell] + add
        return carry

    lax.fori_loop(0, (count + BATCH - 1) // BATCH, batch, 0)


def own_pass(
    half_ref, table_ref, nbr_ref, cnt_ref, off_ref, own_ref, vel_ref, desc_ref,
    list_ref, count_ref, acc_ref, base_ref, link_ref, st_ref, mc_ref, *, cap
):
    cx, cy = nbr_ref.shape[:2]
    width = nbr_ref.shape[3]
    half = half_ref[0]
    lane = lax.broadcasted_iota(I32, (1, 128), 1)
    for kind in range(CLASSES):
        count_ref[kind] = 0
    acc_ref[...] = jnp.zeros(acc_ref.shape, F32)

    def one_row(x, carry):
        xe = jnp.where(x == 0, 0, jnp.where(x == cx - 1, 2, 1))
        for y in range(cy):
            cell = x * cy + y
            ye = (0 if y == 0 else 1) if y < cy - 1 else 2
            row = ((half * 3 + xe) * 3 + ye) * 27
            for k in range(width):
                entry = table_ref[row + nbr_ref[x, y, 0, k]]
                kind = entry & 3
                item = (entry >> 2) + jnp.where(kind == 3, cell + 1024 * x, 1025 * cell)
                place = count_ref[kind]
                list_ref[kind * cap + place] = item
                count_ref[kind] = place + 1
            own = own_ref[cell]
            source_features(own, cell, st_ref, mc_ref)
            dcode = desc_ref[x, y, 0, 0:1, :]
            ox = (dcode >= 9).astype(I32) + (dcode >= 18).astype(I32)
            rest = dcode - 9 * ox
            oy = (rest >= 3).astype(I32) + (rest >= 6).astype(I32)
            oz = rest - 3 * oy
            offset = jnp.concatenate([ox, oy, oz], axis=0).astype(F32) - 1.0
            base_ref[cell, :3] = offset - (own[:3] + STEP_DT * vel_ref[x, y, :, 0])
            base_ref[cell, 3:4] = (lane < cnt_ref[y, 0, x]).astype(F32)
            link_ref[cell, :2] = desc_ref[x, y, 0]
        return carry

    lax.fori_loop(0, cx, one_row, 0)
    run_items(0, cap, list_ref, count_ref, st_ref, mc_ref, lambda c: own_ref[c], off_ref, acc_ref)


def all_features(ref, count, st_ref, mc_ref):
    part = count // 2

    def some(i, carry):
        for step in range(part):
            source_features(ref[i * part + step], i * part + step, st_ref, mc_ref)
        return carry

    lax.fori_loop(0, 2, some, 0)


def other_pass(
    list_ref, count_ref, off_ref, own_ref, other_ref, acc_ref, top_ref, bottom_ref, st_ref, mc_ref, *, cap
):
    px = top_ref.shape[1]
    cells = own_ref.shape[0]
    cy = cells // px
    acc_ref[...] = jnp.zeros(acc_ref.shape, F32)
    for plane, ref in enumerate((own_ref, other_ref)):
        for x in range(px):
            top_ref[plane, x] = ref[x * cy + cy - 1]
            bottom_ref[plane, x] = ref[x * cy]
    all_features(other_ref, cells, st_ref, mc_ref)
    for y in range(cy):
        source_features(own_ref[y], cells + y, st_ref, mc_ref)
        source_features(own_ref[cells - cy + y], cells + cy + y, st_ref, mc_ref)
    run_items(1, cap, list_ref, count_ref, st_ref, mc_ref, lambda c: own_ref[c + cy], off_ref, acc_ref)


def far_pass(list_ref, count_ref, off_ref, own_ref, far_ref, acc_ref, st_ref, mc_ref, *, cap):
    edge = (own_ref.shape[0] - acc_ref.shape[0]) // 2
    acc_ref[...] = jnp.zeros(acc_ref.shape, F32)
    all_features(far_ref, far_ref.shape[0], st_ref, mc_ref)
    run_items(2, cap, list_ref, count_ref, st_ref, mc_ref, lambda c: own_ref[c + edge], off_ref, acc_ref)


def last_pass(
    half_ref, list_ref, count_ref, off_ref, own_ref, other_ref, far_ref, low_ref, high_ref,
    acc0_ref, acc1_ref, acc2_ref, base_ref, link_ref,
    drift_ref, sq_ref, part_ref,
    acc_ref, st_ref, mc_ref, cube_ref, out_ref, sems, *, cap
):
    cx, cy = out_ref.shape[:2]
    px = cx + 2
    half = half_ref[0]
    lane = lax.broadcasted_iota(I32, (1, 128), 1)
    acc_ref[...] = acc0_ref[...] + acc1_ref[...] + acc2_ref[...]
    rows = px // 2

    def strips(part, carry):
        for step in range(rows):
            x = part * rows + step
            for plane in range(3):
                source_features(low_ref[plane, x], plane * px + x, st_ref, mc_ref)
                source_features(high_ref[plane, x], (3 + plane) * px + x, st_ref, mc_ref)
        return carry

    lax.fori_loop(0, 2, strips, 0)
    run_items(3, cap, list_ref, count_ref, st_ref, mc_ref, lambda c: own_ref[c + cy], off_ref, acc_ref)

    def fill(z, ref, plane):
        for x in range(px):
            cube_ref[z, x, 0] = low_ref[plane, x]
            cube_ref[z, x, 1 : cy + 1] = ref[x * cy : (x + 1) * cy]
            cube_ref[z, x, cy + 1] = high_ref[plane, x]

    fill(1, own_ref, 0)

    @pl.when(half == 0)
    def _():
        fill(0, far_ref, 2)
        fill(2, other_ref, 1)

    @pl.when(half != 0)
    def _():
        fill(0, other_ref, 1)
        fill(2, far_ref, 2)

    def one_cell(x, y):
        cell = x * cy + y
        dcode = link_ref[cell, 0:1]
        dslot = jnp.broadcast_to(link_ref[cell, 1:2], (8, 128))
        found = jnp.zeros((8, 128), F32)
        for code in range(27):
            dx, dy, dz = code // 9, code // 3 % 3, code % 3
            got = jnp.take_along_axis(cube_ref[dz, x + dx, y + dy], dslot, axis=1)
            found = jnp.where(dcode == code, got, found)
        error = base_ref[cell, :3] + found[4:7] - HALF_KICK * acc_ref[cell, :3]
        alive = base_ref[cell, 3:4]
        out_ref[x, y, :, 0] = jnp.where(alive > 0.0, error, 0.0)
        squared = jnp.where(alive > 0.0, jnp.sum(error * error, axis=0, keepdims=True), 0.0)
        sq_ref[x, y] = squared
        return squared, alive

    def one_row(x, carry):
        total, live = carry
        for y in range(cy):
            squared, alive = one_cell(x, y)
            total = total + squared
            live = live + alive
        pltpu.make_async_copy(out_ref.at[x], drift_ref.at[x], sems.at[x]).start()
        return total, live

    zero = jnp.zeros((1, 128), F32)
    total, live = lax.fori_loop(0, cx, one_row, (zero, zero))

    def folded(v):
        return v + pltpu.roll(jnp.broadcast_to(v, (8, 128)), 64, 1)[:1]

    part_ref[...] = jnp.where(lane < 64, folded(total), folded(live))
    for x in range(cx):
        pltpu.make_async_copy(out_ref.at[x], drift_ref.at[x], sems.at[x]).wait()


def scaled(rows_ref, sq_ref, tension_ref):
    lane = lax.broadcasted_iota(I32, (1, 128), 1)
    sums = jnp.sum(rows_ref[...], axis=0, keepdims=True)
    total = jnp.sum(jnp.where(lane < 64, sums, 0.0), axis=1, keepdims=True)
    live = jnp.sum(jnp.where(lane < 64, 0.0, sums), axis=1, keepdims=True)
    bound = jnp.broadcast_to(total / live + 1e-06, (1, 128))
    for x in range(sq_ref.shape[0]):
        for y in range(sq_ref.shape[1]):
            tension_ref[x, y] = sq_ref[x, y] / bound


SMEM = pl.BlockSpec(memory_space=pltpu.SMEM)
VMEM = pl.BlockSpec(memory_space=pltpu.VMEM)


def cost(items):
    pairs = items * 128 * 128
    return pl.CostEstimate(flops=400 * pairs, transcendentals=pairs, bytes_accessed=1 << 20)


def params():
    return pltpu.CompilerParams(vmem_limit_bytes=40 << 20)


def features_of(sources):
    return [pltpu.VMEM((sources, 128, 48), BF16), pltpu.VMEM((sources, 32, 128), BF16)]


def first_forces(half, neighbour_lists, cnt, own, vel, descendants):
    cx, cy = neighbour_lists.shape[:2]
    cells = cx * cy
    items = cells * neighbour_lists.shape[3]
    cap = items + 2 * BATCH
    rows = jax.ShapeDtypeStruct((cells, 8, 128), F32)
    return pl.pallas_call(
        functools.partial(own_pass, cap=cap),
        in_specs=[SMEM] * 4 + [VMEM] * 4,
        out_specs=[SMEM, SMEM, VMEM, VMEM, VMEM],
        out_shape=[
            jax.ShapeDtypeStruct((CLASSES * cap,), I32),
            jax.ShapeDtypeStruct((CLASSES,), I32),
            rows,
            rows,
            jax.ShapeDtypeStruct((cells, 8, 128), I32),
        ],
        scratch_shapes=features_of(cells),
        cost_estimate=cost(items // 4),
        compiler_params=params(),
    )(half, item_table(cx, cy), neighbour_lists, cnt, offset_table(), own, vel, descendants)


def other_forces(lists, counts, own, other, cells, px):
    cap = lists.shape[0] // CLASSES
    strip = jax.ShapeDtypeStruct((2, px, 8, 128), F32)
    return pl.pallas_call(
        functools.partial(other_pass, cap=cap),
        in_specs=[SMEM, SMEM, VMEM, VMEM, VMEM],
        out_specs=[VMEM] * 3,
        out_shape=[jax.ShapeDtypeStruct((cells, 8, 128), F32), strip, strip],
        scratch_shapes=features_of(2 * own.shape[0] - cells),
        cost_estimate=cost(cap // 4),
        compiler_params=params(),
    )(lists, counts, offset_table(), own, other)


def far_forces(lists, counts, own, far, cells):
    cap = lists.shape[0] // CLASSES
    return pl.pallas_call(
        functools.partial(far_pass, cap=cap),
        in_specs=[SMEM, SMEM, VMEM, VMEM, VMEM],
        out_specs=VMEM,
        out_shape=jax.ShapeDtypeStruct((cells, 8, 128), F32),
        scratch_shapes=features_of(far.shape[0]),
        cost_estimate=cost(cap // 4),
        compiler_params=params(),
    )(lists, counts, offset_table(), own, far)


def finish(half, lists, counts, planes, low, high, sums, base, links, cx, cy):
    px = cx + 2
    cap = lists.shape[0] // CLASSES
    return pl.pallas_call(
        functools.partial(last_pass, cap=cap),
        in_specs=[SMEM] * 3 + [VMEM] * 11,
        out_specs=[pl.BlockSpec(memory_space=pl.ANY), VMEM, VMEM],
        out_shape=[
            jax.ShapeDtypeStruct((cx, cy, 3, 1, 128), F32),
            jax.ShapeDtypeStruct((cx, cy, 1, 128), F32),
            jax.ShapeDtypeStruct((1, 128), F32),
        ],
        scratch_shapes=[pltpu.VMEM((cx * cy, 8, 128), F32)]
        + features_of(6 * px)
        + [
            pltpu.VMEM((3, px, cy + 2, 8, 128), F32),
            pltpu.VMEM((cx, cy, 3, 1, 128), F32),
            pltpu.SemaphoreType.DMA((cx,)),
        ],
        cost_estimate=cost(cap // 4),
        compiler_params=params(),
    )(half, lists, counts, offset_table(), *planes, low, high, *sums, base, links)


def shards(positions_now, velocities, positions_next, halo_counts, neighbour_lists, descendants):
    cx, cy, cz, _, slots = positions_now.shape
    half = lax.axis_index("gz_1")
    xs = lax.axis_size("gz_0")
    zs = lax.axis_size("gx")
    ny = lax.axis_size(GY)
    nxt = jnp.transpose(positions_next, (0, 1, 3, 2, 4))
    vel = jnp.transpose(velocities, (0, 1, 3, 2, 4))
    cnt = jnp.transpose(halo_counts, (1, 2, 0))
    own = pl.pallas_call(
        assemble,
        in_specs=[SMEM, VMEM, VMEM],
        out_specs=VMEM,
        out_shape=jax.ShapeDtypeStruct((cx * cy, 8, slots), F32),
    )(cnt, positions_now, nxt)
    other = lax.ppermute(own, "gz_1", [(0, 1), (1, 0)])
    lists, counts, acc0, base, links = first_forces(half[None], neighbour_lists, cnt, own, vel, descendants)

    def both(start):
        ends = own[start : start + cy], other[start : start + cy]
        return jnp.where(half == 0, jnp.stack(ends), jnp.stack(ends[::-1]))

    below = lax.ppermute(both(cx * cy - cy), ZRING, zring_pairs(zs, 1))
    above = lax.ppermute(both(0), ZRING, zring_pairs(zs, -1))

    def widened(block, plane):
        ends = [jnp.where(plane == 0, v[0], v[1]) for v in (below, above)]
        return jnp.concatenate([ends[0], block, ends[1]], axis=0)

    own = widened(own, half)
    other = widened(other, 1 - half)
    far = lax.ppermute(other, GZ, xhop_pairs(xs))
    acc1, top, bottom = other_forces(lists, counts, own, other, cx * cy, cx + 2)
    rows = far.reshape(cx + 2, cy * 8, slots)
    low = lax.ppermute(jnp.concatenate([top, rows[None, :, 8 * cy - 8 :]]), GY, ring(ny, 1))
    high = lax.ppermute(jnp.concatenate([bottom, rows[None, :, :8]]), GY, ring(ny, -1))
    acc2 = far_forces(lists, counts, own, far, cx * cy)
    drift, squared, part = finish(
        half[None], lists, counts, (own, other, far), low, high, (acc0, acc1, acc2), base, links, cx, cy
    )

    def gathered(row, axes):
        count = lax.axis_size(axes)
        return lax.all_to_all(jnp.broadcast_to(row, (count, slots)), axes, 0, 0, tiled=True)

    sums = jnp.sum(gathered(part, XYC), axis=0, keepdims=True)
    tension = pl.pallas_call(
        scaled,
        in_specs=[VMEM, VMEM],
        out_specs=VMEM,
        out_shape=jax.ShapeDtypeStruct((cx, cy, cz, slots), F32),
    )(gathered(sums, ZRING), squared)
    return jnp.transpose(drift, (0, 1, 3, 2, 4)), tension


def solution(mesh):
    finer = Mesh(mesh.devices.reshape(mesh.shape["gx"], 4, 2, 4, 2), AXES)
    return jax.shard_map(
        shards,
        mesh=finer,
        in_specs=(
            P("gx", GY, GZ, None, None),
            P("gx", GY, GZ, None, None),
            P("gx", GY, GZ, None, None),
            P("gx", GY, GZ),
            P("gx", GY, GZ, None),
            P("gx", GY, GZ, None, None),
        ),
        out_specs=(P("gx", GY, GZ, None, None), P("gx", GY, GZ, None)),
        check_vma=False,
    )
```

```python
import functools

import jax
import jax.numpy as jnp
import numpy as np
from jax import lax
from jax.experimental import pallas as pl
from jax.experimental.pallas import tpu as pltpu
from jax.sharding import Mesh
from jax.sharding import PartitionSpec as P

AXES = ("gx", "gy_0", "gy_1", "gz_0", "gz_1")
GY = ("gy_0", "gy_1")
GZ = ("gz_0", "gz_1")
ZRING = ("gx", "gz_1")
XYC = ("gz_0", "gy_0", "gy_1")

EPS_SQ = 0.01
STEP_DT = 0.3
HALF_KICK = 0.045


def ring(count, step):
    return [(i, (i + step) % count) for i in range(count)]


def xhop_pairs(count):
    pairs = []
    for x in range(count):
        pairs.append((2 * x, 2 * ((x + 1) % count)))
        pairs.append((2 * x + 1, 2 * ((x - 1) % count) + 1))
    return pairs


def zring_pairs(low, step):
    total = 2 * low

    def flat(z):
        return (z % low) * 2 + z // low

    return [(flat(z), flat((z + step) % total)) for z in range(total)]


def split3(v):
    high = v.astype(jnp.bfloat16).astype(jnp.float32)
    rest = v - high
    mid = rest.astype(jnp.bfloat16).astype(jnp.float32)
    return high, mid, rest - mid


def assemble(cnt_ref, now_ref, next_ref, own_ref):
    lane = lax.broadcasted_iota(jnp.int32, (1, 128), 1)
    cx, cy = now_ref.shape[:2]
    for x in range(cx):
        for y in range(cy):
            cell = x * cy + y
            own_ref[cell, :3] = now_ref[x, y, 0, :3]
            own_ref[cell, 3:4] = jnp.where(lane < cnt_ref[y, 0, x], now_ref[x, y, 0, 3:4], 0.0)
            own_ref[cell, 4:7] = next_ref[x, y, :, 0]
            own_ref[cell, 7:] = jnp.zeros((1, 128), jnp.float32)


CLASSES = 4
BATCHES = (40, 38, 47, 44)
F32, BF16, I32 = jnp.float32, jnp.bfloat16, jnp.int32


def item_table(cx, cy):
    px = cx + 2
    table = np.zeros((2, 3, 3, 27), np.int32)
    for half in range(2):
        for xe in range(3):
            for ye in range(3):
                for code in range(27):
                    dx, dy, dz = code // 9, code // 3 % 3, code % 3
                    plane = 0 if dz == 1 else (1 if (dz == 2) == (half == 0) else 2)
                    x_in = not (xe == 0 and dx == 0 or xe == 2 and dx == 2)
                    if ye == 0 and dy == 0 or ye == 2 and dy == 2:
                        kind, step = 3, (3 * px if dy == 2 else 0) + plane * px + dx
                    elif plane == 2:
                        kind, step = 2, dx * cy + dy - 1
                    elif plane == 1:
                        kind, step = 1, dx * cy + dy - 1
                    elif x_in:
                        kind, step = 0, (dx - 1) * cy + dy - 1
                    else:
                        kind = 1
                        step = px * cy + dy - 1 if dx == 0 else (px + 1 - (cx - 1)) * cy + dy - 1
                    table[half, xe, ye, code] = 4 * (1024 * step + 32 * code) + kind
    return table.reshape(-1)


def offset_table():
    codes = np.arange(27)
    rows = np.stack([codes // 9, codes // 3 % 3, codes % 3], 1).astype(np.float32) - 0.5
    return np.broadcast_to(np.pad(rows, ((0, 0), (0, 5)))[:, :, None], (27, 8, 128)).copy()


def sublanes():
    return lax.broadcasted_iota(I32, (8, 128), 0)


def source_features(src, index, st_ref, mc_ref):
    sub = sublanes()
    q = jnp.where(sub < 3, src - 0.5, 0.0)
    norm = jnp.sum(q * q, axis=0, keepdims=True)
    s8 = jnp.where(sub < 3, -2.0 * q, jnp.where(sub == 3, norm, jnp.where(sub == 4, 1.0, 0.0)))
    m8 = jnp.where(sub == 3, 1.0, q) * src[3:4]
    sh, sm, sl = split3(s8)
    mh, mm, ml = split3(m8)
    st_ref[index] = jnp.transpose(jnp.concatenate([sh, sm, sl, sh, sm, sh], axis=0)).astype(BF16)
    mc_ref[index] = jnp.concatenate([mh, mm, ml, jnp.zeros_like(ml)], axis=0).astype(BF16)


def run_items(kind, cap, list_ref, count_ref, st_ref, mc_ref, own_of, off_ref, acc_ref):
    sub = sublanes()
    size = BATCHES[kind]
    count = count_ref[kind]

    def batch(b, carry):
        sums = []
        for t in range(size):
            place = b * size + t
            valid = place < count
            item = jnp.where(valid, list_ref[kind * cap + place], 0)
            src, code, cell = item >> 10, (item >> 5) & 31, item & 31
            p = jnp.where(sub < 3, own_of(cell) - off_ref[code], 0.0)
            norm = jnp.sum(p * p, axis=0, keepdims=True) + EPS_SQ
            p8 = jnp.where(sub == 3, 1.0, jnp.where(sub == 4, norm, p))
            ph, pm, pr = split3(p8)
            pcat = jnp.concatenate([ph, ph, ph, pm, pm, pr], axis=0).astype(BF16)
            dist = jnp.dot(st_ref[src], pcat, preferred_element_type=F32)
            inv = lax.rsqrt(dist)
            weight = inv * inv * inv
            wh = weight.astype(BF16)
            wl = (weight - wh.astype(F32)).astype(BF16)
            mc = mc_ref[src]
            a = jnp.dot(
                jnp.concatenate([mc, mc], axis=1), jnp.concatenate([wh, wl], axis=0), preferred_element_type=F32
            )
            a8 = (a[16:24] + a[8:16]) + a[:8]
            sums.append((cell, (a8 - p * a8[3:4]) * valid.astype(F32)))
        for cell, add in sums:
            acc_ref[cell] = acc_ref[cell] + add
        return carry

    lax.fori_loop(0, (count + size - 1) // size, batch, 0)


def own_pass(
    half_ref, table_ref, nbr_ref, cnt_ref, off_ref, own_ref, vel_ref, desc_ref,
    list_ref, count_ref, acc_ref, base_ref, link_ref, st_ref, mc_ref, *, cap
):
    cx, cy = nbr_ref.shape[:2]
    width = nbr_ref.shape[3]
    half = half_ref[0]
    lane = lax.broadcasted_iota(I32, (1, 128), 1)
    for kind in range(CLASSES):
        count_ref[kind] = 0
    acc_ref[...] = jnp.zeros(acc_ref.shape, F32)

    def one_row(x, carry):
        xe = jnp.where(x == 0, 0, jnp.where(x == cx - 1, 2, 1))
        for y in range(cy):
            cell = x * cy + y
            ye = (0 if y == 0 else 1) if y < cy - 1 else 2
            row = ((half * 3 + xe) * 3 + ye) * 27
            for k in range(width):
                entry = table_ref[row + nbr_ref[x, y, 0, k]]
                kind = entry & 3
                item = (entry >> 2) + jnp.where(kind == 3, cell + 1024 * x, 1025 * cell)
                place = count_ref[kind]
                list_ref[kind * cap + place] = item
                count_ref[kind] = place + 1
            own = own_ref[cell]
            source_features(own, cell, st_ref, mc_ref)
            dcode = desc_ref[x, y, 0, 0:1, :]
            ox = (dcode >= 9).astype(I32) + (dcode >= 18).astype(I32)
            rest = dcode - 9 * ox
            oy = (rest >= 3).astype(I32) + (rest >= 6).astype(I32)
            oz = rest - 3 * oy
            offset = jnp.concatenate([ox, oy, oz], axis=0).astype(F32) - 1.0
            base_ref[cell, :3] = offset - (own[:3] + STEP_DT * vel_ref[x, y, :, 0])
            base_ref[cell, 3:4] = (lane < cnt_ref[y, 0, x]).astype(F32)
            link_ref[cell, :2] = desc_ref[x, y, 0]
        return carry

    lax.fori_loop(0, cx, one_row, 0)
    run_items(0, cap, list_ref, count_ref, st_ref, mc_ref, lambda c: own_ref[c], off_ref, acc_ref)


def all_features(ref, count, st_ref, mc_ref):
    part = count // 2

    def some(i, carry):
        for step in range(part):
            source_features(ref[i * part + step], i * part + step, st_ref, mc_ref)
        return carry

    lax.fori_loop(0, 2, some, 0)


def other_pass(
    list_ref, count_ref, off_ref, own_ref, other_ref, acc_ref, top_ref, bottom_ref, st_ref, mc_ref, *, cap
):
    px = top_ref.shape[1]
    cells = own_ref.shape[0]
    cy = cells // px
    acc_ref[...] = jnp.zeros(acc_ref.shape, F32)
    for plane, ref in enumerate((own_ref, other_ref)):
        for x in range(px):
            top_ref[plane, x] = ref[x * cy + cy - 1]
            bottom_ref[plane, x] = ref[x * cy]
    all_features(other_ref, cells, st_ref, mc_ref)
    for y in range(cy):
        source_features(own_ref[y], cells + y, st_ref, mc_ref)
        source_features(own_ref[cells - cy + y], cells + cy + y, st_ref, mc_ref)
    run_items(1, cap, list_ref, count_ref, st_ref, mc_ref, lambda c: own_ref[c + cy], off_ref, acc_ref)


def far_pass(list_ref, count_ref, off_ref, own_ref, far_ref, acc_ref, st_ref, mc_ref, *, cap):
    edge = (own_ref.shape[0] - acc_ref.shape[0]) // 2
    acc_ref[...] = jnp.zeros(acc_ref.shape, F32)
    all_features(far_ref, far_ref.shape[0], st_ref, mc_ref)
    run_items(2, cap, list_ref, count_ref, st_ref, mc_ref, lambda c: own_ref[c + edge], off_ref, acc_ref)


def last_pass(
    half_ref, list_ref, count_ref, off_ref, own_ref, other_ref, far_ref, low_ref, high_ref,
    acc0_ref, acc1_ref, acc2_ref, base_ref, link_ref,
    drift_ref, sq_ref, part_ref,
    acc_ref, st_ref, mc_ref, cube_ref, out_ref, sems, *, cap
):
    cx, cy = out_ref.shape[:2]
    px = cx + 2
    half = half_ref[0]
    lane = lax.broadcasted_iota(I32, (1, 128), 1)
    acc_ref[...] = acc0_ref[...] + acc1_ref[...] + acc2_ref[...]
    rows = px // 2

    def strips(part, carry):
        for step in range(rows):
            x = part * rows + step
            for plane in range(3):
                source_features(low_ref[plane, x], plane * px + x, st_ref, mc_ref)
                source_features(high_ref[plane, x], (3 + plane) * px + x, st_ref, mc_ref)
        return carry

    lax.fori_loop(0, 2, strips, 0)
    run_items(3, cap, list_ref, count_ref, st_ref, mc_ref, lambda c: own_ref[c + cy], off_ref, acc_ref)

    def fill(z, ref, plane):
        for x in range(px):
            cube_ref[z, x, 0] = low_ref[plane, x]
            cube_ref[z, x, 1 : cy + 1] = ref[x * cy : (x + 1) * cy]
            cube_ref[z, x, cy + 1] = high_ref[plane, x]

    fill(1, own_ref, 0)

    @pl.when(half == 0)
    def _():
        fill(0, far_ref, 2)
        fill(2, other_ref, 1)

    @pl.when(half != 0)
    def _():
        fill(0, other_ref, 1)
        fill(2, far_ref, 2)

    def one_cell(x, y):
        cell = x * cy + y
        dcode = link_ref[cell, 0:1]
        dslot = jnp.broadcast_to(link_ref[cell, 1:2], (8, 128))
        found = jnp.zeros((8, 128), F32)
        for code in range(27):
            dx, dy, dz = code // 9, code // 3 % 3, code % 3
            got = jnp.take_along_axis(cube_ref[dz, x + dx, y + dy], dslot, axis=1)
            found = jnp.where(dcode == code, got, found)
        error = base_ref[cell, :3] + found[4:7] - HALF_KICK * acc_ref[cell, :3]
        alive = base_ref[cell, 3:4]
        out_ref[x, y, :, 0] = jnp.where(alive > 0.0, error, 0.0)
        squared = jnp.where(alive > 0.0, jnp.sum(error * error, axis=0, keepdims=True), 0.0)
        sq_ref[x, y] = squared
        return squared, alive

    def one_row(x, carry):
        total, live = carry
        for y in range(cy):
            squared, alive = one_cell(x, y)
            total = total + squared
            live = live + alive
        pltpu.make_async_copy(out_ref.at[x], drift_ref.at[x], sems.at[x]).start()
        return total, live

    zero = jnp.zeros((1, 128), F32)
    total, live = lax.fori_loop(0, cx, one_row, (zero, zero))

    def folded(v):
        return v + pltpu.roll(jnp.broadcast_to(v, (8, 128)), 64, 1)[:1]

    part_ref[...] = jnp.where(lane < 64, folded(total), folded(live))
    for x in range(cx):
        pltpu.make_async_copy(out_ref.at[x], drift_ref.at[x], sems.at[x]).wait()


def scaled(rows_ref, sq_ref, tension_ref):
    lane = lax.broadcasted_iota(I32, (1, 128), 1)
    sums = jnp.sum(rows_ref[...], axis=0, keepdims=True)
    total = jnp.sum(jnp.where(lane < 64, sums, 0.0), axis=1, keepdims=True)
    live = jnp.sum(jnp.where(lane < 64, 0.0, sums), axis=1, keepdims=True)
    bound = jnp.broadcast_to(total / live + 1e-06, (1, 128))
    for x in range(sq_ref.shape[0]):
        for y in range(sq_ref.shape[1]):
            tension_ref[x, y] = sq_ref[x, y] / bound


SMEM = pl.BlockSpec(memory_space=pltpu.SMEM)
VMEM = pl.BlockSpec(memory_space=pltpu.VMEM)


def cost(items):
    pairs = items * 128 * 128
    return pl.CostEstimate(flops=400 * pairs, transcendentals=pairs, bytes_accessed=1 << 20)


def params():
    return pltpu.CompilerParams(vmem_limit_bytes=40 << 20)


def small_params():
    return pltpu.CompilerParams(vmem_limit_bytes=4 << 20)


def features_of(sources):
    return [pltpu.VMEM((sources, 128, 48), BF16), pltpu.VMEM((sources, 32, 128), BF16)]


def first_forces(half, neighbour_lists, cnt, own, vel, descendants):
    cx, cy = neighbour_lists.shape[:2]
    cells = cx * cy
    items = cells * neighbour_lists.shape[3]
    cap = items + max(BATCHES)
    rows = jax.ShapeDtypeStruct((cells, 8, 128), F32)
    return pl.pallas_call(
        functools.partial(own_pass, cap=cap),
        in_specs=[SMEM] * 4 + [VMEM] * 4,
        out_specs=[SMEM, SMEM, VMEM, VMEM, VMEM],
        out_shape=[
            jax.ShapeDtypeStruct((CLASSES * cap,), I32),
            jax.ShapeDtypeStruct((CLASSES,), I32),
            rows,
            rows,
            jax.ShapeDtypeStruct((cells, 8, 128), I32),
        ],
        scratch_shapes=features_of(cells),
        cost_estimate=cost(items // 4),
        compiler_params=params(),
    )(half, item_table(cx, cy), neighbour_lists, cnt, offset_table(), own, vel, descendants)


def other_forces(lists, counts, own, other, cells, px):
    cap = lists.shape[0] // CLASSES
    strip = jax.ShapeDtypeStruct((2, px, 8, 128), F32)
    return pl.pallas_call(
        functools.partial(other_pass, cap=cap),
        in_specs=[SMEM, SMEM, VMEM, VMEM, VMEM],
        out_specs=[VMEM] * 3,
        out_shape=[jax.ShapeDtypeStruct((cells, 8, 128), F32), strip, strip],
        scratch_shapes=features_of(2 * own.shape[0] - cells),
        cost_estimate=cost(cap // 4),
        compiler_params=params(),
    )(lists, counts, offset_table(), own, other)


def far_forces(lists, counts, own, far, cells):
    cap = lists.shape[0] // CLASSES
    return pl.pallas_call(
        functools.partial(far_pass, cap=cap),
        in_specs=[SMEM, SMEM, VMEM, VMEM, VMEM],
        out_specs=VMEM,
        out_shape=jax.ShapeDtypeStruct((cells, 8, 128), F32),
        scratch_shapes=features_of(far.shape[0]),
        cost_estimate=cost(cap // 4),
        compiler_params=params(),
    )(lists, counts, offset_table(), own, far)


def finish(half, lists, counts, planes, low, high, sums, base, links, cx, cy):
    px = cx + 2
    cap = lists.shape[0] // CLASSES
    return pl.pallas_call(
        functools.partial(last_pass, cap=cap),
        in_specs=[SMEM] * 3 + [VMEM] * 11,
        out_specs=[pl.BlockSpec(memory_space=pl.ANY), VMEM, VMEM],
        out_shape=[
            jax.ShapeDtypeStruct((cx, cy, 3, 1, 128), F32),
            jax.ShapeDtypeStruct((cx, cy, 1, 128), F32),
            jax.ShapeDtypeStruct((1, 128), F32),
        ],
        scratch_shapes=[pltpu.VMEM((cx * cy, 8, 128), F32)]
        + features_of(6 * px)
        + [
            pltpu.VMEM((3, px, cy + 2, 8, 128), F32),
            pltpu.VMEM((cx, cy, 3, 1, 128), F32),
            pltpu.SemaphoreType.DMA((cx,)),
        ],
        cost_estimate=cost(cap // 4),
        compiler_params=params(),
    )(half, lists, counts, offset_table(), *planes, low, high, *sums, base, links)


def shards(positions_now, velocities, positions_next, halo_counts, neighbour_lists, descendants):
    cx, cy, cz, _, slots = positions_now.shape
    half = lax.axis_index("gz_1")
    xs = lax.axis_size("gz_0")
    zs = lax.axis_size("gx")
    ny = lax.axis_size(GY)
    nxt = jnp.transpose(positions_next, (0, 1, 3, 2, 4))
    vel = jnp.transpose(velocities, (0, 1, 3, 2, 4))
    cnt = jnp.transpose(halo_counts, (1, 2, 0))
    own = pl.pallas_call(
        assemble,
        in_specs=[SMEM, VMEM, VMEM],
        out_specs=VMEM,
        out_shape=jax.ShapeDtypeStruct((cx * cy, 8, slots), F32),
    )(cnt, positions_now, nxt)
    other = lax.ppermute(own, "gz_1", [(0, 1), (1, 0)])
    lists, counts, acc0, base, links = first_forces(half[None], neighbour_lists, cnt, own, vel, descendants)

    def both(start):
        ends = own[start : start + cy], other[start : start + cy]
        return jnp.where(half == 0, jnp.stack(ends), jnp.stack(ends[::-1]))

    below = lax.ppermute(both(cx * cy - cy), ZRING, zring_pairs(zs, 1))
    above = lax.ppermute(both(0), ZRING, zring_pairs(zs, -1))

    def widened(block, plane):
        ends = [jnp.where(plane == 0, v[0], v[1]) for v in (below, above)]
        return jnp.concatenate([ends[0], block, ends[1]], axis=0)

    own = widened(own, half)
    other = widened(other, 1 - half)
    far = lax.ppermute(other, GZ, xhop_pairs(xs))
    acc1, top, bottom = other_forces(lists, counts, own, other, cx * cy, cx + 2)
    rows = far.reshape(cx + 2, cy * 8, slots)
    low = lax.ppermute(jnp.concatenate([top, rows[None, :, 8 * cy - 8 :]]), GY, ring(ny, 1))
    high = lax.ppermute(jnp.concatenate([bottom, rows[None, :, :8]]), GY, ring(ny, -1))
    acc2 = far_forces(lists, counts, own, far, cx * cy)
    drift, squared, part = finish(
        half[None], lists, counts, (own, other, far), low, high, (acc0, acc1, acc2), base, links, cx, cy
    )

    def gathered(row, axes):
        count = lax.axis_size(axes)
        return lax.all_to_all(jnp.broadcast_to(row, (count, slots)), axes, 0, 0, tiled=True)

    sums = jnp.sum(gathered(part, XYC), axis=0, keepdims=True)
    tension = pl.pallas_call(
        scaled,
        in_specs=[VMEM, VMEM],
        out_specs=VMEM,
        out_shape=jax.ShapeDtypeStruct((cx, cy, cz, slots), F32),
        compiler_params=small_params(),
    )(gathered(sums, ZRING), squared)
    return jnp.transpose(drift, (0, 1, 3, 2, 4)), tension


def solution(mesh):
    finer = Mesh(mesh.devices.reshape(mesh.shape["gx"], 4, 2, 4, 2), AXES)
    return jax.shard_map(
        shards,
        mesh=finer,
        in_specs=(
            P("gx", GY, GZ, None, None),
            P("gx", GY, GZ, None, None),
            P("gx", GY, GZ, None, None),
            P("gx", GY, GZ),
            P("gx", GY, GZ, None),
            P("gx", GY, GZ, None, None),
        ),
        out_specs=(P("gx", GY, GZ, None, None), P("gx", GY, GZ, None)),
        check_vma=False,
    )
```

```python
import functools

import jax
import jax.numpy as jnp
import numpy as np
from jax import lax
from jax.experimental import pallas as pl
from jax.experimental.pallas import tpu as pltpu
from jax.sharding import Mesh
from jax.sharding import PartitionSpec as P

AXES = ("gx", "gy_0", "gy_1", "gz_0", "gz_1")
GY = ("gy_0", "gy_1")
GZ = ("gz_0", "gz_1")
ZRING = ("gx", "gz_1")
XYC = ("gz_0", "gy_0", "gy_1")

EPS_SQ = 0.01
STEP_DT = 0.3
HALF_KICK = 0.045


def ring(count, step):
    return [(i, (i + step) % count) for i in range(count)]


def xhop_pairs(count):
    pairs = []
    for x in range(count):
        pairs.append((2 * x, 2 * ((x + 1) % count)))
        pairs.append((2 * x + 1, 2 * ((x - 1) % count) + 1))
    return pairs


def zring_pairs(low, step):
    total = 2 * low

    def flat(z):
        return (z % low) * 2 + z // low

    return [(flat(z), flat((z + step) % total)) for z in range(total)]


def split3(v):
    high = v.astype(jnp.bfloat16).astype(jnp.float32)
    rest = v - high
    mid = rest.astype(jnp.bfloat16).astype(jnp.float32)
    return high, mid, rest - mid


def assemble(cnt_ref, now_ref, next_ref, own_ref):
    lane = lax.broadcasted_iota(jnp.int32, (1, 128), 1)
    cx, cy = now_ref.shape[:2]
    for x in range(cx):
        for y in range(cy):
            cell = x * cy + y
            own_ref[cell, :3] = now_ref[x, y, 0, :3]
            own_ref[cell, 3:4] = jnp.where(lane < cnt_ref[y, 0, x], now_ref[x, y, 0, 3:4], 0.0)
            own_ref[cell, 4:7] = next_ref[x, y, :, 0]
            own_ref[cell, 7:] = jnp.zeros((1, 128), jnp.float32)


CLASSES = 4
BATCHES = (40, 75, 70, 88)
F32, BF16, I32 = jnp.float32, jnp.bfloat16, jnp.int32


def item_table(cx, cy):
    px = cx + 2
    table = np.zeros((2, 3, 3, 27), np.int32)
    for half in range(2):
        for xe in range(3):
            for ye in range(3):
                for code in range(27):
                    dx, dy, dz = code // 9, code // 3 % 3, code % 3
                    plane = 0 if dz == 1 else (1 if (dz == 2) == (half == 0) else 2)
                    x_in = not (xe == 0 and dx == 0 or xe == 2 and dx == 2)
                    if ye == 0 and dy == 0 or ye == 2 and dy == 2:
                        kind, step = 3, (3 * px if dy == 2 else 0) + plane * px + dx
                    elif plane == 2:
                        kind, step = 2, dx * cy + dy - 1
                    elif plane == 1:
                        kind, step = 1, dx * cy + dy - 1
                    elif x_in:
                        kind, step = 0, (dx - 1) * cy + dy - 1
                    else:
                        kind = 1
                        step = px * cy + dy - 1 if dx == 0 else (px + 1 - (cx - 1)) * cy + dy - 1
                    table[half, xe, ye, code] = 4 * (1024 * step + 32 * code) + kind
    return table.reshape(-1)


def offset_table():
    codes = np.arange(27)
    rows = np.stack([codes // 9, codes // 3 % 3, codes % 3], 1).astype(np.float32) - 0.5
    return np.broadcast_to(np.pad(rows, ((0, 0), (0, 5)))[:, :, None], (27, 8, 128)).copy()


def sublanes():
    return lax.broadcasted_iota(I32, (8, 128), 0)


def source_features(src, index, st_ref, mc_ref):
    sub = sublanes()
    q = jnp.where(sub < 3, src - 0.5, 0.0)
    norm = jnp.sum(q * q, axis=0, keepdims=True)
    s8 = jnp.where(sub < 3, -2.0 * q, jnp.where(sub == 3, norm, jnp.where(sub == 4, 1.0, 0.0)))
    m8 = jnp.where(sub == 3, 1.0, q) * src[3:4]
    sh, sm, sl = split3(s8)
    mh, mm, ml = split3(m8)
    st_ref[index] = jnp.transpose(jnp.concatenate([sh, sm, sl, sh, sm, sh], axis=0)).astype(BF16)
    mc_ref[index] = jnp.concatenate([mh, mm, ml, jnp.zeros_like(ml)], axis=0).astype(BF16)


def run_items(kind, cap, list_ref, count_ref, st_ref, mc_ref, own_of, off_ref, acc_ref):
    sub = sublanes()
    size = BATCHES[kind]
    count = count_ref[kind]

    def batch(b, carry):
        sums = []
        for t in range(size):
            place = b * size + t
            valid = place < count
            item = jnp.where(valid, list_ref[kind * cap + place], 0)
            src, code, cell = item >> 10, (item >> 5) & 31, item & 31
            p = jnp.where(sub < 3, own_of(cell) - off_ref[code], 0.0)
            norm = jnp.sum(p * p, axis=0, keepdims=True) + EPS_SQ
            p8 = jnp.where(sub == 3, 1.0, jnp.where(sub == 4, norm, p))
            ph, pm, pr = split3(p8)
            pcat = jnp.concatenate([ph, ph, ph, pm, pm, pr], axis=0).astype(BF16)
            dist = jnp.dot(st_ref[src], pcat, preferred_element_type=F32)
            inv = lax.rsqrt(dist)
            weight = inv * inv * inv
            wh = weight.astype(BF16)
            wl = (weight - wh.astype(F32)).astype(BF16)
            mc = mc_ref[src]
            a = jnp.dot(
                jnp.concatenate([mc, mc], axis=1), jnp.concatenate([wh, wl], axis=0), preferred_element_type=F32
            )
            a8 = (a[16:24] + a[8:16]) + a[:8]
            sums.append((cell, (a8 - p * a8[3:4]) * valid.astype(F32)))
        for cell, add in sums:
            acc_ref[cell] = acc_ref[cell] + add
        return carry

    lax.fori_loop(0, (count + size - 1) // size, batch, 0)


def own_pass(
    half_ref, table_ref, nbr_ref, cnt_ref, off_ref, own_ref, vel_ref, desc_ref,
    list_ref, count_ref, acc_ref, base_ref, link_ref, st_ref, mc_ref, *, cap
):
    cx, cy = nbr_ref.shape[:2]
    width = nbr_ref.shape[3]
    half = half_ref[0]
    lane = lax.broadcasted_iota(I32, (1, 128), 1)
    for kind in range(CLASSES):
        count_ref[kind] = 0
    acc_ref[...] = jnp.zeros(acc_ref.shape, F32)

    def one_row(x, carry):
        xe = jnp.where(x == 0, 0, jnp.where(x == cx - 1, 2, 1))
        for y in range(cy):
            cell = x * cy + y
            ye = (0 if y == 0 else 1) if y < cy - 1 else 2
            row = ((half * 3 + xe) * 3 + ye) * 27
            for k in range(width):
                entry = table_ref[row + nbr_ref[x, y, 0, k]]
                kind = entry & 3
                item = (entry >> 2) + jnp.where(kind == 3, cell + 1024 * x, 1025 * cell)
                place = count_ref[kind]
                list_ref[kind * cap + place] = item
                count_ref[kind] = place + 1
            own = own_ref[cell]
            source_features(own, cell, st_ref, mc_ref)
            dcode = desc_ref[x, y, 0, 0:1, :]
            ox = (dcode >= 9).astype(I32) + (dcode >= 18).astype(I32)
            rest = dcode - 9 * ox
            oy = (rest >= 3).astype(I32) + (rest >= 6).astype(I32)
            oz = rest - 3 * oy
            offset = jnp.concatenate([ox, oy, oz], axis=0).astype(F32) - 1.0
            base_ref[cell, :3] = offset - (own[:3] + STEP_DT * vel_ref[x, y, :, 0])
            base_ref[cell, 3:4] = (lane < cnt_ref[y, 0, x]).astype(F32)
            link_ref[cell, :2] = desc_ref[x, y, 0]
        return carry

    lax.fori_loop(0, cx, one_row, 0)
    run_items(0, cap, list_ref, count_ref, st_ref, mc_ref, lambda c: own_ref[c], off_ref, acc_ref)


def all_features(ref, count, st_ref, mc_ref):
    part = count // 2

    def some(i, carry):
        for step in range(part):
            source_features(ref[i * part + step], i * part + step, st_ref, mc_ref)
        return carry

    lax.fori_loop(0, 2, some, 0)


def other_pass(
    list_ref, count_ref, off_ref, own_ref, other_ref, acc_ref, top_ref, bottom_ref, st_ref, mc_ref, *, cap
):
    px = top_ref.shape[1]
    cells = own_ref.shape[0]
    cy = cells // px
    acc_ref[...] = jnp.zeros(acc_ref.shape, F32)
    for plane, ref in enumerate((own_ref, other_ref)):
        for x in range(px):
            top_ref[plane, x] = ref[x * cy + cy - 1]
            bottom_ref[plane, x] = ref[x * cy]
    all_features(other_ref, cells, st_ref, mc_ref)
    for y in range(cy):
        source_features(own_ref[y], cells + y, st_ref, mc_ref)
        source_features(own_ref[cells - cy + y], cells + cy + y, st_ref, mc_ref)
    run_items(1, cap, list_ref, count_ref, st_ref, mc_ref, lambda c: own_ref[c + cy], off_ref, acc_ref)


def far_pass(list_ref, count_ref, off_ref, own_ref, far_ref, acc_ref, st_ref, mc_ref, *, cap):
    edge = (own_ref.shape[0] - acc_ref.shape[0]) // 2
    acc_ref[...] = jnp.zeros(acc_ref.shape, F32)
    all_features(far_ref, far_ref.shape[0], st_ref, mc_ref)
    run_items(2, cap, list_ref, count_ref, st_ref, mc_ref, lambda c: own_ref[c + edge], off_ref, acc_ref)


def last_pass(
    half_ref, list_ref, count_ref, off_ref, own_ref, other_ref, far_ref, low_ref, high_ref,
    acc0_ref, acc1_ref, acc2_ref, base_ref, link_ref,
    drift_ref, sq_ref, part_ref,
    acc_ref, st_ref, mc_ref, cube_ref, *, cap
):
    cx, cy = drift_ref.shape[:2]
    px = cx + 2
    half = half_ref[0]
    lane = lax.broadcasted_iota(I32, (1, 128), 1)
    acc_ref[...] = acc0_ref[...] + acc1_ref[...] + acc2_ref[...]
    rows = px // 2

    def strips(part, carry):
        for step in range(rows):
            x = part * rows + step
            for plane in range(3):
                source_features(low_ref[plane, x], plane * px + x, st_ref, mc_ref)
                source_features(high_ref[plane, x], (3 + plane) * px + x, st_ref, mc_ref)
        return carry

    lax.fori_loop(0, 2, strips, 0)
    run_items(3, cap, list_ref, count_ref, st_ref, mc_ref, lambda c: own_ref[c + cy], off_ref, acc_ref)

    def fill(z, ref, plane):
        for x in range(px):
            cube_ref[z, x, 0] = low_ref[plane, x]
            cube_ref[z, x, 1 : cy + 1] = ref[x * cy : (x + 1) * cy]
            cube_ref[z, x, cy + 1] = high_ref[plane, x]

    fill(1, own_ref, 0)

    @pl.when(half == 0)
    def _():
        fill(0, far_ref, 2)
        fill(2, other_ref, 1)

    @pl.when(half != 0)
    def _():
        fill(0, other_ref, 1)
        fill(2, far_ref, 2)

    def one_cell(x, y):
        cell = x * cy + y
        dcode = link_ref[cell, 0:1]
        dslot = jnp.broadcast_to(link_ref[cell, 1:2], (8, 128))
        found = jnp.zeros((8, 128), F32)
        for code in range(27):
            dx, dy, dz = code // 9, code // 3 % 3, code % 3
            got = jnp.take_along_axis(cube_ref[dz, x + dx, y + dy], dslot, axis=1)
            found = jnp.where(dcode == code, got, found)
        error = base_ref[cell, :3] + found[4:7] - HALF_KICK * acc_ref[cell, :3]
        alive = base_ref[cell, 3:4]
        drift_ref[x, y, :, 0] = jnp.where(alive > 0.0, error, 0.0)
        squared = jnp.where(alive > 0.0, jnp.sum(error * error, axis=0, keepdims=True), 0.0)
        sq_ref[x, y] = squared
        return squared, alive

    def one_row(x, carry):
        total, live = carry
        for y in range(cy):
            squared, alive = one_cell(x, y)
            total = total + squared
            live = live + alive
        return total, live

    zero = jnp.zeros((1, 128), F32)
    total, live = lax.fori_loop(0, cx, one_row, (zero, zero), unroll=4)

    def folded(v):
        return v + pltpu.roll(jnp.broadcast_to(v, (8, 128)), 64, 1)[:1]

    part_ref[...] = jnp.where(lane < 64, folded(total), folded(live))


def scaled(rows_ref, sq_ref, drift_ref, tension_ref, out_ref, sem):
    copy = pltpu.make_async_copy(drift_ref, out_ref, sem)
    copy.start()
    lane = lax.broadcasted_iota(I32, (1, 128), 1)
    sums = jnp.sum(rows_ref[...], axis=0, keepdims=True)
    total = jnp.sum(jnp.where(lane < 64, sums, 0.0), axis=1, keepdims=True)
    live = jnp.sum(jnp.where(lane < 64, 0.0, sums), axis=1, keepdims=True)
    bound = jnp.broadcast_to(total / live + 1e-06, (1, 128))
    for x in range(sq_ref.shape[0]):
        for y in range(sq_ref.shape[1]):
            tension_ref[x, y] = sq_ref[x, y] / bound
    copy.wait()


SMEM = pl.BlockSpec(memory_space=pltpu.SMEM)
VMEM = pl.BlockSpec(memory_space=pltpu.VMEM)


def cost(items):
    pairs = items * 128 * 128
    return pl.CostEstimate(flops=400 * pairs, transcendentals=pairs, bytes_accessed=1 << 20)


def params():
    return pltpu.CompilerParams(vmem_limit_bytes=40 << 20)


def small_params():
    return pltpu.CompilerParams(vmem_limit_bytes=4 << 20)


def features_of(sources):
    return [pltpu.VMEM((sources, 128, 48), BF16), pltpu.VMEM((sources, 32, 128), BF16)]


def first_forces(half, neighbour_lists, cnt, own, vel, descendants):
    cx, cy = neighbour_lists.shape[:2]
    cells = cx * cy
    items = cells * neighbour_lists.shape[3]
    cap = items + max(BATCHES)
    rows = jax.ShapeDtypeStruct((cells, 8, 128), F32)
    return pl.pallas_call(
        functools.partial(own_pass, cap=cap),
        in_specs=[SMEM] * 4 + [VMEM] * 4,
        out_specs=[SMEM, SMEM, VMEM, VMEM, VMEM],
        out_shape=[
            jax.ShapeDtypeStruct((CLASSES * cap,), I32),
            jax.ShapeDtypeStruct((CLASSES,), I32),
            rows,
            rows,
            jax.ShapeDtypeStruct((cells, 8, 128), I32),
        ],
        scratch_shapes=features_of(cells),
        cost_estimate=cost(items // 4),
        compiler_params=params(),
    )(half, item_table(cx, cy), neighbour_lists, cnt, offset_table(), own, vel, descendants)


def other_forces(lists, counts, own, other, cells, px):
    cap = lists.shape[0] // CLASSES
    strip = jax.ShapeDtypeStruct((2, px, 8, 128), F32)
    return pl.pallas_call(
        functools.partial(other_pass, cap=cap),
        in_specs=[SMEM, SMEM, VMEM, VMEM, VMEM],
        out_specs=[VMEM] * 3,
        out_shape=[jax.ShapeDtypeStruct((cells, 8, 128), F32), strip, strip],
        scratch_shapes=features_of(2 * own.shape[0] - cells),
        cost_estimate=cost(cap // 4),
        compiler_params=params(),
    )(lists, counts, offset_table(), own, other)


def far_forces(lists, counts, own, far, cells):
    cap = lists.shape[0] // CLASSES
    return pl.pallas_call(
        functools.partial(far_pass, cap=cap),
        in_specs=[SMEM, SMEM, VMEM, VMEM, VMEM],
        out_specs=VMEM,
        out_shape=jax.ShapeDtypeStruct((cells, 8, 128), F32),
        scratch_shapes=features_of(far.shape[0]),
        cost_estimate=cost(cap // 4),
        compiler_params=params(),
    )(lists, counts, offset_table(), own, far)


def finish(half, lists, counts, planes, low, high, sums, base, links, cx, cy):
    px = cx + 2
    cap = lists.shape[0] // CLASSES
    return pl.pallas_call(
        functools.partial(last_pass, cap=cap),
        in_specs=[SMEM] * 3 + [VMEM] * 11,
        out_specs=[VMEM, VMEM, VMEM],
        out_shape=[
            jax.ShapeDtypeStruct((cx, cy, 3, 1, 128), F32),
            jax.ShapeDtypeStruct((cx, cy, 1, 128), F32),
            jax.ShapeDtypeStruct((1, 128), F32),
        ],
        scratch_shapes=[pltpu.VMEM((cx * cy, 8, 128), F32)]
        + features_of(6 * px)
        + [pltpu.VMEM((3, px, cy + 2, 8, 128), F32)],
        cost_estimate=cost(cap // 4),
        compiler_params=params(),
    )(half, lists, counts, offset_table(), *planes, low, high, *sums, base, links)


def shards(positions_now, velocities, positions_next, halo_counts, neighbour_lists, descendants):
    cx, cy, cz, _, slots = positions_now.shape
    half = lax.axis_index("gz_1")
    xs = lax.axis_size("gz_0")
    zs = lax.axis_size("gx")
    ny = lax.axis_size(GY)
    nxt = jnp.transpose(positions_next, (0, 1, 3, 2, 4))
    vel = jnp.transpose(velocities, (0, 1, 3, 2, 4))
    cnt = jnp.transpose(halo_counts, (1, 2, 0))
    own = pl.pallas_call(
        assemble,
        in_specs=[SMEM, VMEM, VMEM],
        out_specs=VMEM,
        out_shape=jax.ShapeDtypeStruct((cx * cy, 8, slots), F32),
    )(cnt, positions_now, nxt)
    other = lax.ppermute(own, "gz_1", [(0, 1), (1, 0)])
    lists, counts, acc0, base, links = first_forces(half[None], neighbour_lists, cnt, own, vel, descendants)

    def both(start):
        ends = own[start : start + cy], other[start : start + cy]
        return jnp.where(half == 0, jnp.stack(ends), jnp.stack(ends[::-1]))

    below = lax.ppermute(both(cx * cy - cy), ZRING, zring_pairs(zs, 1))
    above = lax.ppermute(both(0), ZRING, zring_pairs(zs, -1))

    def widened(block, plane):
        ends = [jnp.where(plane == 0, v[0], v[1]) for v in (below, above)]
        return jnp.concatenate([ends[0], block, ends[1]], axis=0)

    own = widened(own, half)
    other = widened(other, 1 - half)
    far = lax.ppermute(other, GZ, xhop_pairs(xs))
    acc1, top, bottom = other_forces(lists, counts, own, other, cx * cy, cx + 2)
    rows = far.reshape(cx + 2, cy * 8, slots)
    low = lax.ppermute(jnp.concatenate([top, rows[None, :, 8 * cy - 8 :]]), GY, ring(ny, 1))
    high = lax.ppermute(jnp.concatenate([bottom, rows[None, :, :8]]), GY, ring(ny, -1))
    acc2 = far_forces(lists, counts, own, far, cx * cy)
    drift, squared, part = finish(
        half[None], lists, counts, (own, other, far), low, high, (acc0, acc1, acc2), base, links, cx, cy
    )

    def gathered(row, axes):
        count = lax.axis_size(axes)
        return lax.all_to_all(jnp.broadcast_to(row, (count, slots)), axes, 0, 0, tiled=True)

    sums = jnp.sum(gathered(part, XYC), axis=0, keepdims=True)
    tension, drift = pl.pallas_call(
        scaled,
        in_specs=[VMEM, VMEM, VMEM],
        out_specs=[VMEM, pl.BlockSpec(memory_space=pl.ANY)],
        out_shape=[
            jax.ShapeDtypeStruct((cx, cy, cz, slots), F32),
            jax.ShapeDtypeStruct(drift.shape, F32),
        ],
        scratch_shapes=[pltpu.SemaphoreType.DMA],
        compiler_params=small_params(),
    )(gathered(sums, ZRING), squared, drift)
    return jnp.transpose(drift, (0, 1, 3, 2, 4)), tension


def solution(mesh):
    finer = Mesh(mesh.devices.reshape(mesh.shape["gx"], 4, 2, 4, 2), AXES)
    return jax.shard_map(
        shards,
        mesh=finer,
        in_specs=(
            P("gx", GY, GZ, None, None),
            P("gx", GY, GZ, None, None),
            P("gx", GY, GZ, None, None),
            P("gx", GY, GZ),
            P("gx", GY, GZ, None),
            P("gx", GY, GZ, None, None),
        ),
        out_specs=(P("gx", GY, GZ, None, None), P("gx", GY, GZ, None)),
        check_vma=False,
    )
```

```python
import functools

import jax
import jax.numpy as jnp
import numpy as np
from jax import lax
from jax.experimental import pallas as pl
from jax.experimental.pallas import tpu as pltpu
from jax.sharding import Mesh
from jax.sharding import PartitionSpec as P

AXES = ("gx", "gy_0", "gy_1", "gz_0", "gz_1")
GY = ("gy_0", "gy_1")
GZ = ("gz_0", "gz_1")
ZRING = ("gx", "gz_1")
XYC = ("gz_0", "gy_0", "gy_1")

EPS_SQ = 0.01
STEP_DT = 0.3
HALF_KICK = 0.045


def ring(count, step):
    return [(i, (i + step) % count) for i in range(count)]


def xhop_pairs(count):
    pairs = []
    for x in range(count):
        pairs.append((2 * x, 2 * ((x + 1) % count)))
        pairs.append((2 * x + 1, 2 * ((x - 1) % count) + 1))
    return pairs


def zring_pairs(low, step):
    total = 2 * low

    def flat(z):
        return (z % low) * 2 + z // low

    return [(flat(z), flat((z + step) % total)) for z in range(total)]


def split3(v):
    high = v.astype(jnp.bfloat16).astype(jnp.float32)
    rest = v - high
    mid = rest.astype(jnp.bfloat16).astype(jnp.float32)
    return high, mid, rest - mid


def carried(cx, cy):
    assert 7 * cy <= cx * cy - cy
    return cx // 2 * cy - cy


def unpacked(sent, cx, cy):
    first = carried(cx, cy)
    rows = sent[: 7 * cy, 7].reshape(cy, 7, sent.shape[2])
    cells = jnp.pad(rows, ((0, 0), (0, 1), (0, 0)))
    return jnp.concatenate([sent[:first], cells, sent[first:]])


def assemble(cnt_ref, now_ref, next_ref, own_ref, sent_ref):
    lane = lax.broadcasted_iota(jnp.int32, (1, 128), 1)
    cx, cy = now_ref.shape[:2]
    for x in range(cx):
        for y in range(cy):
            cell = x * cy + y
            own_ref[cell, :3] = now_ref[x, y, 0, :3]
            own_ref[cell, 3:4] = jnp.where(lane < cnt_ref[y, 0, x], now_ref[x, y, 0, 3:4], 0.0)
            own_ref[cell, 4:7] = next_ref[x, y, :, 0]
            own_ref[cell, 7:] = jnp.zeros((1, 128), jnp.float32)
    first = carried(cx, cy)
    for t in range(cx * cy - cy):
        sent_ref[t] = own_ref[t if t < first else t + cy]
    for k in range(cy):
        for r in range(7):
            sent_ref[7 * k + r, 7:] = own_ref[first + k, r : r + 1]


CLASSES = 4
BATCHES = (40, 75, 70, 88)
F32, BF16, I32 = jnp.float32, jnp.bfloat16, jnp.int32


def item_table(cx, cy):
    px = cx + 2
    table = np.zeros((2, 3, 3, 27), np.int32)
    for half in range(2):
        for xe in range(3):
            for ye in range(3):
                for code in range(27):
                    dx, dy, dz = code // 9, code // 3 % 3, code % 3
                    plane = 0 if dz == 1 else (1 if (dz == 2) == (half == 0) else 2)
                    x_in = not (xe == 0 and dx == 0 or xe == 2 and dx == 2)
                    if ye == 0 and dy == 0 or ye == 2 and dy == 2:
                        kind, step = 3, (3 * px if dy == 2 else 0) + plane * px + dx
                    elif plane == 2:
                        kind, step = 2, dx * cy + dy - 1
                    elif plane == 1:
                        kind, step = 1, dx * cy + dy - 1
                    elif x_in:
                        kind, step = 0, (dx - 1) * cy + dy - 1
                    else:
                        kind = 1
                        step = px * cy + dy - 1 if dx == 0 else (px + 1 - (cx - 1)) * cy + dy - 1
                    table[half, xe, ye, code] = 4 * (1024 * step + 32 * code) + kind
    return table.reshape(-1)


def offset_table():
    codes = np.arange(27)
    rows = np.stack([codes // 9, codes // 3 % 3, codes % 3], 1).astype(np.float32) - 0.5
    return np.broadcast_to(np.pad(rows, ((0, 0), (0, 5)))[:, :, None], (27, 8, 128)).copy()


def sublanes():
    return lax.broadcasted_iota(I32, (8, 128), 0)


def source_features(src, index, st_ref, mc_ref):
    sub = sublanes()
    q = jnp.where(sub < 3, src - 0.5, 0.0)
    norm = jnp.sum(q * q, axis=0, keepdims=True)
    s8 = jnp.where(sub < 3, -2.0 * q, jnp.where(sub == 3, norm, jnp.where(sub == 4, 1.0, 0.0)))
    m8 = jnp.where(sub == 3, 1.0, q) * src[3:4]
    sh, sm, sl = split3(s8)
    mh, mm, ml = split3(m8)
    st_ref[index] = jnp.transpose(jnp.concatenate([sh, sm, sl, sh, sm, sh], axis=0)).astype(BF16)
    mc_ref[index] = jnp.concatenate([mh, mm, ml, jnp.zeros_like(ml)], axis=0).astype(BF16)


def run_items(kind, cap, list_ref, count_ref, st_ref, mc_ref, own_of, off_ref, acc_ref):
    sub = sublanes()
    size = BATCHES[kind]
    count = count_ref[kind]

    def batch(b, carry):
        sums = []
        for t in range(size):
            place = b * size + t
            valid = place < count
            item = jnp.where(valid, list_ref[kind * cap + place], 0)
            src, code, cell = item >> 10, (item >> 5) & 31, item & 31
            p = jnp.where(sub < 3, own_of(cell) - off_ref[code], 0.0)
            norm = jnp.sum(p * p, axis=0, keepdims=True) + EPS_SQ
            p8 = jnp.where(sub == 3, 1.0, jnp.where(sub == 4, norm, p))
            ph, pm, pr = split3(p8)
            pcat = jnp.concatenate([ph, ph, ph, pm, pm, pr], axis=0).astype(BF16)
            dist = jnp.dot(st_ref[src], pcat, preferred_element_type=F32)
            inv = lax.rsqrt(dist)
            weight = inv * inv * inv
            wh = weight.astype(BF16)
            wl = (weight - wh.astype(F32)).astype(BF16)
            mc = mc_ref[src]
            a = jnp.dot(
                jnp.concatenate([mc, mc], axis=1), jnp.concatenate([wh, wl], axis=0), preferred_element_type=F32
            )
            a8 = (a[16:24] + a[8:16]) + a[:8]
            sums.append((cell, (a8 - p * a8[3:4]) * valid.astype(F32)))
        for cell, add in sums:
            acc_ref[cell] = acc_ref[cell] + add
        return carry

    lax.fori_loop(0, (count + size - 1) // size, batch, 0)


def own_pass(
    half_ref, table_ref, nbr_ref, cnt_ref, off_ref, own_ref, vel_ref, desc_ref,
    list_ref, count_ref, acc_ref, base_ref, link_ref, st_ref, mc_ref, *, cap
):
    cx, cy = nbr_ref.shape[:2]
    width = nbr_ref.shape[3]
    half = half_ref[0]
    lane = lax.broadcasted_iota(I32, (1, 128), 1)
    for kind in range(CLASSES):
        count_ref[kind] = 0
    acc_ref[...] = jnp.zeros(acc_ref.shape, F32)

    def one_row(x, carry):
        xe = jnp.where(x == 0, 0, jnp.where(x == cx - 1, 2, 1))
        for y in range(cy):
            cell = x * cy + y
            ye = (0 if y == 0 else 1) if y < cy - 1 else 2
            row = ((half * 3 + xe) * 3 + ye) * 27
            for k in range(width):
                entry = table_ref[row + nbr_ref[x, y, 0, k]]
                kind = entry & 3
                item = (entry >> 2) + jnp.where(kind == 3, cell + 1024 * x, 1025 * cell)
                place = count_ref[kind]
                list_ref[kind * cap + place] = item
                count_ref[kind] = place + 1
            own = own_ref[cell]
            source_features(own, cell, st_ref, mc_ref)
            dcode = desc_ref[x, y, 0, 0:1, :]
            ox = (dcode >= 9).astype(I32) + (dcode >= 18).astype(I32)
            rest = dcode - 9 * ox
            oy = (rest >= 3).astype(I32) + (rest >= 6).astype(I32)
            oz = rest - 3 * oy
            offset = jnp.concatenate([ox, oy, oz], axis=0).astype(F32) - 1.0
            base_ref[cell, :3] = offset - (own[:3] + STEP_DT * vel_ref[x, y, :, 0])
            base_ref[cell, 3:4] = (lane < cnt_ref[y, 0, x]).astype(F32)
            link_ref[cell, :2] = desc_ref[x, y, 0]
        return carry

    lax.fori_loop(0, cx, one_row, 0)
    run_items(0, cap, list_ref, count_ref, st_ref, mc_ref, lambda c: own_ref[c], off_ref, acc_ref)


def all_features(ref, count, st_ref, mc_ref):
    part = count // 2

    def some(i, carry):
        for step in range(part):
            source_features(ref[i * part + step], i * part + step, st_ref, mc_ref)
        return carry

    lax.fori_loop(0, 2, some, 0)


def other_pass(
    list_ref, count_ref, off_ref, own_ref, other_ref, acc_ref, top_ref, bottom_ref, st_ref, mc_ref, *, cap
):
    px = top_ref.shape[1]
    cells = own_ref.shape[0]
    cy = cells // px
    acc_ref[...] = jnp.zeros(acc_ref.shape, F32)
    for plane, ref in enumerate((own_ref, other_ref)):
        for x in range(px):
            top_ref[plane, x] = ref[x * cy + cy - 1]
            bottom_ref[plane, x] = ref[x * cy]
    all_features(other_ref, cells, st_ref, mc_ref)
    for y in range(cy):
        source_features(own_ref[y], cells + y, st_ref, mc_ref)
        source_features(own_ref[cells - cy + y], cells + cy + y, st_ref, mc_ref)
    run_items(1, cap, list_ref, count_ref, st_ref, mc_ref, lambda c: own_ref[c + cy], off_ref, acc_ref)


def far_pass(list_ref, count_ref, off_ref, own_ref, far_ref, acc_ref, st_ref, mc_ref, *, cap):
    edge = (own_ref.shape[0] - acc_ref.shape[0]) // 2
    acc_ref[...] = jnp.zeros(acc_ref.shape, F32)
    all_features(far_ref, far_ref.shape[0], st_ref, mc_ref)
    run_items(2, cap, list_ref, count_ref, st_ref, mc_ref, lambda c: own_ref[c + edge], off_ref, acc_ref)


def last_pass(
    half_ref, list_ref, count_ref, off_ref, own_ref, other_ref, far_ref, low_ref, high_ref,
    acc0_ref, acc1_ref, acc2_ref, base_ref, link_ref,
    drift_ref, sq_ref, part_ref,
    acc_ref, st_ref, mc_ref, cube_ref, *, cap
):
    cx, cy = drift_ref.shape[:2]
    px = cx + 2
    half = half_ref[0]
    lane = lax.broadcasted_iota(I32, (1, 128), 1)
    acc_ref[...] = acc0_ref[...] + acc1_ref[...] + acc2_ref[...]
    rows = px // 2

    def strips(part, carry):
        for step in range(rows):
            x = part * rows + step
            for plane in range(3):
                source_features(low_ref[plane, x], plane * px + x, st_ref, mc_ref)
                source_features(high_ref[plane, x], (3 + plane) * px + x, st_ref, mc_ref)
        return carry

    lax.fori_loop(0, 2, strips, 0)
    run_items(3, cap, list_ref, count_ref, st_ref, mc_ref, lambda c: own_ref[c + cy], off_ref, acc_ref)

    def fill(z, ref, plane):
        for x in range(px):
            cube_ref[z, x, 0] = low_ref[plane, x]
            cube_ref[z, x, 1 : cy + 1] = ref[x * cy : (x + 1) * cy]
            cube_ref[z, x, cy + 1] = high_ref[plane, x]

    fill(1, own_ref, 0)

    @pl.when(half == 0)
    def _():
        fill(0, far_ref, 2)
        fill(2, other_ref, 1)

    @pl.when(half != 0)
    def _():
        fill(0, other_ref, 1)
        fill(2, far_ref, 2)

    def one_cell(x, y):
        cell = x * cy + y
        dcode = link_ref[cell, 0:1]
        dslot = jnp.broadcast_to(link_ref[cell, 1:2], (8, 128))
        found = jnp.zeros((8, 128), F32)
        for code in range(27):
            dx, dy, dz = code // 9, code // 3 % 3, code % 3
            got = jnp.take_along_axis(cube_ref[dz, x + dx, y + dy], dslot, axis=1)
            found = jnp.where(dcode == code, got, found)
        error = base_ref[cell, :3] + found[4:7] - HALF_KICK * acc_ref[cell, :3]
        alive = base_ref[cell, 3:4]
        drift_ref[x, y, :, 0] = jnp.where(alive > 0.0, error, 0.0)
        squared = jnp.where(alive > 0.0, jnp.sum(error * error, axis=0, keepdims=True), 0.0)
        sq_ref[x, y] = squared
        return squared, alive

    def one_row(x, carry):
        total, live = carry
        for y in range(cy):
            squared, alive = one_cell(x, y)
            total = total + squared
            live = live + alive
        return total, live

    zero = jnp.zeros((1, 128), F32)
    total, live = lax.fori_loop(0, cx, one_row, (zero, zero), unroll=4)

    def folded(v):
        return v + pltpu.roll(jnp.broadcast_to(v, (8, 128)), 64, 1)[:1]

    part_ref[...] = jnp.where(lane < 64, folded(total), folded(live))


def scaled(rows_ref, sq_ref, drift_ref, tension_ref, out_ref, sem):
    copy = pltpu.make_async_copy(drift_ref, out_ref, sem)
    copy.start()
    lane = lax.broadcasted_iota(I32, (1, 128), 1)
    sums = jnp.sum(rows_ref[...], axis=0, keepdims=True)
    total = jnp.sum(jnp.where(lane < 64, sums, 0.0), axis=1, keepdims=True)
    live = jnp.sum(jnp.where(lane < 64, 0.0, sums), axis=1, keepdims=True)
    bound = jnp.broadcast_to(total / live + 1e-06, (1, 128))
    for x in range(sq_ref.shape[0]):
        for y in range(sq_ref.shape[1]):
            tension_ref[x, y] = sq_ref[x, y] / bound
    copy.wait()


SMEM = pl.BlockSpec(memory_space=pltpu.SMEM)
VMEM = pl.BlockSpec(memory_space=pltpu.VMEM)


def cost(items):
    pairs = items * 128 * 128
    return pl.CostEstimate(flops=400 * pairs, transcendentals=pairs, bytes_accessed=1 << 20)


def params():
    return pltpu.CompilerParams(vmem_limit_bytes=40 << 20)


def small_params():
    return pltpu.CompilerParams(vmem_limit_bytes=4 << 20)


def features_of(sources):
    return [pltpu.VMEM((sources, 128, 48), BF16), pltpu.VMEM((sources, 32, 128), BF16)]


def first_forces(half, neighbour_lists, cnt, own, vel, descendants):
    cx, cy = neighbour_lists.shape[:2]
    cells = cx * cy
    items = cells * neighbour_lists.shape[3]
    cap = items + max(BATCHES)
    rows = jax.ShapeDtypeStruct((cells, 8, 128), F32)
    return pl.pallas_call(
        functools.partial(own_pass, cap=cap),
        in_specs=[SMEM] * 4 + [VMEM] * 4,
        out_specs=[SMEM, SMEM, VMEM, VMEM, VMEM],
        out_shape=[
            jax.ShapeDtypeStruct((CLASSES * cap,), I32),
            jax.ShapeDtypeStruct((CLASSES,), I32),
            rows,
            rows,
            jax.ShapeDtypeStruct((cells, 8, 128), I32),
        ],
        scratch_shapes=features_of(cells),
        cost_estimate=cost(items // 4),
        compiler_params=params(),
    )(half, item_table(cx, cy), neighbour_lists, cnt, offset_table(), own, vel, descendants)


def other_forces(lists, counts, own, other, cells, px):
    cap = lists.shape[0] // CLASSES
    strip = jax.ShapeDtypeStruct((2, px, 8, 128), F32)
    return pl.pallas_call(
        functools.partial(other_pass, cap=cap),
        in_specs=[SMEM, SMEM, VMEM, VMEM, VMEM],
        out_specs=[VMEM] * 3,
        out_shape=[jax.ShapeDtypeStruct((cells, 8, 128), F32), strip, strip],
        scratch_shapes=features_of(2 * own.shape[0] - cells),
        cost_estimate=cost(cap // 4),
        compiler_params=params(),
    )(lists, counts, offset_table(), own, other)


def far_forces(lists, counts, own, far, cells):
    cap = lists.shape[0] // CLASSES
    return pl.pallas_call(
        functools.partial(far_pass, cap=cap),
        in_specs=[SMEM, SMEM, VMEM, VMEM, VMEM],
        out_specs=VMEM,
        out_shape=jax.ShapeDtypeStruct((cells, 8, 128), F32),
        scratch_shapes=features_of(far.shape[0]),
        cost_estimate=cost(cap // 4),
        compiler_params=params(),
    )(lists, counts, offset_table(), own, far)


def finish(half, lists, counts, planes, low, high, sums, base, links, cx, cy):
    px = cx + 2
    cap = lists.shape[0] // CLASSES
    return pl.pallas_call(
        functools.partial(last_pass, cap=cap),
        in_specs=[SMEM] * 3 + [VMEM] * 11,
        out_specs=[VMEM, VMEM, VMEM],
        out_shape=[
            jax.ShapeDtypeStruct((cx, cy, 3, 1, 128), F32),
            jax.ShapeDtypeStruct((cx, cy, 1, 128), F32),
            jax.ShapeDtypeStruct((1, 128), F32),
        ],
        scratch_shapes=[pltpu.VMEM((cx * cy, 8, 128), F32)]
        + features_of(6 * px)
        + [pltpu.VMEM((3, px, cy + 2, 8, 128), F32)],
        cost_estimate=cost(cap // 4),
        compiler_params=params(),
    )(half, lists, counts, offset_table(), *planes, low, high, *sums, base, links)


def shards(positions_now, velocities, positions_next, halo_counts, neighbour_lists, descendants):
    cx, cy, cz, _, slots = positions_now.shape
    half = lax.axis_index("gz_1")
    xs = lax.axis_size("gz_0")
    zs = lax.axis_size("gx")
    ny = lax.axis_size(GY)
    nxt = jnp.transpose(positions_next, (0, 1, 3, 2, 4))
    vel = jnp.transpose(velocities, (0, 1, 3, 2, 4))
    cnt = jnp.transpose(halo_counts, (1, 2, 0))
    own, sent = pl.pallas_call(
        assemble,
        in_specs=[SMEM, VMEM, VMEM],
        out_specs=[VMEM, VMEM],
        out_shape=[
            jax.ShapeDtypeStruct((cx * cy, 8, slots), F32),
            jax.ShapeDtypeStruct((cx * cy - cy, 8, slots), F32),
        ],
    )(cnt, positions_now, nxt)
    sent = lax.ppermute(sent, "gz_1", [(0, 1), (1, 0)])
    other = unpacked(sent, cx, cy)
    lists, counts, acc0, base, links = first_forces(half[None], neighbour_lists, cnt, own, vel, descendants)

    def both(start):
        place = start if start == 0 else start - cy
        ends = own[start : start + cy], sent[place : place + cy]
        return jnp.where(half == 0, jnp.stack(ends), jnp.stack(ends[::-1]))

    below = lax.ppermute(both(cx * cy - cy), ZRING, zring_pairs(zs, 1))
    above = lax.ppermute(both(0), ZRING, zring_pairs(zs, -1))

    def widened(block, plane):
        ends = [jnp.where(plane == 0, v[0], v[1]) for v in (below, above)]
        return jnp.concatenate([ends[0], block, ends[1]], axis=0)

    own = widened(own, half)
    other = widened(other, 1 - half)
    far = lax.ppermute(other, GZ, xhop_pairs(xs))
    acc1, top, bottom = other_forces(lists, counts, own, other, cx * cy, cx + 2)
    rows = far.reshape(cx + 2, cy * 8, slots)
    low = lax.ppermute(jnp.concatenate([top, rows[None, :, 8 * cy - 8 :]]), GY, ring(ny, 1))
    high = lax.ppermute(jnp.concatenate([bottom, rows[None, :, :8]]), GY, ring(ny, -1))
    acc2 = far_forces(lists, counts, own, far, cx * cy)
    drift, squared, part = finish(
        half[None], lists, counts, (own, other, far), low, high, (acc0, acc1, acc2), base, links, cx, cy
    )

    def gathered(row, axes):
        count = lax.axis_size(axes)
        return lax.all_to_all(jnp.broadcast_to(row, (count, slots)), axes, 0, 0, tiled=True)

    sums = jnp.sum(gathered(part, XYC), axis=0, keepdims=True)
    tension, drift = pl.pallas_call(
        scaled,
        in_specs=[VMEM, VMEM, VMEM],
        out_specs=[VMEM, pl.BlockSpec(memory_space=pl.ANY)],
        out_shape=[
            jax.ShapeDtypeStruct((cx, cy, cz, slots), F32),
            jax.ShapeDtypeStruct(drift.shape, F32),
        ],
        scratch_shapes=[pltpu.SemaphoreType.DMA],
        compiler_params=small_params(),
    )(gathered(sums, ZRING), squared, drift)
    return jnp.transpose(drift, (0, 1, 3, 2, 4)), tension


def solution(mesh):
    finer = Mesh(mesh.devices.reshape(mesh.shape["gx"], 4, 2, 4, 2), AXES)
    return jax.shard_map(
        shards,
        mesh=finer,
        in_specs=(
            P("gx", GY, GZ, None, None),
            P("gx", GY, GZ, None, None),
            P("gx", GY, GZ, None, None),
            P("gx", GY, GZ),
            P("gx", GY, GZ, None),
            P("gx", GY, GZ, None, None),
        ),
        out_specs=(P("gx", GY, GZ, None, None), P("gx", GY, GZ, None)),
        check_vma=False,
    )
```

```python
import functools

import jax
import jax.numpy as jnp
import numpy as np
from jax import lax
from jax.experimental import pallas as pl
from jax.experimental.pallas import tpu as pltpu
from jax.sharding import Mesh
from jax.sharding import PartitionSpec as P

AXES = ("gx", "gy_0", "gy_1", "gz_0", "gz_1")
GY = ("gy_0", "gy_1")
GZ = ("gz_0", "gz_1")
ZRING = ("gx", "gz_1")
XYC = ("gz_0", "gy_0", "gy_1")

EPS_SQ = 0.01
STEP_DT = 0.3
HALF_KICK = 0.045


def ring(count, step):
    return [(i, (i + step) % count) for i in range(count)]


def xhop_pairs(count):
    pairs = []
    for x in range(count):
        pairs.append((2 * x, 2 * ((x + 1) % count)))
        pairs.append((2 * x + 1, 2 * ((x - 1) % count) + 1))
    return pairs


def zring_pairs(low, step):
    total = 2 * low

    def flat(z):
        return (z % low) * 2 + z // low

    return [(flat(z), flat((z + step) % total)) for z in range(total)]


def split3(v):
    high = v.astype(jnp.bfloat16).astype(jnp.float32)
    rest = v - high
    mid = rest.astype(jnp.bfloat16).astype(jnp.float32)
    return high, mid, rest - mid


def carried(cx, cy):
    assert 7 * cy <= cx * cy - cy
    return cx // 2 * cy - cy


def unpacked(sent, cx, cy):
    first = carried(cx, cy)
    rows = sent[: 7 * cy, 7].reshape(cy, 7, sent.shape[2])
    cells = jnp.pad(rows, ((0, 0), (0, 1), (0, 0)))
    return jnp.concatenate([sent[:first], cells, sent[first:]])


def assemble(cnt_ref, now_ref, next_ref, own_ref, sent_ref):
    lane = lax.broadcasted_iota(jnp.int32, (1, 128), 1)
    cx, cy = now_ref.shape[:2]
    for x in range(cx):
        for y in range(cy):
            cell = x * cy + y
            own_ref[cell, :3] = now_ref[x, y, 0, :3]
            own_ref[cell, 3:4] = jnp.where(lane < cnt_ref[y, 0, x], now_ref[x, y, 0, 3:4], 0.0)
            own_ref[cell, 4:7] = next_ref[x, y, :, 0]
            own_ref[cell, 7:] = jnp.zeros((1, 128), jnp.float32)
    first = carried(cx, cy)
    for t in range(cx * cy - cy):
        sent_ref[t] = own_ref[t if t < first else t + cy]
    for k in range(cy):
        for r in range(7):
            sent_ref[7 * k + r, 7:] = own_ref[first + k, r : r + 1]


CLASSES = 4
BATCHES = (40, 75, 70, 88)
F32, BF16, I32 = jnp.float32, jnp.bfloat16, jnp.int32


def item_table(cx, cy):
    px = cx + 2
    table = np.zeros((2, 3, 3, 27), np.int32)
    for half in range(2):
        for xe in range(3):
            for ye in range(3):
                for code in range(27):
                    dx, dy, dz = code // 9, code // 3 % 3, code % 3
                    plane = 0 if dz == 1 else (1 if (dz == 2) == (half == 0) else 2)
                    x_in = not (xe == 0 and dx == 0 or xe == 2 and dx == 2)
                    if ye == 0 and dy == 0 or ye == 2 and dy == 2:
                        kind, step = 3, (3 * px if dy == 2 else 0) + plane * px + dx
                    elif plane == 2:
                        kind, step = 2, dx * cy + dy - 1
                    elif plane == 1:
                        kind, step = 1, dx * cy + dy - 1
                    elif x_in:
                        kind, step = 0, (dx - 1) * cy + dy - 1
                    else:
                        kind = 1
                        step = px * cy + dy - 1 if dx == 0 else (px + 1 - (cx - 1)) * cy + dy - 1
                    table[half, xe, ye, code] = 4 * (1024 * step + 32 * code) + kind
    return table.reshape(-1)


def offset_table():
    codes = np.arange(27)
    rows = np.stack([codes // 9, codes // 3 % 3, codes % 3], 1).astype(np.float32) - 0.5
    return np.broadcast_to(np.pad(rows, ((0, 0), (0, 5)))[:, :, None], (27, 8, 128)).copy()


def sublanes():
    return lax.broadcasted_iota(I32, (8, 128), 0)


def source_features(src, index, st_ref, mc_ref):
    sub = sublanes()
    q = jnp.where(sub < 3, src - 0.5, 0.0)
    norm = jnp.sum(q * q, axis=0, keepdims=True)
    s8 = jnp.where(sub < 3, -2.0 * q, jnp.where(sub == 3, norm, jnp.where(sub == 4, 1.0, 0.0)))
    m8 = jnp.where(sub == 3, 1.0, q) * src[3:4]
    sh, sm, sl = split3(s8)
    mh, mm, ml = split3(m8)
    st_ref[index] = jnp.transpose(jnp.concatenate([sh, sm, sl, sh, sm, sh], axis=0)).astype(BF16)
    mc_ref[index] = jnp.concatenate([mh, mm, ml, jnp.zeros_like(ml)], axis=0).astype(BF16)


def run_items(kind, cap, list_ref, count_ref, st_ref, mc_ref, own_of, off_ref, acc_ref):
    sub = sublanes()
    size = BATCHES[kind]
    count = count_ref[kind]

    def batch(b, carry):
        sums = []
        for t in range(size):
            place = b * size + t
            valid = place < count
            item = jnp.where(valid, list_ref[kind * cap + place], 0)
            src, code, cell = item >> 10, (item >> 5) & 31, item & 31
            p = jnp.where(sub < 3, own_of(cell) - off_ref[code], 0.0)
            norm = jnp.sum(p * p, axis=0, keepdims=True) + EPS_SQ
            p8 = jnp.where(sub == 3, 1.0, jnp.where(sub == 4, norm, p))
            ph, pm, pr = split3(p8)
            pcat = jnp.concatenate([ph, ph, ph, pm, pm, pr], axis=0).astype(BF16)
            dist = jnp.dot(st_ref[src], pcat, preferred_element_type=F32)
            inv = lax.rsqrt(dist)
            weight = inv * inv * inv
            wh = weight.astype(BF16)
            wl = (weight - wh.astype(F32)).astype(BF16)
            mc = mc_ref[src]
            a = jnp.dot(
                jnp.concatenate([mc, mc], axis=1), jnp.concatenate([wh, wl], axis=0), preferred_element_type=F32
            )
            a8 = (a[16:24] + a[8:16]) + a[:8]
            sums.append((cell, (a8 - p * a8[3:4]) * valid.astype(F32)))
        for cell, add in sums:
            acc_ref[cell] = acc_ref[cell] + add
        return carry

    lax.fori_loop(0, (count + size - 1) // size, batch, 0)


def own_pass(
    half_ref, table_ref, nbr_ref, cnt_ref, off_ref, own_ref, vel_ref, desc_ref,
    list_ref, count_ref, acc_ref, base_ref, link_ref, kept_ref, table_out_ref, st_ref, mc_ref, *, cap
):
    cx, cy = nbr_ref.shape[:2]
    kept_ref[...] = own_ref[...]
    table_out_ref[...] = off_ref[...]
    width = nbr_ref.shape[3]
    half = half_ref[0]
    lane = lax.broadcasted_iota(I32, (1, 128), 1)
    for kind in range(CLASSES):
        count_ref[kind] = 0
    acc_ref[...] = jnp.zeros(acc_ref.shape, F32)

    def one_row(x, carry):
        xe = jnp.where(x == 0, 0, jnp.where(x == cx - 1, 2, 1))
        for y in range(cy):
            cell = x * cy + y
            ye = (0 if y == 0 else 1) if y < cy - 1 else 2
            row = ((half * 3 + xe) * 3 + ye) * 27
            for k in range(width):
                entry = table_ref[row + nbr_ref[x, y, 0, k]]
                kind = entry & 3
                item = (entry >> 2) + jnp.where(kind == 3, cell + 1024 * x, 1025 * cell)
                place = count_ref[kind]
                list_ref[kind * cap + place] = item
                count_ref[kind] = place + 1
            own = own_ref[cell]
            source_features(own, cell, st_ref, mc_ref)
            dcode = desc_ref[x, y, 0, 0:1, :]
            ox = (dcode >= 9).astype(I32) + (dcode >= 18).astype(I32)
            rest = dcode - 9 * ox
            oy = (rest >= 3).astype(I32) + (rest >= 6).astype(I32)
            oz = rest - 3 * oy
            offset = jnp.concatenate([ox, oy, oz], axis=0).astype(F32) - 1.0
            base_ref[cell, :3] = offset - (own[:3] + STEP_DT * vel_ref[x, y, :, 0])
            base_ref[cell, 3:4] = (lane < cnt_ref[y, 0, x]).astype(F32)
            link_ref[cell, :2] = desc_ref[x, y, 0]
        return carry

    lax.fori_loop(0, cx, one_row, 0)
    run_items(0, cap, list_ref, count_ref, st_ref, mc_ref, lambda c: own_ref[c], off_ref, acc_ref)


def all_features(ref, count, st_ref, mc_ref):
    part = count // 2

    def some(i, carry):
        for step in range(part):
            source_features(ref[i * part + step], i * part + step, st_ref, mc_ref)
        return carry

    lax.fori_loop(0, 2, some, 0)


def other_pass(
    list_ref, count_ref, off_ref, own_ref, other_ref, acc_ref, top_ref, bottom_ref, st_ref, mc_ref, *, cap
):
    px = top_ref.shape[1]
    cells = own_ref.shape[0]
    cy = cells // px
    acc_ref[...] = jnp.zeros(acc_ref.shape, F32)
    for plane, ref in enumerate((own_ref, other_ref)):
        for x in range(px):
            top_ref[plane, x] = ref[x * cy + cy - 1]
            bottom_ref[plane, x] = ref[x * cy]
    all_features(other_ref, cells, st_ref, mc_ref)
    for y in range(cy):
        source_features(own_ref[y], cells + y, st_ref, mc_ref)
        source_features(own_ref[cells - cy + y], cells + cy + y, st_ref, mc_ref)
    run_items(1, cap, list_ref, count_ref, st_ref, mc_ref, lambda c: own_ref[c + cy], off_ref, acc_ref)


def far_pass(list_ref, count_ref, off_ref, own_ref, far_ref, acc_ref, st_ref, mc_ref, *, cap):
    edge = (own_ref.shape[0] - acc_ref.shape[0]) // 2
    acc_ref[...] = jnp.zeros(acc_ref.shape, F32)
    all_features(far_ref, far_ref.shape[0], st_ref, mc_ref)
    run_items(2, cap, list_ref, count_ref, st_ref, mc_ref, lambda c: own_ref[c + edge], off_ref, acc_ref)


def last_pass(
    half_ref, list_ref, count_ref, off_ref, own_ref, other_ref, far_ref, low_ref, high_ref,
    acc0_ref, acc1_ref, acc2_ref, base_ref, link_ref,
    drift_ref, sq_ref, part_ref,
    acc_ref, st_ref, mc_ref, cube_ref, *, cap
):
    cx, cy = drift_ref.shape[:2]
    px = cx + 2
    half = half_ref[0]
    lane = lax.broadcasted_iota(I32, (1, 128), 1)
    acc_ref[...] = acc0_ref[...] + acc1_ref[...] + acc2_ref[...]
    rows = px // 2

    def strips(part, carry):
        for step in range(rows):
            x = part * rows + step
            for plane in range(3):
                source_features(low_ref[plane, x], plane * px + x, st_ref, mc_ref)
                source_features(high_ref[plane, x], (3 + plane) * px + x, st_ref, mc_ref)
        return carry

    lax.fori_loop(0, 2, strips, 0)
    run_items(3, cap, list_ref, count_ref, st_ref, mc_ref, lambda c: own_ref[c + cy], off_ref, acc_ref)

    def fill(z, ref, plane):
        for x in range(px):
            cube_ref[z, x, 0] = low_ref[plane, x]
            cube_ref[z, x, 1 : cy + 1] = ref[x * cy : (x + 1) * cy]
            cube_ref[z, x, cy + 1] = high_ref[plane, x]

    fill(1, own_ref, 0)

    @pl.when(half == 0)
    def _():
        fill(0, far_ref, 2)
        fill(2, other_ref, 1)

    @pl.when(half != 0)
    def _():
        fill(0, other_ref, 1)
        fill(2, far_ref, 2)

    sub = sublanes()
    for x in range(px):
        for y in range(cy + 2):
            cube_ref[0, x, y] = jnp.where(sub < 4, pltpu.roll(cube_ref[0, x, y], 4, 0), cube_ref[2, x, y])

    def one_cell(x, y):
        cell = x * cy + y
        dcode = link_ref[cell, 0:1]
        dslot = jnp.broadcast_to(link_ref[cell, 1:2], (8, 128))
        key = jnp.where(sub < 4, dcode, dcode - 2)
        level = jnp.zeros((8, 128), F32)
        sides = jnp.zeros((8, 128), F32)
        for dx in range(3):
            for dy in range(3):
                code = 9 * dx + 3 * dy
                got = jnp.take_along_axis(cube_ref[1, x + dx, y + dy], dslot, axis=1)
                level = jnp.where(dcode == code + 1, got, level)
                got = jnp.take_along_axis(cube_ref[0, x + dx, y + dy], dslot, axis=1)
                sides = jnp.where(key == code, got, sides)
        found = (level[4:7] + sides[4:7]) + sides[:3]
        error = base_ref[cell, :3] + found - HALF_KICK * acc_ref[cell, :3]
        alive = base_ref[cell, 3:4]
        drift_ref[x, y, :, 0] = jnp.where(alive > 0.0, error, 0.0)
        squared = jnp.where(alive > 0.0, jnp.sum(error * error, axis=0, keepdims=True), 0.0)
        sq_ref[x, y] = squared
        return squared, alive

    def one_row(x, carry):
        total, live = carry
        for y in range(cy):
            squared, alive = one_cell(x, y)
            total = total + squared
            live = live + alive
        return total, live

    zero = jnp.zeros((1, 128), F32)
    total, live = lax.fori_loop(0, cx, one_row, (zero, zero), unroll=4)

    def folded(v):
        return v + pltpu.roll(jnp.broadcast_to(v, (8, 128)), 64, 1)[:1]

    part_ref[...] = jnp.where(lane < 64, folded(total), folded(live))


def scaled(rows_ref, sq_ref, drift_ref, tension_ref, out_ref, sem):
    copy = pltpu.make_async_copy(drift_ref, out_ref, sem)
    copy.start()
    lane = lax.broadcasted_iota(I32, (1, 128), 1)
    sums = jnp.sum(rows_ref[...], axis=0, keepdims=True)
    total = jnp.sum(jnp.where(lane < 64, sums, 0.0), axis=1, keepdims=True)
    live = jnp.sum(jnp.where(lane < 64, 0.0, sums), axis=1, keepdims=True)
    bound = jnp.broadcast_to(total / live + 1e-06, (1, 128))
    for x in range(sq_ref.shape[0]):
        for y in range(sq_ref.shape[1]):
            tension_ref[x, y] = sq_ref[x, y] / bound
    copy.wait()


SMEM = pl.BlockSpec(memory_space=pltpu.SMEM)
VMEM = pl.BlockSpec(memory_space=pltpu.VMEM)


def cost(items):
    pairs = items * 128 * 128
    return pl.CostEstimate(flops=400 * pairs, transcendentals=pairs, bytes_accessed=1 << 20)


def params():
    return pltpu.CompilerParams(vmem_limit_bytes=40 << 20)


def small_params():
    return pltpu.CompilerParams(vmem_limit_bytes=4 << 20)


def features_of(sources):
    return [pltpu.VMEM((sources, 128, 48), BF16), pltpu.VMEM((sources, 32, 128), BF16)]


def first_forces(half, neighbour_lists, cnt, own, vel, descendants):
    cx, cy = neighbour_lists.shape[:2]
    cells = cx * cy
    items = cells * neighbour_lists.shape[3]
    cap = items + max(BATCHES)
    rows = jax.ShapeDtypeStruct((cells, 8, 128), F32)
    return pl.pallas_call(
        functools.partial(own_pass, cap=cap),
        in_specs=[SMEM] * 4 + [VMEM] * 4,
        out_specs=[SMEM, SMEM] + [VMEM] * 5,
        out_shape=[
            jax.ShapeDtypeStruct((CLASSES * cap,), I32),
            jax.ShapeDtypeStruct((CLASSES,), I32),
            rows,
            rows,
            jax.ShapeDtypeStruct((cells, 8, 128), I32),
            rows,
            jax.ShapeDtypeStruct((27, 8, 128), F32),
        ],
        scratch_shapes=features_of(cells),
        cost_estimate=cost(items // 4),
        compiler_params=params(),
    )(half, item_table(cx, cy), neighbour_lists, cnt, offset_table(), own, vel, descendants)


def other_forces(lists, counts, offsets, own, other, cells, px):
    cap = lists.shape[0] // CLASSES
    strip = jax.ShapeDtypeStruct((2, px, 8, 128), F32)
    return pl.pallas_call(
        functools.partial(other_pass, cap=cap),
        in_specs=[SMEM, SMEM, VMEM, VMEM, VMEM],
        out_specs=[VMEM] * 3,
        out_shape=[jax.ShapeDtypeStruct((cells, 8, 128), F32), strip, strip],
        scratch_shapes=features_of(2 * own.shape[0] - cells),
        cost_estimate=cost(cap // 4),
        compiler_params=params(),
    )(lists, counts, offsets, own, other)


def far_forces(lists, counts, offsets, own, far, cells):
    cap = lists.shape[0] // CLASSES
    return pl.pallas_call(
        functools.partial(far_pass, cap=cap),
        in_specs=[SMEM, SMEM, VMEM, VMEM, VMEM],
        out_specs=VMEM,
        out_shape=jax.ShapeDtypeStruct((cells, 8, 128), F32),
        scratch_shapes=features_of(far.shape[0]),
        cost_estimate=cost(cap // 4),
        compiler_params=params(),
    )(lists, counts, offsets, own, far)


def finish(half, lists, counts, offsets, planes, low, high, sums, base, links, cx, cy):
    px = cx + 2
    cap = lists.shape[0] // CLASSES
    return pl.pallas_call(
        functools.partial(last_pass, cap=cap),
        in_specs=[SMEM] * 3 + [VMEM] * 11,
        out_specs=[VMEM, VMEM, VMEM],
        out_shape=[
            jax.ShapeDtypeStruct((cx, cy, 3, 1, 128), F32),
            jax.ShapeDtypeStruct((cx, cy, 1, 128), F32),
            jax.ShapeDtypeStruct((1, 128), F32),
        ],
        scratch_shapes=[pltpu.VMEM((cx * cy, 8, 128), F32)]
        + features_of(6 * px)
        + [pltpu.VMEM((3, px, cy + 2, 8, 128), F32)],
        cost_estimate=cost(cap // 4),
        compiler_params=params(),
    )(half, lists, counts, offsets, *planes, low, high, *sums, base, links)


def shards(positions_now, velocities, positions_next, halo_counts, neighbour_lists, descendants):
    cx, cy, cz, _, slots = positions_now.shape
    half = lax.axis_index("gz_1")
    xs = lax.axis_size("gz_0")
    zs = lax.axis_size("gx")
    ny = lax.axis_size(GY)
    nxt = jnp.transpose(positions_next, (0, 1, 3, 2, 4))
    vel = jnp.transpose(velocities, (0, 1, 3, 2, 4))
    cnt = jnp.transpose(halo_counts, (1, 2, 0))
    own, sent = pl.pallas_call(
        assemble,
        in_specs=[SMEM, VMEM, VMEM],
        out_specs=[VMEM, VMEM],
        out_shape=[
            jax.ShapeDtypeStruct((cx * cy, 8, slots), F32),
            jax.ShapeDtypeStruct((cx * cy - cy, 8, slots), F32),
        ],
    )(cnt, positions_now, nxt)
    sent = lax.ppermute(sent, "gz_1", [(0, 1), (1, 0)])
    other = unpacked(sent, cx, cy)
    lists, counts, acc0, base, links, own, offsets = first_forces(
        half[None], neighbour_lists, cnt, own, vel, descendants
    )

    def both(start):
        place = start if start == 0 else start - cy
        ends = own[start : start + cy], sent[place : place + cy]
        return jnp.where(half == 0, jnp.stack(ends), jnp.stack(ends[::-1]))

    below = lax.ppermute(both(cx * cy - cy), ZRING, zring_pairs(zs, 1))
    above = lax.ppermute(both(0), ZRING, zring_pairs(zs, -1))

    def widened(block, plane):
        ends = [jnp.where(plane == 0, v[0], v[1]) for v in (below, above)]
        return jnp.concatenate([ends[0], block, ends[1]], axis=0)

    own = widened(own, half)
    other = widened(other, 1 - half)
    far = lax.ppermute(other, GZ, xhop_pairs(xs))
    acc1, top, bottom = other_forces(lists, counts, offsets, own, other, cx * cy, cx + 2)
    rows = far.reshape(cx + 2, cy * 8, slots)
    low = lax.ppermute(jnp.concatenate([top, rows[None, :, 8 * cy - 8 :]]), GY, ring(ny, 1))
    high = lax.ppermute(jnp.concatenate([bottom, rows[None, :, :8]]), GY, ring(ny, -1))
    acc2 = far_forces(lists, counts, offsets, own, far, cx * cy)
    drift, squared, part = finish(
        half[None], lists, counts, offsets, (own, other, far), low, high, (acc0, acc1, acc2), base, links, cx, cy
    )

    def gathered(row, axes):
        count = lax.axis_size(axes)
        return lax.all_to_all(jnp.broadcast_to(row, (count, slots)), axes, 0, 0, tiled=True)

    sums = jnp.sum(gathered(part, XYC), axis=0, keepdims=True)
    tension, drift = pl.pallas_call(
        scaled,
        in_specs=[VMEM, VMEM, VMEM],
        out_specs=[VMEM, pl.BlockSpec(memory_space=pl.ANY)],
        out_shape=[
            jax.ShapeDtypeStruct((cx, cy, cz, slots), F32),
            jax.ShapeDtypeStruct(drift.shape, F32),
        ],
        scratch_shapes=[pltpu.SemaphoreType.DMA],
        compiler_params=small_params(),
    )(gathered(sums, ZRING), squared, drift)
    return jnp.transpose(drift, (0, 1, 3, 2, 4)), tension


def solution(mesh):
    finer = Mesh(mesh.devices.reshape(mesh.shape["gx"], 4, 2, 4, 2), AXES)
    return jax.shard_map(
        shards,
        mesh=finer,
        in_specs=(
            P("gx", GY, GZ, None, None),
            P("gx", GY, GZ, None, None),
            P("gx", GY, GZ, None, None),
            P("gx", GY, GZ),
            P("gx", GY, GZ, None),
            P("gx", GY, GZ, None, None),
        ),
        out_specs=(P("gx", GY, GZ, None, None), P("gx", GY, GZ, None)),
        check_vma=False,
    )
```

```python
import functools

import jax
import jax.numpy as jnp
import numpy as np
from jax import lax
from jax.experimental import pallas as pl
from jax.experimental.pallas import tpu as pltpu
from jax.sharding import Mesh
from jax.sharding import PartitionSpec as P

AXES = ("gx", "gy_0", "gy_1", "gz_0", "gz_1")
GY = ("gy_0", "gy_1")
GZ = ("gz_0", "gz_1")
ZRING = ("gx", "gz_1")
XYC = ("gz_0", "gy_0", "gy_1")

EPS_SQ = 0.01
STEP_DT = 0.3
HALF_KICK = 0.045


def ring(count, step):
    return [(i, (i + step) % count) for i in range(count)]


def xhop_pairs(count):
    pairs = []
    for x in range(count):
        pairs.append((2 * x, 2 * ((x + 1) % count)))
        pairs.append((2 * x + 1, 2 * ((x - 1) % count) + 1))
    return pairs


def zring_pairs(low, step):
    total = 2 * low

    def flat(z):
        return (z % low) * 2 + z // low

    return [(flat(z), flat((z + step) % total)) for z in range(total)]


def split3(v):
    high = v.astype(jnp.bfloat16).astype(jnp.float32)
    rest = v - high
    mid = rest.astype(jnp.bfloat16).astype(jnp.float32)
    return high, mid, rest - mid


def carried(cx, cy):
    assert 7 * cy <= cx * cy - cy
    return cx // 2 * cy - cy


def unpacked(sent, cx, cy):
    first = carried(cx, cy)
    rows = sent[: 7 * cy, 7].reshape(cy, 7, sent.shape[2])
    cells = jnp.pad(rows, ((0, 0), (0, 1), (0, 0)))
    return jnp.concatenate([sent[:first], cells, sent[first:]])


def assemble(cnt_ref, now_ref, next_ref, own_ref, sent_ref):
    lane = lax.broadcasted_iota(jnp.int32, (1, 128), 1)
    cx, cy = now_ref.shape[:2]
    for x in range(cx):
        for y in range(cy):
            cell = x * cy + y
            own_ref[cell, :3] = now_ref[x, y, 0, :3]
            own_ref[cell, 3:4] = jnp.where(lane < cnt_ref[y, 0, x], now_ref[x, y, 0, 3:4], 0.0)
            own_ref[cell, 4:7] = next_ref[x, y, :, 0]
            own_ref[cell, 7:] = jnp.zeros((1, 128), jnp.float32)
    first = carried(cx, cy)
    for t in range(cx * cy - cy):
        sent_ref[t] = own_ref[t if t < first else t + cy]
    for k in range(cy):
        for r in range(7):
            sent_ref[7 * k + r, 7:] = own_ref[first + k, r : r + 1]


CLASSES = 4
BATCHES = (40, 75, 70, 88)
F32, BF16, I32 = jnp.float32, jnp.bfloat16, jnp.int32


def item_table(cx, cy):
    px = cx + 2
    table = np.zeros((2, 3, 3, 27), np.int32)
    for half in range(2):
        for xe in range(3):
            for ye in range(3):
                for code in range(27):
                    dx, dy, dz = code // 9, code // 3 % 3, code % 3
                    plane = 0 if dz == 1 else (1 if (dz == 2) == (half == 0) else 2)
                    x_in = not (xe == 0 and dx == 0 or xe == 2 and dx == 2)
                    if ye == 0 and dy == 0 or ye == 2 and dy == 2:
                        kind, step = 3, (3 * px if dy == 2 else 0) + plane * px + dx
                    elif plane == 2:
                        kind, step = 2, dx * cy + dy - 1
                    elif plane == 1:
                        kind, step = 1, dx * cy + dy - 1
                    elif x_in:
                        kind, step = 0, (dx - 1) * cy + dy - 1
                    else:
                        kind = 1
                        step = px * cy + dy - 1 if dx == 0 else (px + 1 - (cx - 1)) * cy + dy - 1
                    table[half, xe, ye, code] = 4 * (1024 * step + 32 * code) + kind
    return table.reshape(-1)


def offset_table():
    codes = np.arange(27)
    rows = np.stack([codes // 9, codes // 3 % 3, codes % 3], 1).astype(np.float32) - 0.5
    return np.broadcast_to(np.pad(rows, ((0, 0), (0, 5)))[:, :, None], (27, 8, 128)).copy()


def sublanes():
    return lax.broadcasted_iota(I32, (8, 128), 0)


def source_features(src, index, st_ref, mc_ref):
    sub = sublanes()
    q = jnp.where(sub < 3, src - 0.5, 0.0)
    norm = jnp.sum(q * q, axis=0, keepdims=True)
    s8 = jnp.where(sub < 3, -2.0 * q, jnp.where(sub == 3, norm, jnp.where(sub == 4, 1.0, 0.0)))
    m8 = jnp.where(sub == 3, 1.0, q) * src[3:4]
    sh, sm, sl = split3(s8)
    mh, mm, ml = split3(m8)
    st_ref[index] = jnp.transpose(jnp.concatenate([sh, sm, sl, sh, sm, sh], axis=0)).astype(BF16)
    mc_ref[index] = jnp.concatenate([mh, mm, ml, jnp.zeros_like(ml)], axis=0).astype(BF16)


def run_items(kind, cap, list_ref, count_ref, st_ref, mc_ref, own_of, off_ref, acc_ref):
    sub = sublanes()
    size = BATCHES[kind]
    count = count_ref[kind]

    def batch(b, carry):
        sums = []
        for t in range(size):
            place = b * size + t
            valid = place < count
            item = jnp.where(valid, list_ref[kind * cap + place], 0)
            src, code, cell = item >> 10, (item >> 5) & 31, item & 31
            p = jnp.where(sub < 3, own_of(cell) - off_ref[code], 0.0)
            norm = jnp.sum(p * p, axis=0, keepdims=True) + EPS_SQ
            p8 = jnp.where(sub == 3, 1.0, jnp.where(sub == 4, norm, p))
            ph, pm, pr = split3(p8)
            pcat = jnp.concatenate([ph, ph, ph, pm, pm, pr], axis=0).astype(BF16)
            dist = jnp.dot(st_ref[src], pcat, preferred_element_type=F32)
            inv = lax.rsqrt(dist)
            weight = inv * inv * inv
            wh = weight.astype(BF16)
            wl = (weight - wh.astype(F32)).astype(BF16)
            mc = mc_ref[src]
            a = jnp.dot(
                jnp.concatenate([mc, mc], axis=1), jnp.concatenate([wh, wl], axis=0), preferred_element_type=F32
            )
            a8 = (a[16:24] + a[8:16]) + a[:8]
            sums.append((cell, (a8 - p * a8[3:4]) * valid.astype(F32)))
        for cell, add in sums:
            acc_ref[cell] = acc_ref[cell] + add
        return carry

    lax.fori_loop(0, (count + size - 1) // size, batch, 0)


def own_pass(
    half_ref, table_ref, nbr_ref, cnt_ref, off_ref, own_ref, vel_ref, desc_ref,
    list_ref, count_ref, acc_ref, base_ref, link_ref, kept_ref, table_out_ref, st_ref, mc_ref, *, cap
):
    cx, cy = nbr_ref.shape[:2]
    kept_ref[...] = own_ref[...]
    table_out_ref[...] = off_ref[...]
    width = nbr_ref.shape[3]
    half = half_ref[0]
    lane = lax.broadcasted_iota(I32, (1, 128), 1)
    for kind in range(CLASSES):
        count_ref[kind] = 0
    acc_ref[...] = jnp.zeros(acc_ref.shape, F32)

    def one_row(x, carry):
        xe = jnp.where(x == 0, 0, jnp.where(x == cx - 1, 2, 1))
        for y in range(cy):
            cell = x * cy + y
            ye = (0 if y == 0 else 1) if y < cy - 1 else 2
            row = ((half * 3 + xe) * 3 + ye) * 27
            for k in range(width):
                entry = table_ref[row + nbr_ref[x, y, 0, k]]
                kind = entry & 3
                item = (entry >> 2) + jnp.where(kind == 3, cell + 1024 * x, 1025 * cell)
                place = count_ref[kind]
                list_ref[kind * cap + place] = item
                count_ref[kind] = place + 1
            own = own_ref[cell]
            source_features(own, cell, st_ref, mc_ref)
            dcode = desc_ref[x, y, 0, 0:1, :]
            ox = (dcode >= 9).astype(I32) + (dcode >= 18).astype(I32)
            rest = dcode - 9 * ox
            oy = (rest >= 3).astype(I32) + (rest >= 6).astype(I32)
            oz = rest - 3 * oy
            offset = jnp.concatenate([ox, oy, oz], axis=0).astype(F32) - 1.0
            base_ref[cell, :3] = offset - (own[:3] + STEP_DT * vel_ref[x, y, :, 0])
            base_ref[cell, 3:4] = (lane < cnt_ref[y, 0, x]).astype(F32)
            link_ref[cell, :2] = desc_ref[x, y, 0]
        return carry

    lax.fori_loop(0, cx, one_row, 0)
    run_items(0, cap, list_ref, count_ref, st_ref, mc_ref, lambda c: own_ref[c], off_ref, acc_ref)


def all_features(ref, count, st_ref, mc_ref):
    part = count // 2

    def some(i, carry):
        for step in range(part):
            source_features(ref[i * part + step], i * part + step, st_ref, mc_ref)
        return carry

    lax.fori_loop(0, 2, some, 0)


def other_pass(
    list_ref, count_ref, off_ref, own_ref, other_ref, acc_ref, top_ref, bottom_ref, st_ref, mc_ref, *, cap
):
    px = top_ref.shape[1]
    cells = own_ref.shape[0]
    cy = cells // px
    acc_ref[...] = jnp.zeros(acc_ref.shape, F32)
    for plane, ref in enumerate((own_ref, other_ref)):
        for x in range(px):
            top_ref[plane, x] = ref[x * cy + cy - 1]
            bottom_ref[plane, x] = ref[x * cy]
    all_features(other_ref, cells, st_ref, mc_ref)
    for y in range(cy):
        source_features(own_ref[y], cells + y, st_ref, mc_ref)
        source_features(own_ref[cells - cy + y], cells + cy + y, st_ref, mc_ref)
    run_items(1, cap, list_ref, count_ref, st_ref, mc_ref, lambda c: own_ref[c + cy], off_ref, acc_ref)


def far_pass(list_ref, count_ref, off_ref, own_ref, far_ref, acc_ref, st_ref, mc_ref, *, cap):
    edge = (own_ref.shape[0] - acc_ref.shape[0]) // 2
    acc_ref[...] = jnp.zeros(acc_ref.shape, F32)
    all_features(far_ref, far_ref.shape[0], st_ref, mc_ref)
    run_items(2, cap, list_ref, count_ref, st_ref, mc_ref, lambda c: own_ref[c + edge], off_ref, acc_ref)


def last_pass(
    half_ref, list_ref, count_ref, off_ref, own_ref, other_ref, far_ref, low_ref, high_ref,
    acc0_ref, acc1_ref, acc2_ref, base_ref, link_ref,
    drift_ref, sq_ref, part_ref,
    acc_ref, st_ref, mc_ref, cube_ref, *, cap
):
    cx, cy = drift_ref.shape[:2]
    px = cx + 2
    half = half_ref[0]
    lane = lax.broadcasted_iota(I32, (1, 128), 1)
    acc_ref[...] = acc0_ref[...] + acc1_ref[...] + acc2_ref[...]
    rows = px // 2

    def strips(part, carry):
        for step in range(rows):
            x = part * rows + step
            for plane in range(3):
                source_features(low_ref[plane, x], plane * px + x, st_ref, mc_ref)
                source_features(high_ref[plane, x], (3 + plane) * px + x, st_ref, mc_ref)
        return carry

    lax.fori_loop(0, 2, strips, 0)
    run_items(3, cap, list_ref, count_ref, st_ref, mc_ref, lambda c: own_ref[c + cy], off_ref, acc_ref)

    def fill(z, ref, plane):
        for x in range(px):
            cube_ref[z, x, 0] = low_ref[plane, x]
            cube_ref[z, x, 1 : cy + 1] = ref[x * cy : (x + 1) * cy]
            cube_ref[z, x, cy + 1] = high_ref[plane, x]

    fill(1, own_ref, 0)

    @pl.when(half == 0)
    def _():
        fill(0, far_ref, 2)
        fill(2, other_ref, 1)

    @pl.when(half != 0)
    def _():
        fill(0, other_ref, 1)
        fill(2, far_ref, 2)

    sub = sublanes()
    for x in range(px):
        for y in range(cy + 2):
            cube_ref[0, x, y] = jnp.where(sub < 4, pltpu.roll(cube_ref[0, x, y], 4, 0), cube_ref[2, x, y])

    def one_cell(x, y):
        cell = x * cy + y
        dcode = link_ref[cell, 0:1]
        dslot = jnp.broadcast_to(link_ref[cell, 1:2], (8, 128))
        key = jnp.where(sub < 4, dcode, dcode - 2)
        level = jnp.zeros((8, 128), F32)
        sides = jnp.zeros((8, 128), F32)
        for dx in range(3):
            for dy in range(3):
                code = 9 * dx + 3 * dy
                got = jnp.take_along_axis(cube_ref[1, x + dx, y + dy], dslot, axis=1)
                level = jnp.where(dcode == code + 1, got, level)
                got = jnp.take_along_axis(cube_ref[0, x + dx, y + dy], dslot, axis=1)
                sides = jnp.where(key == code, got, sides)
        found = (level[4:7] + sides[4:7]) + sides[:3]
        error = base_ref[cell, :3] + found - HALF_KICK * acc_ref[cell, :3]
        alive = base_ref[cell, 3:4]
        drift_ref[x, y, :, 0] = jnp.where(alive > 0.0, error, 0.0)
        squared = jnp.where(alive > 0.0, jnp.sum(error * error, axis=0, keepdims=True), 0.0)
        sq_ref[x, y] = squared
        return squared, alive

    def one_row(x, carry):
        total, live = carry
        for y in range(cy):
            squared, alive = one_cell(x, y)
            total = total + squared
            live = live + alive
        return total, live

    zero = jnp.zeros((1, 128), F32)
    total, live = lax.fori_loop(0, cx, one_row, (zero, zero), unroll=4)

    def folded(v):
        return v + pltpu.roll(jnp.broadcast_to(v, (8, 128)), 64, 1)[:1]

    part_ref[...] = jnp.where(lane < 64, folded(total), folded(live))


def scaled(rows_ref, sq_ref, drift_ref, tension_ref, out_ref, sem):
    copy = pltpu.make_async_copy(drift_ref, out_ref, sem)
    copy.start()
    lane = lax.broadcasted_iota(I32, (1, 128), 1)
    sums = jnp.sum(rows_ref[...], axis=0, keepdims=True)
    total = jnp.sum(jnp.where(lane < 64, sums, 0.0), axis=1, keepdims=True)
    live = jnp.sum(jnp.where(lane < 64, 0.0, sums), axis=1, keepdims=True)
    bound = jnp.broadcast_to(total / live + 1e-06, (1, 128))
    for x in range(sq_ref.shape[0]):
        for y in range(sq_ref.shape[1]):
            tension_ref[x, y] = sq_ref[x, y] / bound
    copy.wait()


SMEM = pl.BlockSpec(memory_space=pltpu.SMEM)
VMEM = pl.BlockSpec(memory_space=pltpu.VMEM)


def cost(items):
    pairs = items * 128 * 128
    return pl.CostEstimate(flops=400 * pairs, transcendentals=pairs, bytes_accessed=1 << 20)


def params():
    return pltpu.CompilerParams(vmem_limit_bytes=40 << 20)


def small_params():
    return pltpu.CompilerParams(vmem_limit_bytes=4 << 20)


def features_of(sources):
    return [pltpu.VMEM((sources, 128, 48), BF16), pltpu.VMEM((sources, 32, 128), BF16)]


def first_forces(half, neighbour_lists, cnt, own, vel, descendants):
    cx, cy = neighbour_lists.shape[:2]
    cells = cx * cy
    items = cells * neighbour_lists.shape[3]
    cap = items + max(BATCHES)
    rows = jax.ShapeDtypeStruct((cells, 8, 128), F32)
    return pl.pallas_call(
        functools.partial(own_pass, cap=cap),
        in_specs=[SMEM] * 4 + [VMEM] * 4,
        out_specs=[SMEM, SMEM] + [VMEM] * 5,
        out_shape=[
            jax.ShapeDtypeStruct((CLASSES * cap,), I32),
            jax.ShapeDtypeStruct((CLASSES,), I32),
            rows,
            rows,
            jax.ShapeDtypeStruct((cells, 8, 128), I32),
            rows,
            jax.ShapeDtypeStruct((27, 8, 128), F32),
        ],
        scratch_shapes=features_of(cells),
        cost_estimate=cost(items // 4),
        compiler_params=params(),
    )(half, item_table(cx, cy), neighbour_lists, cnt, offset_table(), own, vel, descendants)


def other_forces(lists, counts, offsets, own, other, cells, px):
    cap = lists.shape[0] // CLASSES
    strip = jax.ShapeDtypeStruct((2, px, 8, 128), F32)
    return pl.pallas_call(
        functools.partial(other_pass, cap=cap),
        in_specs=[SMEM, SMEM, VMEM, VMEM, VMEM],
        out_specs=[VMEM] * 3,
        out_shape=[jax.ShapeDtypeStruct((cells, 8, 128), F32), strip, strip],
        scratch_shapes=features_of(2 * own.shape[0] - cells),
        cost_estimate=cost(cap // 4),
        compiler_params=params(),
    )(lists, counts, offsets, own, other)


def far_forces(lists, counts, offsets, own, far, cells):
    cap = lists.shape[0] // CLASSES
    return pl.pallas_call(
        functools.partial(far_pass, cap=cap),
        in_specs=[SMEM, SMEM, VMEM, VMEM, VMEM],
        out_specs=VMEM,
        out_shape=jax.ShapeDtypeStruct((cells, 8, 128), F32),
        scratch_shapes=features_of(far.shape[0]),
        cost_estimate=cost(cap // 4),
        compiler_params=params(),
    )(lists, counts, offsets, own, far)


def finish(half, lists, counts, offsets, planes, low, high, sums, base, links, cx, cy):
    px = cx + 2
    cap = lists.shape[0] // CLASSES
    return pl.pallas_call(
        functools.partial(last_pass, cap=cap),
        in_specs=[SMEM] * 3 + [VMEM] * 11,
        out_specs=[VMEM, VMEM, VMEM],
        out_shape=[
            jax.ShapeDtypeStruct((cx, cy, 3, 1, 128), F32),
            jax.ShapeDtypeStruct((cx, cy, 1, 128), F32),
            jax.ShapeDtypeStruct((1, 128), F32),
        ],
        scratch_shapes=[pltpu.VMEM((cx * cy, 8, 128), F32)]
        + features_of(6 * px)
        + [pltpu.VMEM((3, px, cy + 2, 8, 128), F32)],
        cost_estimate=cost(cap // 4),
        compiler_params=params(),
    )(half, lists, counts, offsets, *planes, low, high, *sums, base, links)


def shards(positions_now, velocities, positions_next, halo_counts, neighbour_lists, descendants):
    cx, cy, cz, _, slots = positions_now.shape
    half = lax.axis_index("gz_1")
    xs = lax.axis_size("gz_0")
    zs = lax.axis_size("gx")
    ny = lax.axis_size(GY)
    nxt = jnp.transpose(positions_next, (0, 1, 3, 2, 4))
    vel = jnp.transpose(velocities, (0, 1, 3, 2, 4))
    cnt = jnp.transpose(halo_counts, (1, 2, 0))
    own, sent = pl.pallas_call(
        assemble,
        in_specs=[SMEM, VMEM, VMEM],
        out_specs=[VMEM, VMEM],
        out_shape=[
            jax.ShapeDtypeStruct((cx * cy, 8, slots), F32),
            jax.ShapeDtypeStruct((cx * cy - cy, 8, slots), F32),
        ],
    )(cnt, positions_now, nxt)
    swap = [(0, 1), (1, 0)]
    sent = lax.ppermute(sent, "gz_1", swap)
    last = cx * cy - cy
    below = lax.ppermute(own[last:], ZRING, zring_pairs(zs, 1))
    above = lax.ppermute(own[:cy], ZRING, zring_pairs(zs, -1))
    edges = jnp.concatenate([below, above])
    traded = lax.ppermute(edges, "gz_1", swap)
    lists, counts, acc0, base, links, own, offsets = first_forces(
        half[None], neighbour_lists, cnt, own, vel, descendants
    )
    place = lax.axis_index("gx")
    ends = ((slice(0, cy), place == 0), (slice(cy, 2 * cy), place == zs - 1))
    own_ends = [jnp.where(crossing, traded[part], edges[part]) for part, crossing in ends]
    other_ends = [jnp.where(crossing, edges[part], traded[part]) for part, crossing in ends]
    own = jnp.concatenate([own_ends[0], own, own_ends[1]])
    other = jnp.concatenate([other_ends[0], unpacked(sent, cx, cy), other_ends[1]])
    far = lax.ppermute(other, GZ, xhop_pairs(xs))
    acc1, top, bottom = other_forces(lists, counts, offsets, own, other, cx * cy, cx + 2)
    rows = far.reshape(cx + 2, cy * 8, slots)
    low = lax.ppermute(jnp.concatenate([top, rows[None, :, 8 * cy - 8 :]]), GY, ring(ny, 1))
    high = lax.ppermute(jnp.concatenate([bottom, rows[None, :, :8]]), GY, ring(ny, -1))
    acc2 = far_forces(lists, counts, offsets, own, far, cx * cy)
    drift, squared, part = finish(
        half[None], lists, counts, offsets, (own, other, far), low, high, (acc0, acc1, acc2), base, links, cx, cy
    )

    def gathered(row, axes):
        count = lax.axis_size(axes)
        return lax.all_to_all(jnp.broadcast_to(row, (count, slots)), axes, 0, 0, tiled=True)

    sums = jnp.sum(gathered(part, XYC), axis=0, keepdims=True)
    tension, drift = pl.pallas_call(
        scaled,
        in_specs=[VMEM, VMEM, VMEM],
        out_specs=[VMEM, pl.BlockSpec(memory_space=pl.ANY)],
        out_shape=[
            jax.ShapeDtypeStruct((cx, cy, cz, slots), F32),
            jax.ShapeDtypeStruct(drift.shape, F32),
        ],
        scratch_shapes=[pltpu.SemaphoreType.DMA],
        compiler_params=small_params(),
    )(gathered(sums, ZRING), squared, drift)
    return jnp.transpose(drift, (0, 1, 3, 2, 4)), tension


def solution(mesh):
    finer = Mesh(mesh.devices.reshape(mesh.shape["gx"], 4, 2, 4, 2), AXES)
    return jax.shard_map(
        shards,
        mesh=finer,
        in_specs=(
            P("gx", GY, GZ, None, None),
            P("gx", GY, GZ, None, None),
            P("gx", GY, GZ, None, None),
            P("gx", GY, GZ),
            P("gx", GY, GZ, None),
            P("gx", GY, GZ, None, None),
        ),
        out_specs=(P("gx", GY, GZ, None, None), P("gx", GY, GZ, None)),
        check_vma=False,
    )
```

```python
import functools

import jax
import jax.numpy as jnp
import numpy as np
from jax import lax
from jax.experimental import pallas as pl
from jax.experimental.pallas import tpu as pltpu
from jax.sharding import Mesh
from jax.sharding import PartitionSpec as P

AXES = ("gx", "gy_0", "gy_1", "gz_0", "gz_1")
GY = ("gy_0", "gy_1")
GZ = ("gz_0", "gz_1")
ZRING = ("gx", "gz_1")
XYC = ("gz_0", "gy_0", "gy_1")

EPS_SQ = 0.01
STEP_DT = 0.3
HALF_KICK = 0.045


def ring(count, step):
    return [(i, (i + step) % count) for i in range(count)]


def xhop_pairs(count):
    pairs = []
    for x in range(count):
        pairs.append((2 * x, 2 * ((x + 1) % count)))
        pairs.append((2 * x + 1, 2 * ((x - 1) % count) + 1))
    return pairs


def zring_pairs(low, step):
    total = 2 * low

    def flat(z):
        return (z % low) * 2 + z // low

    return [(flat(z), flat((z + step) % total)) for z in range(total)]


def split3(v):
    high = v.astype(jnp.bfloat16).astype(jnp.float32)
    rest = v - high
    mid = rest.astype(jnp.bfloat16).astype(jnp.float32)
    return high, mid, rest - mid


def carried(cx, cy):
    assert 7 * cy <= cx * cy - cy
    return cx // 2 * cy - cy


def unpacked(sent, cx, cy):
    first = carried(cx, cy)
    rows = sent[: 7 * cy, 7].reshape(cy, 7, sent.shape[2])
    cells = jnp.pad(rows, ((0, 0), (0, 1), (0, 0)))
    return jnp.concatenate([sent[:first], cells, sent[first:]])


def assemble(cnt_ref, now_ref, next_ref, own_ref, sent_ref):
    lane = lax.broadcasted_iota(jnp.int32, (1, 128), 1)
    cx, cy = now_ref.shape[:2]
    for x in range(cx):
        for y in range(cy):
            cell = x * cy + y
            own_ref[cell, :3] = now_ref[x, y, 0, :3]
            own_ref[cell, 3:4] = jnp.where(lane < cnt_ref[y, 0, x], now_ref[x, y, 0, 3:4], 0.0)
            own_ref[cell, 4:7] = next_ref[x, y, :, 0]
            own_ref[cell, 7:] = jnp.zeros((1, 128), jnp.float32)
    first = carried(cx, cy)
    for t in range(cx * cy - cy):
        sent_ref[t] = own_ref[t if t < first else t + cy]
    for k in range(cy):
        for r in range(7):
            sent_ref[7 * k + r, 7:] = own_ref[first + k, r : r + 1]


CLASSES = 4
BATCHES = (40, 75, 70, 88)
F32, BF16, I32 = jnp.float32, jnp.bfloat16, jnp.int32


def item_table(cx, cy):
    px = cx + 2
    table = np.zeros((2, 3, 3, 27), np.int32)
    for half in range(2):
        for xe in range(3):
            for ye in range(3):
                for code in range(27):
                    dx, dy, dz = code // 9, code // 3 % 3, code % 3
                    plane = 0 if dz == 1 else (1 if (dz == 2) == (half == 0) else 2)
                    x_in = not (xe == 0 and dx == 0 or xe == 2 and dx == 2)
                    if ye == 0 and dy == 0 or ye == 2 and dy == 2:
                        kind, step = 3, (3 * px if dy == 2 else 0) + plane * px + dx
                    elif plane == 2:
                        kind, step = 2, dx * cy + dy - 1
                    elif plane == 1:
                        kind, step = 1, dx * cy + dy - 1
                    elif x_in:
                        kind, step = 0, (dx - 1) * cy + dy - 1
                    else:
                        kind = 1
                        step = px * cy + dy - 1 if dx == 0 else (px + 1 - (cx - 1)) * cy + dy - 1
                    table[half, xe, ye, code] = 4 * (1024 * step + 32 * code) + kind
    return table.reshape(-1)


def offset_table():
    codes = np.arange(27)
    rows = np.stack([codes // 9, codes // 3 % 3, codes % 3], 1).astype(np.float32) - 0.5
    return np.broadcast_to(np.pad(rows, ((0, 0), (0, 5)))[:, :, None], (27, 8, 128)).copy()


def sublanes():
    return lax.broadcasted_iota(I32, (8, 128), 0)


def source_features(src, index, st_ref, mc_ref):
    sub = sublanes()
    q = jnp.where(sub < 3, src - 0.5, 0.0)
    norm = jnp.sum(q * q, axis=0, keepdims=True)
    s8 = jnp.where(sub < 3, -2.0 * q, jnp.where(sub == 3, norm, jnp.where(sub == 4, 1.0, 0.0)))
    m8 = jnp.where(sub == 3, 1.0, q) * src[3:4]
    sh, sm, sl = split3(s8)
    mh, mm, ml = split3(m8)
    st_ref[index] = jnp.transpose(jnp.concatenate([sh, sm, sl, sh, sm, sh], axis=0)).astype(BF16)
    mc_ref[index] = jnp.concatenate([mh, mm, ml, jnp.zeros_like(ml)], axis=0).astype(BF16)


def run_items(kind, cap, list_ref, count_ref, st_ref, mc_ref, own_of, off_ref, acc_ref):
    sub = sublanes()
    size = BATCHES[kind]
    count = count_ref[kind]

    def batch(b, carry):
        sums = []
        for t in range(size):
            place = b * size + t
            valid = place < count
            item = jnp.where(valid, list_ref[kind * cap + place], 0)
            src, code, cell = item >> 10, (item >> 5) & 31, item & 31
            p = jnp.where(sub < 3, own_of(cell) - off_ref[code], 0.0)
            norm = jnp.sum(p * p, axis=0, keepdims=True) + EPS_SQ
            p8 = jnp.where(sub == 3, 1.0, jnp.where(sub == 4, norm, p))
            ph, pm, pr = split3(p8)
            pcat = jnp.concatenate([ph, ph, ph, pm, pm, pr], axis=0).astype(BF16)
            dist = jnp.dot(st_ref[src], pcat, preferred_element_type=F32)
            inv = lax.rsqrt(dist)
            weight = inv * inv * inv
            wh = weight.astype(BF16)
            wl = (weight - wh.astype(F32)).astype(BF16)
            mc = mc_ref[src]
            a = jnp.dot(
                jnp.concatenate([mc, mc], axis=1), jnp.concatenate([wh, wl], axis=0), preferred_element_type=F32
            )
            a8 = (a[16:24] + a[8:16]) + a[:8]
            sums.append((cell, (a8 - p * a8[3:4]) * valid.astype(F32)))
        for cell, add in sums:
            acc_ref[cell] = acc_ref[cell] + add
        return carry

    lax.fori_loop(0, (count + size - 1) // size, batch, 0)


def own_pass(
    half_ref, table_ref, nbr_ref, cnt_ref, off_ref, own_ref, vel_ref, desc_ref,
    list_ref, count_ref, acc_ref, base_ref, link_ref, kept_ref, table_out_ref, st_ref, mc_ref, *, cap
):
    cx, cy = nbr_ref.shape[:2]
    kept_ref[...] = own_ref[...]
    table_out_ref[...] = off_ref[...]
    width = nbr_ref.shape[3]
    half = half_ref[0]
    lane = lax.broadcasted_iota(I32, (1, 128), 1)
    for kind in range(CLASSES):
        count_ref[kind] = 0
    acc_ref[...] = jnp.zeros(acc_ref.shape, F32)

    def one_row(x, carry):
        xe = jnp.where(x == 0, 0, jnp.where(x == cx - 1, 2, 1))
        for y in range(cy):
            cell = x * cy + y
            ye = (0 if y == 0 else 1) if y < cy - 1 else 2
            row = ((half * 3 + xe) * 3 + ye) * 27
            for k in range(width):
                entry = table_ref[row + nbr_ref[x, y, 0, k]]
                kind = entry & 3
                item = (entry >> 2) + jnp.where(kind == 3, cell + 1024 * x, 1025 * cell)
                place = count_ref[kind]
                list_ref[kind * cap + place] = item
                count_ref[kind] = place + 1
            own = own_ref[cell]
            source_features(own, cell, st_ref, mc_ref)
            dcode = desc_ref[x, y, 0, 0:1, :]
            ox = (dcode >= 9).astype(I32) + (dcode >= 18).astype(I32)
            rest = dcode - 9 * ox
            oy = (rest >= 3).astype(I32) + (rest >= 6).astype(I32)
            oz = rest - 3 * oy
            offset = jnp.concatenate([ox, oy, oz], axis=0).astype(F32) - 1.0
            base_ref[cell, :3] = offset - (own[:3] + STEP_DT * vel_ref[x, y, :, 0])
            base_ref[cell, 3:4] = (lane < cnt_ref[y, 0, x]).astype(F32)
            link_ref[cell, :2] = desc_ref[x, y, 0]
        return carry

    lax.fori_loop(0, cx, one_row, 0)
    run_items(0, cap, list_ref, count_ref, st_ref, mc_ref, lambda c: own_ref[c], off_ref, acc_ref)


def all_features(ref, count, st_ref, mc_ref):
    part = count // 2

    def some(i, carry):
        for step in range(part):
            source_features(ref[i * part + step], i * part + step, st_ref, mc_ref)
        return carry

    lax.fori_loop(0, 2, some, 0)


def other_pass(
    list_ref, count_ref, off_ref, own_ref, other_ref, acc_ref, top_ref, bottom_ref, st_ref, mc_ref, *, cap
):
    px = top_ref.shape[1]
    cells = own_ref.shape[0]
    cy = cells // px
    acc_ref[...] = jnp.zeros(acc_ref.shape, F32)
    for plane, ref in enumerate((own_ref, other_ref)):
        for x in range(px):
            top_ref[plane, x] = ref[x * cy + cy - 1]
            bottom_ref[plane, x] = ref[x * cy]
    all_features(other_ref, cells, st_ref, mc_ref)
    for y in range(cy):
        source_features(own_ref[y], cells + y, st_ref, mc_ref)
        source_features(own_ref[cells - cy + y], cells + cy + y, st_ref, mc_ref)
    run_items(1, cap, list_ref, count_ref, st_ref, mc_ref, lambda c: own_ref[c + cy], off_ref, acc_ref)


def far_pass(list_ref, count_ref, off_ref, own_ref, far_ref, acc_ref, st_ref, mc_ref, *, cap):
    edge = (own_ref.shape[0] - acc_ref.shape[0]) // 2
    acc_ref[...] = jnp.zeros(acc_ref.shape, F32)
    all_features(far_ref, far_ref.shape[0], st_ref, mc_ref)
    run_items(2, cap, list_ref, count_ref, st_ref, mc_ref, lambda c: own_ref[c + edge], off_ref, acc_ref)


def last_pass(
    half_ref, list_ref, count_ref, off_ref, own_ref, other_ref, far_ref, low_ref, high_ref,
    acc0_ref, acc1_ref, acc2_ref, base_ref, link_ref,
    drift_ref, sq_ref, part_ref,
    acc_ref, st_ref, mc_ref, cube_ref, out_ref, sems, *, cap
):
    cx, cy = out_ref.shape[:2]
    px = cx + 2
    half = half_ref[0]
    lane = lax.broadcasted_iota(I32, (1, 128), 1)
    acc_ref[...] = acc0_ref[...] + acc1_ref[...] + acc2_ref[...]
    rows = px // 2

    def strips(part, carry):
        for step in range(rows):
            x = part * rows + step
            for plane in range(3):
                source_features(low_ref[plane, x], plane * px + x, st_ref, mc_ref)
                source_features(high_ref[plane, x], (3 + plane) * px + x, st_ref, mc_ref)
        return carry

    lax.fori_loop(0, 2, strips, 0)
    run_items(3, cap, list_ref, count_ref, st_ref, mc_ref, lambda c: own_ref[c + cy], off_ref, acc_ref)

    def fill(z, ref, plane):
        for x in range(px):
            cube_ref[z, x, 0] = low_ref[plane, x]
            cube_ref[z, x, 1 : cy + 1] = ref[x * cy : (x + 1) * cy]
            cube_ref[z, x, cy + 1] = high_ref[plane, x]

    fill(1, own_ref, 0)

    @pl.when(half == 0)
    def _():
        fill(0, far_ref, 2)
        fill(2, other_ref, 1)

    @pl.when(half != 0)
    def _():
        fill(0, other_ref, 1)
        fill(2, far_ref, 2)

    sub = sublanes()
    for x in range(px):
        for y in range(cy + 2):
            cube_ref[0, x, y] = jnp.where(sub < 4, pltpu.roll(cube_ref[0, x, y], 4, 0), cube_ref[2, x, y])

    def one_cell(x, y):
        cell = x * cy + y
        dcode = link_ref[cell, 0:1]
        dslot = jnp.broadcast_to(link_ref[cell, 1:2], (8, 128))
        key = jnp.where(sub < 4, dcode, dcode - 2)
        level = jnp.zeros((8, 128), F32)
        sides = jnp.zeros((8, 128), F32)
        for dx in range(3):
            for dy in range(3):
                code = 9 * dx + 3 * dy
                got = jnp.take_along_axis(cube_ref[1, x + dx, y + dy], dslot, axis=1)
                level = jnp.where(dcode == code + 1, got, level)
                got = jnp.take_along_axis(cube_ref[0, x + dx, y + dy], dslot, axis=1)
                sides = jnp.where(key == code, got, sides)
        found = (level[4:7] + sides[4:7]) + sides[:3]
        error = base_ref[cell, :3] + found - HALF_KICK * acc_ref[cell, :3]
        alive = base_ref[cell, 3:4]
        out_ref[x, y, :, 0] = jnp.where(alive > 0.0, error, 0.0)
        squared = jnp.where(alive > 0.0, jnp.sum(error * error, axis=0, keepdims=True), 0.0)
        sq_ref[x, y] = squared
        return squared, alive

    def one_row(x, carry):
        total, live = carry
        for y in range(cy):
            squared, alive = one_cell(x, y)
            total = total + squared
            live = live + alive
        pltpu.make_async_copy(out_ref.at[x], drift_ref.at[x], sems.at[x]).start()
        return total, live

    zero = jnp.zeros((1, 128), F32)
    total, live = lax.fori_loop(0, cx, one_row, (zero, zero), unroll=4)

    def folded(v):
        return v + pltpu.roll(jnp.broadcast_to(v, (8, 128)), 64, 1)[:1]

    part_ref[...] = jnp.where(lane < 64, folded(total), folded(live))
    for x in range(cx):
        pltpu.make_async_copy(out_ref.at[x], drift_ref.at[x], sems.at[x]).wait()


def scaled(rows_ref, sq_ref, tension_ref):
    lane = lax.broadcasted_iota(I32, (1, 128), 1)
    sums = jnp.sum(rows_ref[...], axis=0, keepdims=True)
    total = jnp.sum(jnp.where(lane < 64, sums, 0.0), axis=1, keepdims=True)
    live = jnp.sum(jnp.where(lane < 64, 0.0, sums), axis=1, keepdims=True)
    bound = jnp.broadcast_to(total / live + 1e-06, (1, 128))
    for x in range(sq_ref.shape[0]):
        for y in range(sq_ref.shape[1]):
            tension_ref[x, y] = sq_ref[x, y] / bound


SMEM = pl.BlockSpec(memory_space=pltpu.SMEM)
VMEM = pl.BlockSpec(memory_space=pltpu.VMEM)


def cost(items):
    pairs = items * 128 * 128
    return pl.CostEstimate(flops=400 * pairs, transcendentals=pairs, bytes_accessed=1 << 20)


def params():
    return pltpu.CompilerParams(vmem_limit_bytes=40 << 20)


def small_params():
    return pltpu.CompilerParams(vmem_limit_bytes=4 << 20)


def features_of(sources):
    return [pltpu.VMEM((sources, 128, 48), BF16), pltpu.VMEM((sources, 32, 128), BF16)]


def first_forces(half, neighbour_lists, cnt, own, vel, descendants):
    cx, cy = neighbour_lists.shape[:2]
    cells = cx * cy
    items = cells * neighbour_lists.shape[3]
    cap = items + max(BATCHES)
    rows = jax.ShapeDtypeStruct((cells, 8, 128), F32)
    return pl.pallas_call(
        functools.partial(own_pass, cap=cap),
        in_specs=[SMEM] * 4 + [VMEM] * 4,
        out_specs=[SMEM, SMEM] + [VMEM] * 5,
        out_shape=[
            jax.ShapeDtypeStruct((CLASSES * cap,), I32),
            jax.ShapeDtypeStruct((CLASSES,), I32),
            rows,
            rows,
            jax.ShapeDtypeStruct((cells, 8, 128), I32),
            rows,
            jax.ShapeDtypeStruct((27, 8, 128), F32),
        ],
        scratch_shapes=features_of(cells),
        cost_estimate=cost(items // 4),
        compiler_params=params(),
    )(half, item_table(cx, cy), neighbour_lists, cnt, offset_table(), own, vel, descendants)


def other_forces(lists, counts, offsets, own, other, cells, px):
    cap = lists.shape[0] // CLASSES
    strip = jax.ShapeDtypeStruct((2, px, 8, 128), F32)
    return pl.pallas_call(
        functools.partial(other_pass, cap=cap),
        in_specs=[SMEM, SMEM, VMEM, VMEM, VMEM],
        out_specs=[VMEM] * 3,
        out_shape=[jax.ShapeDtypeStruct((cells, 8, 128), F32), strip, strip],
        scratch_shapes=features_of(2 * own.shape[0] - cells),
        cost_estimate=cost(cap // 4),
        compiler_params=params(),
    )(lists, counts, offsets, own, other)


def far_forces(lists, counts, offsets, own, far, cells):
    cap = lists.shape[0] // CLASSES
    return pl.pallas_call(
        functools.partial(far_pass, cap=cap),
        in_specs=[SMEM, SMEM, VMEM, VMEM, VMEM],
        out_specs=VMEM,
        out_shape=jax.ShapeDtypeStruct((cells, 8, 128), F32),
        scratch_shapes=features_of(far.shape[0]),
        cost_estimate=cost(cap // 4),
        compiler_params=params(),
    )(lists, counts, offsets, own, far)


def finish(half, lists, counts, offsets, planes, low, high, sums, base, links, cx, cy):
    px = cx + 2
    cap = lists.shape[0] // CLASSES
    return pl.pallas_call(
        functools.partial(last_pass, cap=cap),
        in_specs=[SMEM] * 3 + [VMEM] * 11,
        out_specs=[pl.BlockSpec(memory_space=pl.ANY), VMEM, VMEM],
        out_shape=[
            jax.ShapeDtypeStruct((cx, cy, 3, 1, 128), F32),
            jax.ShapeDtypeStruct((cx, cy, 1, 128), F32),
            jax.ShapeDtypeStruct((1, 128), F32),
        ],
        scratch_shapes=[pltpu.VMEM((cx * cy, 8, 128), F32)]
        + features_of(6 * px)
        + [
            pltpu.VMEM((3, px, cy + 2, 8, 128), F32),
            pltpu.VMEM((cx, cy, 3, 1, 128), F32),
            pltpu.SemaphoreType.DMA((cx,)),
        ],
        cost_estimate=cost(cap // 4),
        compiler_params=params(),
    )(half, lists, counts, offsets, *planes, low, high, *sums, base, links)


def shards(positions_now, velocities, positions_next, halo_counts, neighbour_lists, descendants):
    cx, cy, cz, _, slots = positions_now.shape
    half = lax.axis_index("gz_1")
    xs = lax.axis_size("gz_0")
    zs = lax.axis_size("gx")
    ny = lax.axis_size(GY)
    nxt = jnp.transpose(positions_next, (0, 1, 3, 2, 4))
    vel = jnp.transpose(velocities, (0, 1, 3, 2, 4))
    cnt = jnp.transpose(halo_counts, (1, 2, 0))
    own, sent = pl.pallas_call(
        assemble,
        in_specs=[SMEM, VMEM, VMEM],
        out_specs=[VMEM, VMEM],
        out_shape=[
            jax.ShapeDtypeStruct((cx * cy, 8, slots), F32),
            jax.ShapeDtypeStruct((cx * cy - cy, 8, slots), F32),
        ],
    )(cnt, positions_now, nxt)
    sent = lax.ppermute(sent, "gz_1", [(0, 1), (1, 0)])
    other = unpacked(sent, cx, cy)
    lists, counts, acc0, base, links, own, offsets = first_forces(
        half[None], neighbour_lists, cnt, own, vel, descendants
    )

    def both(start):
        place = start if start == 0 else start - cy
        ends = own[start : start + cy], sent[place : place + cy]
        return jnp.where(half == 0, jnp.stack(ends), jnp.stack(ends[::-1]))

    below = lax.ppermute(both(cx * cy - cy), ZRING, zring_pairs(zs, 1))
    above = lax.ppermute(both(0), ZRING, zring_pairs(zs, -1))

    def widened(block, plane):
        ends = [jnp.where(plane == 0, v[0], v[1]) for v in (below, above)]
        return jnp.concatenate([ends[0], block, ends[1]], axis=0)

    own = widened(own, half)
    other = widened(other, 1 - half)
    far = lax.ppermute(other, GZ, xhop_pairs(xs))
    acc1, top, bottom = other_forces(lists, counts, offsets, own, other, cx * cy, cx + 2)
    rows = far.reshape(cx + 2, cy * 8, slots)
    low = lax.ppermute(jnp.concatenate([top, rows[None, :, 8 * cy - 8 :]]), GY, ring(ny, 1))
    high = lax.ppermute(jnp.concatenate([bottom, rows[None, :, :8]]), GY, ring(ny, -1))
    acc2 = far_forces(lists, counts, offsets, own, far, cx * cy)
    drift, squared, part = finish(
        half[None], lists, counts, offsets, (own, other, far), low, high, (acc0, acc1, acc2), base, links, cx, cy
    )

    def gathered(row, axes):
        count = lax.axis_size(axes)
        return lax.all_to_all(jnp.broadcast_to(row, (count, slots)), axes, 0, 0, tiled=True)

    sums = jnp.sum(gathered(part, XYC), axis=0, keepdims=True)
    tension = pl.pallas_call(
        scaled,
        in_specs=[VMEM, VMEM],
        out_specs=VMEM,
        out_shape=jax.ShapeDtypeStruct((cx, cy, cz, slots), F32),
        compiler_params=small_params(),
    )(gathered(sums, ZRING), squared)
    return jnp.transpose(drift, (0, 1, 3, 2, 4)), tension


def solution(mesh):
    finer = Mesh(mesh.devices.reshape(mesh.shape["gx"], 4, 2, 4, 2), AXES)
    return jax.shard_map(
        shards,
        mesh=finer,
        in_specs=(
            P("gx", GY, GZ, None, None),
            P("gx", GY, GZ, None, None),
            P("gx", GY, GZ, None, None),
            P("gx", GY, GZ),
            P("gx", GY, GZ, None),
            P("gx", GY, GZ, None, None),
        ),
        out_specs=(P("gx", GY, GZ, None, None), P("gx", GY, GZ, None)),
        check_vma=False,
    )
```

```python
import functools

import jax
import jax.numpy as jnp
import numpy as np
from jax import lax
from jax.experimental import pallas as pl
from jax.experimental.pallas import tpu as pltpu
from jax.sharding import Mesh
from jax.sharding import PartitionSpec as P

AXES = ("gx", "gy_0", "gy_1", "gz_0", "gz_1")
GY = ("gy_0", "gy_1")
GZ = ("gz_0", "gz_1")
ZRING = ("gx", "gz_1")
XY = ("gz_0", "gy_0")
ZC = ("gx", "gz_1", "gy_1")

EPS_SQ = 0.01
STEP_DT = 0.3
HALF_KICK = 0.045


def ring(count, step):
    return [(i, (i + step) % count) for i in range(count)]


def xhop_pairs(count):
    pairs = []
    for x in range(count):
        pairs.append((2 * x, 2 * ((x + 1) % count)))
        pairs.append((2 * x + 1, 2 * ((x - 1) % count) + 1))
    return pairs


def zring_pairs(low, step):
    total = 2 * low

    def flat(z):
        return (z % low) * 2 + z // low

    return [(flat(z), flat((z + step) % total)) for z in range(total)]


def split3(v):
    high = v.astype(jnp.bfloat16).astype(jnp.float32)
    rest = v - high
    mid = rest.astype(jnp.bfloat16).astype(jnp.float32)
    return high, mid, rest - mid


def carried(cx, cy):
    assert 7 * cy <= cx * cy - cy
    return cx // 2 * cy - cy


def unpacked(sent, cx, cy):
    first = carried(cx, cy)
    rows = sent[: 7 * cy, 7].reshape(cy, 7, sent.shape[2])
    cells = jnp.pad(rows, ((0, 0), (0, 1), (0, 0)))
    return jnp.concatenate([sent[:first], cells, sent[first:]])


def assemble(cnt_ref, now_ref, next_ref, own_ref, sent_ref):
    lane = lax.broadcasted_iota(jnp.int32, (1, 128), 1)
    cx, cy = now_ref.shape[:2]
    for x in range(cx):
        for y in range(cy):
            cell = x * cy + y
            own_ref[cell, :3] = now_ref[x, y, 0, :3]
            own_ref[cell, 3:4] = jnp.where(lane < cnt_ref[y, 0, x], now_ref[x, y, 0, 3:4], 0.0)
            own_ref[cell, 4:7] = next_ref[x, y, :, 0]
            own_ref[cell, 7:] = jnp.zeros((1, 128), jnp.float32)
    first = carried(cx, cy)
    for t in range(cx * cy - cy):
        sent_ref[t] = own_ref[t if t < first else t + cy]
    for k in range(cy):
        for r in range(7):
            sent_ref[7 * k + r, 7:] = own_ref[first + k, r : r + 1]


CLASSES = 4
BATCHES = (40, 75, 70, 88)
F32, BF16, I32 = jnp.float32, jnp.bfloat16, jnp.int32


def item_table(cx, cy):
    px = cx + 2
    table = np.zeros((2, 3, 3, 27), np.int32)
    for half in range(2):
        for xe in range(3):
            for ye in range(3):
                for code in range(27):
                    dx, dy, dz = code // 9, code // 3 % 3, code % 3
                    plane = 0 if dz == 1 else (1 if (dz == 2) == (half == 0) else 2)
                    x_in = not (xe == 0 and dx == 0 or xe == 2 and dx == 2)
                    if ye == 0 and dy == 0 or ye == 2 and dy == 2:
                        kind, step = 3, (3 * px if dy == 2 else 0) + plane * px + dx
                    elif plane == 2:
                        kind, step = 2, dx * cy + dy - 1
                    elif plane == 1:
                        kind, step = 1, dx * cy + dy - 1
                    elif x_in:
                        kind, step = 0, (dx - 1) * cy + dy - 1
                    else:
                        kind = 1
                        step = px * cy + dy - 1 if dx == 0 else (px + 1 - (cx - 1)) * cy + dy - 1
                    table[half, xe, ye, code] = 4 * (1024 * step + 32 * code) + kind
    return table.reshape(-1)


def offset_table():
    codes = np.arange(27)
    rows = np.stack([codes // 9, codes // 3 % 3, codes % 3], 1).astype(np.float32) - 0.5
    return np.broadcast_to(np.pad(rows, ((0, 0), (0, 5)))[:, :, None], (27, 8, 128)).copy()


def sublanes():
    return lax.broadcasted_iota(I32, (8, 128), 0)


def source_features(src, index, st_ref, mc_ref):
    sub = sublanes()
    q = jnp.where(sub < 3, src - 0.5, 0.0)
    norm = jnp.sum(q * q, axis=0, keepdims=True)
    s8 = jnp.where(sub < 3, -2.0 * q, jnp.where(sub == 3, norm, jnp.where(sub == 4, 1.0, 0.0)))
    m8 = jnp.where(sub == 3, 1.0, q) * src[3:4]
    sh, sm, sl = split3(s8)
    mh, mm, ml = split3(m8)
    st_ref[index] = jnp.transpose(jnp.concatenate([sh, sm, sl, sh, sm, sh], axis=0)).astype(BF16)
    mc_ref[index] = jnp.concatenate([mh, mm, ml, jnp.zeros_like(ml)], axis=0).astype(BF16)


def run_items(kind, cap, list_ref, count_ref, st_ref, mc_ref, own_of, off_ref, acc_ref):
    sub = sublanes()
    size = BATCHES[kind]
    count = count_ref[kind]

    def batch(b, carry):
        sums = []
        for t in range(size):
            place = b * size + t
            valid = place < count
            item = jnp.where(valid, list_ref[kind * cap + place], 0)
            src, code, cell = item >> 10, (item >> 5) & 31, item & 31
            p = jnp.where(sub < 3, own_of(cell) - off_ref[code], 0.0)
            norm = jnp.sum(p * p, axis=0, keepdims=True) + EPS_SQ
            p8 = jnp.where(sub == 3, 1.0, jnp.where(sub == 4, norm, p))
            ph, pm, pr = split3(p8)
            pcat = jnp.concatenate([ph, ph, ph, pm, pm, pr], axis=0).astype(BF16)
            dist = jnp.dot(st_ref[src], pcat, preferred_element_type=F32)
            inv = lax.rsqrt(dist)
            weight = inv * inv * inv
            wh = weight.astype(BF16)
            wl = (weight - wh.astype(F32)).astype(BF16)
            mc = mc_ref[src]
            a = jnp.dot(
                jnp.concatenate([mc, mc], axis=1), jnp.concatenate([wh, wl], axis=0), preferred_element_type=F32
            )
            a8 = (a[16:24] + a[8:16]) + a[:8]
            sums.append((cell, (a8 - p * a8[3:4]) * valid.astype(F32)))
        for cell, add in sums:
            acc_ref[cell] = acc_ref[cell] + add
        return carry

    lax.fori_loop(0, (count + size - 1) // size, batch, 0)


def own_pass(
    half_ref, table_ref, nbr_ref, cnt_ref, off_ref, own_ref, vel_ref, desc_ref,
    list_ref, count_ref, acc_ref, base_ref, link_ref, kept_ref, table_out_ref, st_ref, mc_ref, *, cap
):
    cx, cy = nbr_ref.shape[:2]
    kept_ref[...] = own_ref[...]
    table_out_ref[...] = off_ref[...]
    width = nbr_ref.shape[3]
    half = half_ref[0]
    lane = lax.broadcasted_iota(I32, (1, 128), 1)
    for kind in range(CLASSES):
        count_ref[kind] = 0
    acc_ref[...] = jnp.zeros(acc_ref.shape, F32)

    def one_row(x, carry):
        xe = jnp.where(x == 0, 0, jnp.where(x == cx - 1, 2, 1))
        for y in range(cy):
            cell = x * cy + y
            ye = (0 if y == 0 else 1) if y < cy - 1 else 2
            row = ((half * 3 + xe) * 3 + ye) * 27
            for k in range(width):
                entry = table_ref[row + nbr_ref[x, y, 0, k]]
                kind = entry & 3
                item = (entry >> 2) + jnp.where(kind == 3, cell + 1024 * x, 1025 * cell)
                place = count_ref[kind]
                list_ref[kind * cap + place] = item
                count_ref[kind] = place + 1
            own = own_ref[cell]
            source_features(own, cell, st_ref, mc_ref)
            dcode = desc_ref[x, y, 0, 0:1, :]
            ox = (dcode >= 9).astype(I32) + (dcode >= 18).astype(I32)
            rest = dcode - 9 * ox
            oy = (rest >= 3).astype(I32) + (rest >= 6).astype(I32)
            oz = rest - 3 * oy
            offset = jnp.concatenate([ox, oy, oz], axis=0).astype(F32) - 1.0
            base_ref[cell, :3] = offset - (own[:3] + STEP_DT * vel_ref[x, y, :, 0])
            base_ref[cell, 3:4] = (lane < cnt_ref[y, 0, x]).astype(F32)
            link_ref[cell, :2] = desc_ref[x, y, 0]
        return carry

    lax.fori_loop(0, cx, one_row, 0)
    run_items(0, cap, list_ref, count_ref, st_ref, mc_ref, lambda c: own_ref[c], off_ref, acc_ref)


def all_features(ref, count, st_ref, mc_ref):
    part = count // 2

    def some(i, carry):
        for step in range(part):
            source_features(ref[i * part + step], i * part + step, st_ref, mc_ref)
        return carry

    lax.fori_loop(0, 2, some, 0)


def other_pass(
    list_ref, count_ref, off_ref, own_ref, other_ref, acc_ref, top_ref, bottom_ref, st_ref, mc_ref, *, cap
):
    px = top_ref.shape[1]
    cells = own_ref.shape[0]
    cy = cells // px
    acc_ref[...] = jnp.zeros(acc_ref.shape, F32)
    for plane, ref in enumerate((own_ref, other_ref)):
        for x in range(px):
            top_ref[plane, x] = ref[x * cy + cy - 1]
            bottom_ref[plane, x] = ref[x * cy]
    all_features(other_ref, cells, st_ref, mc_ref)
    for y in range(cy):
        source_features(own_ref[y], cells + y, st_ref, mc_ref)
        source_features(own_ref[cells - cy + y], cells + cy + y, st_ref, mc_ref)
    run_items(1, cap, list_ref, count_ref, st_ref, mc_ref, lambda c: own_ref[c + cy], off_ref, acc_ref)


def far_pass(list_ref, count_ref, off_ref, own_ref, far_ref, acc_ref, st_ref, mc_ref, *, cap):
    edge = (own_ref.shape[0] - acc_ref.shape[0]) // 2
    acc_ref[...] = jnp.zeros(acc_ref.shape, F32)
    all_features(far_ref, far_ref.shape[0], st_ref, mc_ref)
    run_items(2, cap, list_ref, count_ref, st_ref, mc_ref, lambda c: own_ref[c + edge], off_ref, acc_ref)


def last_pass(
    half_ref, list_ref, count_ref, off_ref, own_ref, other_ref, far_ref, low_ref, high_ref,
    acc0_ref, acc1_ref, acc2_ref, base_ref, link_ref,
    drift_ref, sq_ref, part_ref,
    acc_ref, st_ref, mc_ref, cube_ref, out_ref, sems, *, cap
):
    cx, cy = out_ref.shape[:2]
    px = cx + 2
    half = half_ref[0]
    lane = lax.broadcasted_iota(I32, (1, 128), 1)
    acc_ref[...] = acc0_ref[...] + acc1_ref[...] + acc2_ref[...]
    rows = px // 2

    def strips(part, carry):
        for step in range(rows):
            x = part * rows + step
            for plane in range(3):
                source_features(low_ref[plane, x], plane * px + x, st_ref, mc_ref)
                source_features(high_ref[plane, x], (3 + plane) * px + x, st_ref, mc_ref)
        return carry

    lax.fori_loop(0, 2, strips, 0)
    run_items(3, cap, list_ref, count_ref, st_ref, mc_ref, lambda c: own_ref[c + cy], off_ref, acc_ref)

    def fill(z, ref, plane):
        for x in range(px):
            cube_ref[z, x, 0] = low_ref[plane, x]
            cube_ref[z, x, 1 : cy + 1] = ref[x * cy : (x + 1) * cy]
            cube_ref[z, x, cy + 1] = high_ref[plane, x]

    fill(1, own_ref, 0)

    @pl.when(half == 0)
    def _():
        fill(0, far_ref, 2)
        fill(2, other_ref, 1)

    @pl.when(half != 0)
    def _():
        fill(0, other_ref, 1)
        fill(2, far_ref, 2)

    sub = sublanes()
    for x in range(px):
        for y in range(cy + 2):
            cube_ref[0, x, y] = jnp.where(sub < 4, pltpu.roll(cube_ref[0, x, y], 4, 0), cube_ref[2, x, y])

    def one_cell(x, y):
        cell = x * cy + y
        dcode = link_ref[cell, 0:1]
        dslot = jnp.broadcast_to(link_ref[cell, 1:2], (8, 128))
        key = jnp.where(sub < 4, dcode, dcode - 2)
        level = jnp.zeros((8, 128), F32)
        sides = jnp.zeros((8, 128), F32)
        for dx in range(3):
            for dy in range(3):
                code = 9 * dx + 3 * dy
                got = jnp.take_along_axis(cube_ref[1, x + dx, y + dy], dslot, axis=1)
                level = jnp.where(dcode == code + 1, got, level)
                got = jnp.take_along_axis(cube_ref[0, x + dx, y + dy], dslot, axis=1)
                sides = jnp.where(key == code, got, sides)
        found = (level[4:7] + sides[4:7]) + sides[:3]
        error = base_ref[cell, :3] + found - HALF_KICK * acc_ref[cell, :3]
        alive = base_ref[cell, 3:4]
        out_ref[x, y, :, 0] = jnp.where(alive > 0.0, error, 0.0)
        squared = jnp.where(alive > 0.0, jnp.sum(error * error, axis=0, keepdims=True), 0.0)
        sq_ref[x, y] = squared
        return squared, alive

    def one_row(x, carry):
        total, live = carry
        for y in range(cy):
            squared, alive = one_cell(x, y)
            total = total + squared
            live = live + alive
        pltpu.make_async_copy(out_ref.at[x], drift_ref.at[x], sems.at[x]).start()
        return total, live

    zero = jnp.zeros((1, 128), F32)
    total, live = lax.fori_loop(0, cx, one_row, (zero, zero), unroll=4)

    def folded(v):
        return v + pltpu.roll(jnp.broadcast_to(v, (8, 128)), 64, 1)[:1]

    part_ref[...] = jnp.where(lane < 64, folded(total), folded(live))
    for x in range(cx):
        pltpu.make_async_copy(out_ref.at[x], drift_ref.at[x], sems.at[x]).wait()


def scaled(rows_ref, sq_ref, tension_ref):
    lane = lax.broadcasted_iota(I32, (1, 128), 1)
    sums = jnp.sum(rows_ref[...], axis=0, keepdims=True)
    total = jnp.sum(jnp.where(lane < 64, sums, 0.0), axis=1, keepdims=True)
    live = jnp.sum(jnp.where(lane < 64, 0.0, sums), axis=1, keepdims=True)
    bound = jnp.broadcast_to(total / live + 1e-06, (1, 128))
    for x in range(sq_ref.shape[0]):
        for y in range(sq_ref.shape[1]):
            tension_ref[x, y] = sq_ref[x, y] / bound


SMEM = pl.BlockSpec(memory_space=pltpu.SMEM)
VMEM = pl.BlockSpec(memory_space=pltpu.VMEM)


def cost(items):
    pairs = items * 128 * 128
    return pl.CostEstimate(flops=400 * pairs, transcendentals=pairs, bytes_accessed=1 << 20)


def params():
    return pltpu.CompilerParams(vmem_limit_bytes=40 << 20)


def small_params():
    return pltpu.CompilerParams(vmem_limit_bytes=4 << 20)


def features_of(sources):
    return [pltpu.VMEM((sources, 128, 48), BF16), pltpu.VMEM((sources, 32, 128), BF16)]


def first_forces(half, neighbour_lists, cnt, own, vel, descendants):
    cx, cy = neighbour_lists.shape[:2]
    cells = cx * cy
    items = cells * neighbour_lists.shape[3]
    cap = items + max(BATCHES)
    rows = jax.ShapeDtypeStruct((cells, 8, 128), F32)
    return pl.pallas_call(
        functools.partial(own_pass, cap=cap),
        in_specs=[SMEM] * 4 + [VMEM] * 4,
        out_specs=[SMEM, SMEM] + [VMEM] * 5,
        out_shape=[
            jax.ShapeDtypeStruct((CLASSES * cap,), I32),
            jax.ShapeDtypeStruct((CLASSES,), I32),
            rows,
            rows,
            jax.ShapeDtypeStruct((cells, 8, 128), I32),
            rows,
            jax.ShapeDtypeStruct((27, 8, 128), F32),
        ],
        scratch_shapes=features_of(cells),
        cost_estimate=cost(items // 4),
        compiler_params=params(),
    )(half, item_table(cx, cy), neighbour_lists, cnt, offset_table(), own, vel, descendants)


def other_forces(lists, counts, offsets, own, other, cells, px):
    cap = lists.shape[0] // CLASSES
    strip = jax.ShapeDtypeStruct((2, px, 8, 128), F32)
    return pl.pallas_call(
        functools.partial(other_pass, cap=cap),
        in_specs=[SMEM, SMEM, VMEM, VMEM, VMEM],
        out_specs=[VMEM] * 3,
        out_shape=[jax.ShapeDtypeStruct((cells, 8, 128), F32), strip, strip],
        scratch_shapes=features_of(2 * own.shape[0] - cells),
        cost_estimate=cost(cap // 4),
        compiler_params=params(),
    )(lists, counts, offsets, own, other)


def far_forces(lists, counts, offsets, own, far, cells):
    cap = lists.shape[0] // CLASSES
    return pl.pallas_call(
        functools.partial(far_pass, cap=cap),
        in_specs=[SMEM, SMEM, VMEM, VMEM, VMEM],
        out_specs=VMEM,
        out_shape=jax.ShapeDtypeStruct((cells, 8, 128), F32),
        scratch_shapes=features_of(far.shape[0]),
        cost_estimate=cost(cap // 4),
        compiler_params=params(),
    )(lists, counts, offsets, own, far)


def finish(half, lists, counts, offsets, planes, low, high, sums, base, links, cx, cy):
    px = cx + 2
    cap = lists.shape[0] // CLASSES
    return pl.pallas_call(
        functools.partial(last_pass, cap=cap),
        in_specs=[SMEM] * 3 + [VMEM] * 11,
        out_specs=[pl.BlockSpec(memory_space=pl.ANY), VMEM, VMEM],
        out_shape=[
            jax.ShapeDtypeStruct((cx, cy, 3, 1, 128), F32),
            jax.ShapeDtypeStruct((cx, cy, 1, 128), F32),
            jax.ShapeDtypeStruct((1, 128), F32),
        ],
        scratch_shapes=[pltpu.VMEM((cx * cy, 8, 128), F32)]
        + features_of(6 * px)
        + [
            pltpu.VMEM((3, px, cy + 2, 8, 128), F32),
            pltpu.VMEM((cx, cy, 3, 1, 128), F32),
            pltpu.SemaphoreType.DMA((cx,)),
        ],
        cost_estimate=cost(cap // 4),
        compiler_params=params(),
    )(half, lists, counts, offsets, *planes, low, high, *sums, base, links)


def shards(positions_now, velocities, positions_next, halo_counts, neighbour_lists, descendants):
    cx, cy, cz, _, slots = positions_now.shape
    half = lax.axis_index("gz_1")
    xs = lax.axis_size("gz_0")
    zs = lax.axis_size("gx")
    ny = lax.axis_size(GY)
    nxt = jnp.transpose(positions_next, (0, 1, 3, 2, 4))
    vel = jnp.transpose(velocities, (0, 1, 3, 2, 4))
    cnt = jnp.transpose(halo_counts, (1, 2, 0))
    own, sent = pl.pallas_call(
        assemble,
        in_specs=[SMEM, VMEM, VMEM],
        out_specs=[VMEM, VMEM],
        out_shape=[
            jax.ShapeDtypeStruct((cx * cy, 8, slots), F32),
            jax.ShapeDtypeStruct((cx * cy - cy, 8, slots), F32),
        ],
    )(cnt, positions_now, nxt)
    sent = lax.ppermute(sent, "gz_1", [(0, 1), (1, 0)])
    other = unpacked(sent, cx, cy)
    lists, counts, acc0, base, links, own, offsets = first_forces(
        half[None], neighbour_lists, cnt, own, vel, descendants
    )

    def both(start):
        place = start if start == 0 else start - cy
        ends = own[start : start + cy], sent[place : place + cy]
        return jnp.where(half == 0, jnp.stack(ends), jnp.stack(ends[::-1]))

    below = lax.ppermute(both(cx * cy - cy), ZRING, zring_pairs(zs, 1))
    above = lax.ppermute(both(0), ZRING, zring_pairs(zs, -1))

    def widened(block, plane):
        ends = [jnp.where(plane == 0, v[0], v[1]) for v in (below, above)]
        return jnp.concatenate([ends[0], block, ends[1]], axis=0)

    own = widened(own, half)
    other = widened(other, 1 - half)
    far = lax.ppermute(other, GZ, xhop_pairs(xs))
    acc1, top, bottom = other_forces(lists, counts, offsets, own, other, cx * cy, cx + 2)
    rows = far.reshape(cx + 2, cy * 8, slots)
    low = lax.ppermute(jnp.concatenate([top, rows[None, :, 8 * cy - 8 :]]), GY, ring(ny, 1))
    high = lax.ppermute(jnp.concatenate([bottom, rows[None, :, :8]]), GY, ring(ny, -1))
    acc2 = far_forces(lists, counts, offsets, own, far, cx * cy)
    drift, squared, part = finish(
        half[None], lists, counts, offsets, (own, other, far), low, high, (acc0, acc1, acc2), base, links, cx, cy
    )

    def gathered(row, axes):
        count = lax.axis_size(axes)
        return lax.all_to_all(jnp.broadcast_to(row, (count, slots)), axes, 0, 0, tiled=True)

    sums = jnp.sum(gathered(part, XY), axis=0, keepdims=True)
    tension = pl.pallas_call(
        scaled,
        in_specs=[VMEM, VMEM],
        out_specs=VMEM,
        out_shape=jax.ShapeDtypeStruct((cx, cy, cz, slots), F32),
        compiler_params=small_params(),
    )(gathered(sums, ZC), squared)
    return jnp.transpose(drift, (0, 1, 3, 2, 4)), tension


def solution(mesh):
    finer = Mesh(mesh.devices.reshape(mesh.shape["gx"], 4, 2, 4, 2), AXES)
    return jax.shard_map(
        shards,
        mesh=finer,
        in_specs=(
            P("gx", GY, GZ, None, None),
            P("gx", GY, GZ, None, None),
            P("gx", GY, GZ, None, None),
            P("gx", GY, GZ),
            P("gx", GY, GZ, None),
            P("gx", GY, GZ, None, None),
        ),
        out_specs=(P("gx", GY, GZ, None, None), P("gx", GY, GZ, None)),
        check_vma=False,
    )
```
